128 devices in a mesh: slab: 16 (over y, x), grp: 8 (over z, core).
Axes of the slice: x: 4, y: 4, z: 4, core: 2. Of those that a mesh axis runs over, the one named last changes fastest.
Arguments:
- initial: float32 [32, 64, 32, 256], P('grp', 'slab'), may hold values from 0 to 1
- target: float32 [32, 64, 32, 256], P('grp', 'slab'), may hold values from 0 to 0.6
- birth_step: int32 [64, 32, 256], P('slab'), may hold values from 0 to 4, as said below
- classes: int32 [32], P('grp'), may hold values from 0 to 3, as said below
- mobility: float32 [4, 4], replicated, may hold values from 0.2 to 2
Outputs:
- final_state: float32 [32, 64, 32, 256], P('grp', 'slab')
- initial_grad: float32 [32, 64, 32, 256], P('grp', 'slab')
- mobility_grad: float32 [4, 4], replicated
The draws below stay inside these ranges and needn't reach their ends.
Inputs may be any that keep to these rules, and one draw needn't show every extreme that they name: A voxel takes part in step n when birth_step <= n; the value 4 means that it never takes part in the window; exactly one voxel has the value 0. Each of the 4 classes is named by exactly 32 // K order parameters.
All inputs are finite; a program needn't handle non-finite values.
Results may differ from the reference program's by a relative error of at most 0.0001.
Values sent between devices are 32-bit elements; how exact they have to be, the bound alone decides.
No kernel may reach another device: no remote copies, remote signals or barrier semaphores. Data moves between devices by JAX's collectives and lax.ppermute only.
A program may use at most 64 MiB of HBM per device.

```python
import math
import jax
import jax.numpy as jnp
from jax import lax

P_SIZE = 32
K = 4
STEPS = 4
ZC = 32
NY = 256
NX = 64


def draw_birth_step(key, part):
    raw_key, seed_key = jax.random.split(key)
    rows = jnp.arange(NX, dtype=jnp.int32)[:, None, None]
    raw = jax.random.randint(raw_key, (NX, ZC, NY), 0, STEPS + 1, dtype=jnp.int32)
    sectioned = jnp.minimum(1 + raw * (NX - rows) // NX, STEPS)
    seed_voxel = jax.random.randint(seed_key, (), 0, NX * ZC * NY, dtype=jnp.int32)
    flat_index = jnp.arange(NX * ZC * NY, dtype=jnp.int32).reshape(NX, ZC, NY)
    return jnp.where(flat_index == seed_voxel, 0, sectioned).astype(jnp.int32)


def draw_classes(key, part):
    return (jax.random.permutation(key, P_SIZE) % K).astype(jnp.int32)


def block_levels(stream_key, dims, cuts, least, high):
    level = 1.0
    for position, parts in cuts:
        draws = jax.random.uniform(jax.random.fold_in(jax.random.fold_in(stream_key, 6), position), (parts,), jnp.float32, least / len(cuts), high / len(cuts))
        level = level * jnp.repeat(jnp.exp(draws), dims[position] // parts).reshape((-1,) + (1,) * (len(dims) - 1 - position))
    return level


def setup_inputs(seed: int = 0) -> dict:
    arg_keys = jax.random.split(jax.random.key(seed), 6)
    return {
        "initial": jnp.clip(1.0 * jax.random.uniform(arg_keys[0], (P_SIZE, NX, ZC, NY), jnp.float32) ** block_levels(arg_keys[0], (P_SIZE, NX, ZC, NY), ((0, 8), (1, 16)), -0.2, 0.2), 0.0, 1.0),
        "target": jnp.clip(0.6 * jax.random.uniform(arg_keys[1], (P_SIZE, NX, ZC, NY), jnp.float32) ** block_levels(arg_keys[1], (P_SIZE, NX, ZC, NY), ((0, 8), (1, 16)), -0.2, 0.2), 0.0, 0.6),
        "birth_step": draw_birth_step(jax.random.fold_in(arg_keys[5], 71), 0),
        "classes": draw_classes(jax.random.fold_in(arg_keys[5], 71), 0),
        "mobility": jnp.clip(jnp.exp(jax.random.uniform(arg_keys[4], (K, K), jnp.float32, math.log(0.2), math.log(2.0))), 0.2, 2.0),
    }


coupling = 0.3
stiffness = 1.0
time_step = 0.06

def laplace(fields):
    padded = jnp.pad(fields, ((0, 0), (1, 1), (1, 1), (1, 1)))
    centre = padded[:, 1:-1, 1:-1, 1:-1]
    return padded[:, 2:, 1:-1, 1:-1] + padded[:, :-2, 1:-1, 1:-1] + padded[:, 1:-1, 2:, 1:-1] + padded[:, 1:-1, :-2, 1:-1] + padded[:, 1:-1, 1:-1, 2:] + padded[:, 1:-1, 1:-1, :-2] - 6.0 * centre

def advance(fields, pair_rates, member, active):
    squared = fields * fields
    class_sums = jnp.einsum('pk,pxzy->kxzy', member, squared, precision=lax.Precision.HIGHEST)
    summed = lax.optimization_barrier(jnp.sum(class_sums, axis=0))
    inverse = 1.0 / (1.0 + summed)
    driving = jnp.einsum('pk,kxzy->pxzy', pair_rates, class_sums, precision=lax.Precision.HIGHEST)
    rates = driving * inverse[None]
    potential = -fields + fields * squared + 2.0 * coupling * fields * (summed[None] - squared) - stiffness * laplace(fields)
    weighted = active[None] * rates
    numerator = lax.optimization_barrier(jnp.sum(weighted * potential, axis=(1, 2, 3)))
    denominator = jnp.maximum(lax.optimization_barrier(jnp.sum(weighted, axis=(1, 2, 3))), 1.0)
    lagrange = numerator / denominator
    return fields - time_step * weighted * (potential - lagrange[:, None, None, None])

def reference(initial, target, birth_step, classes, mobility):
    member = (classes[:, None] == jnp.arange(K, dtype=jnp.int32)[None, :]).astype(jnp.float32)

    def evolve(fields, rates_table):
        pair_rates = jnp.dot(member, rates_table, precision=lax.Precision.HIGHEST)
        for step_index in range(STEPS):
            active = (birth_step <= step_index).astype(jnp.float32)
            fields = jax.checkpoint(advance)(fields, pair_rates, member, active)
        return fields
    final_state, pullback = jax.vjp(evolve, initial, mobility)
    mismatch = final_state - target
    initial_grad, mobility_grad = pullback(mismatch)
    return (final_state, initial_grad, mobility_grad / (time_step * NX * ZC))
```

```python
import jax
import jax.numpy as jnp
from jax import lax
from jax.sharding import PartitionSpec as P

STEPS = 4
coupling = 0.3
stiffness = 1.0
time_step = 0.06
HIGHEST = lax.Precision.HIGHEST


def everywhere(values):
    devices = lax.axis_size("slab") * lax.axis_size("grp")
    copies = jnp.broadcast_to(values[None], (devices,) + values.shape)
    return jnp.sum(lax.all_to_all(copies, ("slab", "grp"), 0, 0, tiled=True), axis=0)


def shift(plane, axis, step):
    count = lax.axis_size(axis)
    return lax.ppermute(plane, axis, [(i, i + step) for i in range(count) if 0 <= i + step < count])


def faces_of(cells):
    return (
        shift(cells[-1:], "slab", 1),
        shift(cells[:1], "slab", -1),
        shift(cells[:, -1:], "grp", 1),
        shift(cells[:, :1], "grp", -1),
    )


def laplace(cells, faces):
    before_x, after_x, before_z, after_z = faces
    padded = jnp.pad(cells, ((0, 0), (0, 0), (0, 0), (1, 1)))
    return (
        jnp.concatenate([cells[1:], after_x], axis=0)
        + jnp.concatenate([before_x, cells[:-1]], axis=0)
        + jnp.concatenate([cells[:, 1:], after_z], axis=1)
        + jnp.concatenate([before_z, cells[:, :-1]], axis=1)
        + padded[..., 2:]
        + padded[..., :-2]
        - 6.0 * cells
    )


def by_class(values, classes):
    x, z, p, y = values.shape
    return jnp.sum(values.reshape(x, z, classes, p // classes, y), axis=3)


def per_order(values, each):
    x, z, k, y = values.shape
    return jnp.broadcast_to(values[:, :, :, None, :], (x, z, k, each, y)).reshape(x, z, k * each, y)


def mix(table, values):
    classes = table.shape[0]
    rows = [
        sum(table[c, k] * values[:, :, k] for k in range(classes)) for c in range(classes)
    ]
    return jnp.stack(rows, axis=2)


def speeds(cells, mobility):
    sums = by_class(cells * cells, mobility.shape[0])
    summed = jnp.sum(sums, axis=2, keepdims=True)
    inverse = 1.0 / (1.0 + summed)
    return sums, summed, inverse, mix(mobility, sums) * inverse


def on_device(initial, target, birth_step, classes, mobility):
    kinds = mobility.shape[0]
    groups = lax.axis_size("grp")
    me = lax.axis_index("grp")
    local_p, local_x, nz, ny = initial.shape
    zb = nz // groups
    orders = local_p * groups
    each = orders // kinds
    rows = 2 * local_p * local_x * zb

    edge = (
        shift(birth_step[-1:], "slab", 1),
        shift(birth_step[:1], "slab", -1),
    )
    both = jnp.stack([initial, target]).reshape(2, local_p, local_x, groups, zb, ny)
    both = jnp.transpose(both, (3, 0, 1, 2, 4, 5)).reshape(groups, rows, ny)
    tag = jnp.pad(classes.astype(jnp.float32), (0, ny - local_p))
    tag = jnp.broadcast_to(tag[None, None], (groups, 8, ny))
    got = lax.all_to_all(
        jnp.concatenate([both, tag], axis=1), "grp", 0, 0, tiled=True
    )
    kind = got[:, rows, :local_p].reshape(orders).astype(jnp.int32)
    index = jnp.arange(orders, dtype=jnp.int32)
    ahead = (kind[None, :] < kind[:, None]) | (
        (kind[None, :] == kind[:, None]) & (index[None, :] < index[:, None])
    )
    rank = jnp.sum(ahead.astype(jnp.int32), axis=1)
    order = (rank[None, :] == index[:, None]).astype(jnp.float32)
    fields = got[:, :rows].reshape(groups, 2, local_p, local_x, zb, ny)
    fields = jnp.transpose(fields, (1, 3, 4, 0, 2, 5)).reshape(2, local_x, zb, orders, ny)
    fields = jnp.einsum("rp,axzpy->axzry", order, fields, precision=HIGHEST)
    cells, goal = fields[0], fields[1]

    never = jnp.full((local_x, 1, ny), STEPS, jnp.int32)
    tall = jnp.concatenate([never, birth_step, never], axis=1)
    tall = lax.dynamic_slice_in_dim(tall, me * zb, zb + 2, axis=1)
    births = (
        tall[:, 1:-1],
        lax.dynamic_slice_in_dim(edge[0], me * zb, zb, axis=1),
        lax.dynamic_slice_in_dim(edge[1], me * zb, zb, axis=1),
        tall[:, :1],
        tall[:, -1:],
    )

    faces = faces_of(cells)
    stored = []
    for step in range(STEPS):
        actives = [(b <= step).astype(jnp.float32)[:, :, None] for b in births]
        sums, summed, inverse, rates = speeds(cells, mobility)
        weights = [actives[0] * rates] + [
            a * speeds(f, mobility)[3] for a, f in zip(actives[1:], faces)
        ]
        potential = (
            -cells
            + cells * cells * cells
            + 2.0 * coupling * cells * (summed - cells * cells)
            - stiffness * laplace(cells, faces)
        )
        wide = [per_order(w, each) for w in weights]
        raw = jnp.sum(weights[0], axis=(0, 1, 3))
        part = [jnp.sum(wide[0] * potential, axis=(0, 1, 3)), raw]
        moved = cells - time_step * wide[0] * potential
        if step == STEPS - 1:
            moved = moved - goal
            part.append(jnp.sum(time_step * wide[0] * moved, axis=(0, 1, 3)))
            part.append(jnp.sum((time_step * weights[0]) ** 2, axis=(0, 1, 3)))
        moved_faces = faces_of(moved)
        total = everywhere(jnp.concatenate(part))
        raw = jnp.repeat(total[orders : orders + kinds], each)
        denominator = jnp.maximum(raw, 1.0)
        lagrange = total[:orders] / denominator
        lag = lagrange[None, None, :, None]
        stored.append(
            (cells, potential, sums, summed, inverse, rates, actives, wide, raw, denominator, lagrange)
        )
        after = [m + lag * time_step * w for m, w in zip((moved,) + moved_faces, wide)]
        cells, faces = after[0], after[1:]
    final_state = cells + goal
    adj, adj_faces = cells, faces
    lagrange_adj = total[orders + kinds : 2 * orders + kinds] + lagrange * jnp.repeat(
        total[2 * orders + kinds :], each
    )
    mobility_acc = jnp.zeros((kinds, kinds), jnp.float32)
    for step in range(STEPS - 1, -1, -1):
        (cells, potential, sums, summed, inverse, rates, actives, wide, raw, denominator, lagrange) = (
            stored[step]
        )
        keep = jnp.where(raw > 1.0, lagrange, 0.0)[None, None, :, None]
        lag = lagrange[None, None, :, None]
        gate = actives[0] * inverse
        if step < STEPS - 1:
            part = [jnp.sum(time_step * wide[0] * adj, axis=(0, 1, 3))]
            adj_faces = faces_of(adj)
            if step == 0:
                base = by_class(-time_step * adj * (potential - lag), kinds) * gate
                mobility_acc = mobility_acc + jnp.einsum(
                    "xzjy,xzky->jk", base, sums, precision=HIGHEST
                )
                linear = jnp.einsum(
                    "xzpy,xzky->pk", potential - keep, gate * sums, precision=HIGHEST
                )
                part += [mobility_acc.reshape(-1), linear.reshape(-1)]
            total = everywhere(jnp.concatenate(part))
            lagrange_adj = total[:orders]
        slope = lagrange_adj / denominator
        slopes = slope[None, None, :, None]
        pushed = [
            w * (slopes - time_step * a) for w, a in zip(wide, (adj,) + tuple(adj_faces))
        ]
        drive = gate * by_class(
            slopes * (potential - keep) - time_step * adj * (potential - lag), kinds
        )
        shared = jnp.sum(2.0 * coupling * pushed[0] * cells, axis=2, keepdims=True) - jnp.sum(
            rates * drive, axis=2, keepdims=True
        )
        class_adj = mix(mobility.T, drive) + shared
        if step > 0:
            mobility_acc = mobility_acc + jnp.einsum(
                "xzjy,xzky->jk", drive, sums, precision=HIGHEST
            )
        adj = (
            adj
            + pushed[0] * (-1.0 + 2.0 * coupling * summed + (3.0 - 6.0 * coupling) * cells * cells)
            - stiffness * laplace(pushed[0], pushed[1:])
            + 2.0 * cells * per_order(class_adj, each)
        )
    mobility_sum = total[orders : orders + kinds * kinds].reshape(kinds, kinds)
    linear = total[orders + kinds * kinds :].reshape(orders, kinds)
    mobility_sum = mobility_sum + jnp.sum(
        (slope[:, None] * linear).reshape(kinds, each, kinds), axis=1
    )
    scale = time_step * (local_x * lax.axis_size("slab")) * nz

    both = jnp.stack([final_state, adj])
    both = jnp.einsum("rp,axzry->axzpy", order, both, precision=HIGHEST)
    both = both.reshape(2, local_x, zb, groups, local_p, ny)
    both = jnp.transpose(both, (3, 0, 4, 1, 2, 5)).reshape(groups, rows, ny)
    both = lax.all_to_all(both, "grp", 0, 0, tiled=True)
    both = both.reshape(groups, 2, local_p, local_x, zb, ny)
    both = jnp.transpose(both, (1, 2, 3, 0, 4, 5)).reshape(2, local_p, local_x, nz, ny)
    return both[0], both[1], mobility_sum / scale


def solution(mesh):
    return jax.shard_map(
        on_device,
        mesh=mesh,
        in_specs=(
            P("grp", "slab", None, None),
            P("grp", "slab", None, None),
            P("slab", None, None),
            P("grp"),
            P(),
        ),
        out_specs=(P("grp", "slab", None, None), P("grp", "slab", None, None), P()),
        check_vma=False,
    )
```

```python
import functools

import jax
import jax.numpy as jnp
from jax import lax
from jax.experimental import pallas as pl
from jax.experimental.pallas import tpu as pltpu
from jax.sharding import PartitionSpec as P

STEPS = 4
coupling = 0.3
stiffness = 1.0
time_step = 0.06
LANES = 128
AXES = ("slab", "grp")


def spread(column, offset):
    n = column.shape[0]
    lane = lax.broadcasted_iota(jnp.int32, (n, LANES), 1)
    row = lax.broadcasted_iota(jnp.int32, (n, LANES), 0)
    return jnp.sum(jnp.where(lane == row + offset, column, 0.0), axis=0, keepdims=True)


def gather(total, offset, n):
    lane = lax.broadcasted_iota(jnp.int32, (n, LANES), 1)
    row = lax.broadcasted_iota(jnp.int32, (n, LANES), 0)
    return jnp.sum(jnp.where(lane == row + offset, total, 0.0), axis=1, keepdims=True)


def beside(cells):
    width = cells.shape[-1]
    lane = lax.broadcasted_iota(jnp.int32, cells.shape, cells.ndim - 1)
    left = jnp.where(lane == 0, 0.0, pltpu.roll(cells, 1, cells.ndim - 1))
    right = jnp.where(lane == width - 1, 0.0, pltpu.roll(cells, width - 1, cells.ndim - 1))
    return left + right


def class_sums(values):
    return [jnp.sum(v, axis=0, keepdims=True) for v in values]


def active(births_ref, row, step):
    return jnp.where(births_ref[pl.ds(row, 1), :] <= step, 1.0, 0.0)


def class_rates(sums, mob_ref, kinds):
    inverse = 1.0 / (1.0 + functools.reduce(jnp.add, sums))
    return inverse, [
        functools.reduce(jnp.add, [mob_ref[c, k] * sums[k] for k in range(kinds)]) * inverse
        for c in range(kinds)
    ]


def forward_kernel(step, kinds, *refs):
    first, last = step == 0, step == STEPS - 1
    refs = list(refs)
    mob_ref, core_ref, births_ref = refs[:3]
    refs = refs[3:]
    if not first:
        got_ref, wprev_ref = refs[:2]
        refs = refs[2:]
    own_ref, before_ref, after_ref, edge_ref = refs[:4]
    refs = refs[4:]
    if last:
        goal_ref = refs.pop(0)
    if not first:
        cells_ref, stats_ref = refs[:2]
        refs = refs[2:]
    moved_ref, send_ref, pot_ref, sums_ref, w_ref, copies_ref, pad_ref = refs[:7]
    refs = refs[7:]
    rows, orders, ny = own_ref.shape
    each = orders // kinds
    cut = [slice(c * each, (c + 1) * each) for c in range(kinds)]
    if first:
        lin_ref = refs[0]
        lin_ref[...] = jnp.zeros_like(lin_ref)
    else:
        width = got_ref.shape[1] // LANES
        total = jnp.sum(got_ref[...], axis=0, keepdims=True)
        raw = gather(total[:, :LANES], orders, orders)
        lag = gather(total[:, :LANES], 0, orders) / jnp.maximum(raw, 1.0)
        stats_ref[0] = jnp.broadcast_to(lag, (orders, LANES))
        stats_ref[1] = jnp.broadcast_to(raw, (orders, LANES))
        for k in range(kinds if width > 1 else 0):
            base = gather(total[:, LANES:], k * orders, orders)
            level = jnp.sum(
                jnp.where(
                    lax.broadcasted_iota(jnp.int32, (1, LANES), 1) == 2 * orders + k * each,
                    total[:, :LANES],
                    0.0,
                ),
                axis=1,
                keepdims=True,
            )
            value = base - jnp.where(raw > 1.0, lag, 0.0) * level
            stats_ref[2 + k] = jnp.broadcast_to(value, (orders, LANES))
        pace = lag * time_step

    def grown(ref, z, place, c):
        value = ref[z, cut[c], :]
        if first:
            return value
        return value + pace[cut[c]] * wprev_ref[pl.ds(place * kinds + c, 1), :]

    core = core_ref[0]

    def fill(z, carry):
        for c in range(kinds):
            value = grown(own_ref, z, z, c)
            pad_ref[z + 1, cut[c], :] = value
            if not first:
                cells_ref[z, cut[c], :] = value
        return carry

    lax.fori_loop(0, rows, fill, 0)
    edge = [grown(edge_ref, 0, 3 * rows, c) for c in range(kinds)]
    for c in range(kinds):
        pad_ref[0, cut[c], :] = jnp.where(core == 1, edge[c], 0.0)
        pad_ref[rows + 1, cut[c], :] = jnp.where(core == 0, edge[c], 0.0)
    _, edge_rates = class_rates(class_sums([e * e for e in edge]), mob_ref, kinds)
    act = active(births_ref, 3 * rows, step)
    for c in range(kinds):
        w_ref[pl.ds(3 * rows * kinds + c, 1), :] = act * edge_rates[c]

    def line(z, carry):
        numer, denom, extra_a, extra_b, level = carry
        numer, denom, extra_a, extra_b, level = (
            list(numer),
            list(denom),
            list(extra_a),
            list(extra_b),
            list(level),
        )
        around = []
        for place, ref in ((rows, before_ref), (2 * rows, after_ref)):
            values = [grown(ref, z, place + z, c) for c in range(kinds)]
            _, rates = class_rates(class_sums([v * v for v in values]), mob_ref, kinds)
            act = active(births_ref, place + z, step)
            for c in range(kinds):
                w_ref[pl.ds((place + z) * kinds + c, 1), :] = act * rates[c]
            around.append(values)
        cells = [pad_ref[z + 1, cut[c], :] for c in range(kinds)]
        squares = [e * e for e in cells]
        sums = class_sums(squares)
        inverse, rates = class_rates(sums, mob_ref, kinds)
        summed = functools.reduce(jnp.add, sums)
        act = active(births_ref, z, step)
        for c in range(kinds):
            e = cells[c]
            w = act * rates[c]
            w_ref[pl.ds(z * kinds + c, 1), :] = w
            sums_ref[pl.ds(z * kinds + c, 1), :] = sums[c]
            curved = (
                around[0][c]
                + around[1][c]
                + pad_ref[z, cut[c], :]
                + pad_ref[z + 2, cut[c], :]
                + beside(e)
                - 6.0 * e
            )
            pot = (
                -e
                + e * squares[c]
                + 2.0 * coupling * e * (summed - squares[c])
                - stiffness * curved
            )
            pot_ref[z, cut[c], :] = pot
            pushed = w * pot
            numer[c] = numer[c] + pushed
            denom[c] = denom[c] + w
            moved = e - time_step * pushed
            if last:
                moved = moved - goal_ref[z, cut[c], :]
                step_w = time_step * w
                extra_a[c] = extra_a[c] + step_w * moved
                extra_b[c] = extra_b[c] + step_w * step_w
            moved_ref[z, cut[c], :] = moved
            if first:
                for k in range(kinds):
                    lin_ref[k, cut[c], :] += pot * (act * inverse * sums[k])
        if first:
            for k in range(kinds):
                level[k] = level[k] + act * inverse * sums[k]
        return tuple(numer), tuple(denom), tuple(extra_a), tuple(extra_b), tuple(level)

    tall = tuple(jnp.zeros((each, ny), jnp.float32) for _ in range(kinds))
    flat = tuple(jnp.zeros((1, ny), jnp.float32) for _ in range(kinds))
    none = ()
    numer, denom, extra_a, extra_b, level = lax.fori_loop(
        0,
        rows,
        line,
        (tall, flat, tall if last else none, flat if last else none, flat if first else none),
    )

    def row_of(parts, offset):
        columns = [
            jnp.broadcast_to(jnp.sum(v, axis=1, keepdims=True), (each, 1)) for v in parts
        ]
        return spread(jnp.concatenate(columns, axis=0), offset)

    row = row_of(numer, 0) + row_of(denom, orders)
    if first:
        row = row + row_of(level, 2 * orders)
    if last:
        row = row + row_of(extra_a, 2 * orders) + row_of(extra_b, 3 * orders)
    devices = copies_ref.shape[0]
    copies_ref[:, :LANES] = jnp.broadcast_to(row, (devices, LANES))
    if first:
        second = functools.reduce(
            jnp.add,
            [
                spread(jnp.sum(lin_ref[k], axis=1, keepdims=True), k * orders)
                for k in range(kinds)
            ],
        )
        copies_ref[:, LANES:] = jnp.broadcast_to(second, (devices, LANES))
    send_ref[0] = moved_ref[jnp.where(core == 0, rows - 1, 0)]


def backward_kernel(step, kinds, *refs):
    top, bottom = step == STEPS - 1, step == 0
    refs = list(refs)
    mob_ref, core_ref, births_ref, got_ref, w_ref, pot_ref, sums_ref = refs[:7]
    refs = refs[7:]
    if top:
        goal_ref = refs.pop(0)
    else:
        stats_ref = refs.pop(0)
    cells_ref, own_ref, before_ref, after_ref, edge_ref = refs[:5]
    refs = refs[5:]
    if not top:
        mobin_ref = refs.pop(0)
    if not bottom:
        wnext_ref = refs.pop(0)
    if step == 1:
        pot0_ref, sums0_ref, stats0_ref = refs[:3]
        refs = refs[3:]
    adj_ref = refs.pop(0)
    if top:
        final_ref = refs.pop(0)
    if bottom:
        mobility_ref = refs.pop(0)
    else:
        send_ref, copies_ref = refs[:2]
        refs = refs[2:]
        if step > 1:
            mobout_ref = refs.pop(0)
    pad_ref = refs.pop(0)
    rows, orders, ny = own_ref.shape
    each = orders // kinds
    cut = [slice(c * each, (c + 1) * each) for c in range(kinds)]
    core = core_ref[0]

    total = jnp.sum(got_ref[...], axis=0, keepdims=True)
    if top:
        raw = gather(total, orders, orders)
        lag = gather(total, 0, orders) / jnp.maximum(raw, 1.0)
        lag_adj = gather(total, 2 * orders, orders) + lag * gather(total, 3 * orders, orders)
        pace = lag * time_step
    else:
        lag = stats_ref[0][:, :1]
        raw = stats_ref[1][:, :1]
        lag_adj = gather(total, orders, orders)
    slope = lag_adj / jnp.maximum(raw, 1.0)
    keep = jnp.where(raw > 1.0, lag, 0.0)

    def grown(ref, z, place, c):
        value = ref[z, cut[c], :]
        weight = w_ref[pl.ds(place * kinds + c, 1), :]
        if top:
            value = value + pace[cut[c]] * weight
        return value, weight * (slope[cut[c]] - time_step * value)

    def fill(z, carry):
        for c in range(kinds):
            value, pushed = grown(own_ref, z, z, c)
            pad_ref[z + 1, cut[c], :] = pushed
            if top:
                adj_ref[z, cut[c], :] = value
                final_ref[z, cut[c], :] = value + goal_ref[z, cut[c], :]
        return carry

    lax.fori_loop(0, rows, fill, 0)
    for c in range(kinds):
        pushed = grown(edge_ref, 0, 3 * rows, c)[1]
        pad_ref[0, cut[c], :] = jnp.where(core == 1, pushed, 0.0)
        pad_ref[rows + 1, cut[c], :] = jnp.where(core == 0, pushed, 0.0)
    lower = lax.broadcasted_iota(jnp.int32, (2 * kinds, ny), 0)

    def pack(values, period):
        out = jnp.broadcast_to(values[0], (2 * kinds, ny))
        for i in range(1, len(values)):
            mask = lower // period == i if period else lower % kinds == i
            out = jnp.where(mask, values[i], out)
        return out

    def outer(acc, drive, sums):
        right = pack(sums, 0)
        return tuple(
            acc[h] + pack(drive[2 * h : 2 * h + 2], kinds) * right for h in range(kinds // 2)
        )

    def line(z, carry):
        mob, onward = carry
        sums = [sums_ref[pl.ds(z * kinds + c, 1), :] for c in range(kinds)]
        weights = [w_ref[pl.ds(z * kinds + c, 1), :] for c in range(kinds)]
        summed = functools.reduce(jnp.add, sums)
        inverse = 1.0 / (1.0 + summed)
        act = active(births_ref, z, step)
        source = adj_ref if top else own_ref
        adj = [source[z, cut[c], :] for c in range(kinds)]
        cells = [cells_ref[z, cut[c], :] for c in range(kinds)]
        pots = [pot_ref[z, cut[c], :] for c in range(kinds)]
        pushed = [pad_ref[z + 1, cut[c], :] for c in range(kinds)]
        drive = class_sums(
            [
                slope[cut[c]] * (pots[c] - keep[cut[c]])
                - time_step * adj[c] * (pots[c] - lag[cut[c]])
                for c in range(kinds)
            ]
        )
        plain = [inverse * d for d in drive]
        drive = [act * d for d in plain]
        shared = 2.0 * coupling * jnp.sum(
            functools.reduce(jnp.add, [pushed[c] * cells[c] for c in range(kinds)]),
            axis=0,
            keepdims=True,
        ) - functools.reduce(jnp.add, [weights[c] * plain[c] for c in range(kinds)])
        if not bottom:
            mob = outer(mob, drive, sums)
        onward = list(onward)
        later = []
        for c in range(kinds):
            class_adj = (
                functools.reduce(jnp.add, [mob_ref[k, c] * drive[k] for k in range(kinds)]) + shared
            )
            curved = (
                grown(before_ref, z, rows + z, c)[1]
                + grown(after_ref, z, 2 * rows + z, c)[1]
                + pad_ref[z, cut[c], :]
                + pad_ref[z + 2, cut[c], :]
                + beside(pushed[c])
                - 6.0 * pushed[c]
            )
            e = cells[c]
            new = (
                adj[c]
                + pushed[c]
                * (-1.0 + 2.0 * coupling * summed + (3.0 - 6.0 * coupling) * (e * e))
                - stiffness * curved
                + 2.0 * e * class_adj
            )
            adj_ref[z, cut[c], :] = new
            if not bottom:
                onward[c] = onward[c] + time_step * wnext_ref[pl.ds(z * kinds + c, 1), :] * new
            later.append(new)
        if step == 1:
            sums0 = [sums0_ref[pl.ds(z * kinds + c, 1), :] for c in range(kinds)]
            gate = active(births_ref, z, 0) / (1.0 + functools.reduce(jnp.add, sums0))
            lag0 = stats0_ref[0][:, :1]
            drive = [
                gate * d
                for d in class_sums(
                    [
                        -time_step * later[c] * (pot0_ref[z, cut[c], :] - lag0[cut[c]])
                        for c in range(kinds)
                    ]
                )
            ]
            mob = outer(mob, drive, sums0)
        return mob, tuple(onward)

    mob = tuple(jnp.zeros((2 * kinds, ny), jnp.float32) for _ in range(kinds // 2))
    tall = tuple(jnp.zeros((each, ny), jnp.float32) for _ in range(kinds))
    mob, onward = lax.fori_loop(
        0, rows, line, (() if bottom else mob, () if bottom else tall)
    )
    if bottom:
        row = total * jnp.where(
            lax.broadcasted_iota(jnp.int32, (1, LANES), 1) < kinds * kinds, 1.0, 0.0
        )
        lane = lax.broadcasted_iota(jnp.int32, (orders, LANES), 1)
        home = lax.broadcasted_iota(jnp.int32, (orders, LANES), 0) // each
        for k in range(kinds):
            value = slope * mobin_ref[2 + k][:, :1]
            row = row + jnp.sum(
                jnp.where(lane == home * kinds + k, value, 0.0), axis=0, keepdims=True
            )
        mobility_ref[...] = jnp.broadcast_to(row, mobility_ref.shape)
    else:
        terms = jnp.concatenate([jnp.sum(m, axis=1, keepdims=True) for m in mob], axis=0)
        if not top:
            terms = terms + mobin_ref[:, :1]
        row = spread(
            jnp.concatenate([jnp.sum(v, axis=1, keepdims=True) for v in onward], axis=0), orders
        )
        if step == 1:
            row = row + spread(terms, 0)
        else:
            mobout_ref[...] = jnp.broadcast_to(terms, mobout_ref.shape)
        copies_ref[...] = jnp.broadcast_to(row, copies_ref.shape)
        send_ref[0] = adj_ref[jnp.where(core == 0, rows - 1, 0)]


def unpack_kernel(rank_ref, got_ref, *refs):
    sources, arrays, local, rows, ny = got_ref.shape
    outs, parts = refs[:arrays], refs[arrays:]
    orders = sources * local
    strips = [slice(h * LANES, (h + 1) * LANES) for h in range(ny // LANES)]
    for a in range(arrays):
        for i in range(orders):
            for h, strip in enumerate(strips):
                parts[h][pl.ds(rank_ref[i], rows, stride=orders), :] = got_ref[
                    i // local, a, i % local, :, strip
                ]
        for h, strip in enumerate(strips):
            outs[a][:, strip] = parts[h][...]


def pack_kernel(rank_ref, *refs):
    fields, out_ref, parts = refs[:2], refs[2], refs[3:]
    groups, arrays, local, rows, ny = out_ref.shape
    orders = groups * local
    strips = [slice(h * LANES, (h + 1) * LANES) for h in range(ny // LANES)]
    for a in range(arrays):
        for h, strip in enumerate(strips):
            parts[h][...] = fields[a][:, strip]
        for i in range(orders):
            for h, strip in enumerate(strips):
                out_ref[i // local, a, i % local, :, strip] = parts[h][
                    pl.ds(rank_ref[i], rows, stride=orders), :
                ]


VMEM = pl.BlockSpec(memory_space=pltpu.VMEM)
SMEM = pl.BlockSpec(memory_space=pltpu.SMEM)


def call(kernel, name, smem, operands, outs, scratch=()):
    return pl.pallas_call(
        kernel,
        name=name,
        out_shape=[jax.ShapeDtypeStruct(s, jnp.float32) for s in outs],
        in_specs=[SMEM] * smem + [VMEM] * (len(operands) - smem),
        out_specs=[VMEM] * len(outs),
        scratch_shapes=[pltpu.VMEM(s, jnp.float32) for s in scratch],
        compiler_params=pltpu.CompilerParams(vmem_limit_bytes=16 * 1024 * 1024),
    )(*operands)


def on_device(initial, target, birth_step, classes, mobility):
    kinds = mobility.shape[0]
    slabs, groups = lax.axis_size("slab"), lax.axis_size("grp")
    devices = slabs * groups
    me = lax.axis_index("grp")
    local, planes, nz, ny = initial.shape
    halves = groups // planes
    rows = nz // halves
    orders = local * groups
    core = (me % halves).astype(jnp.int32)
    plane = me // halves

    def along_x(step):
        pairs = []
        for i in range(slabs * planes):
            j = i + step
            if 0 <= j < slabs * planes:
                pairs += [(i * halves + c, j * halves + c) for c in range(halves)]
        return pairs

    swap = [(g, g ^ 1) for g in range(groups)]

    def faces_of(cells, edge):
        return (
            lax.ppermute(cells, AXES, along_x(1)),
            lax.ppermute(cells, AXES, along_x(-1)),
            lax.ppermute(edge, "grp", swap),
        )

    def everywhere(copies):
        return lax.all_to_all(copies, AXES, 0, 0, tiled=True)

    chain = [(i, i + 1) for i in range(slabs - 1)]
    births = jnp.concatenate(
        [
            lax.ppermute(birth_step[-1:], "slab", chain),
            birth_step,
            lax.ppermute(birth_step[:1], "slab", [(j, i) for i, j in chain]),
        ]
    )
    near = lax.dynamic_slice_in_dim(births, plane, 3, axis=0)
    mine = lax.dynamic_slice_in_dim(near, core * rows, rows, axis=1)
    other = lax.dynamic_slice_in_dim(near[1], jnp.where(core == 0, rows, rows - 1), 1, axis=0)
    births = jnp.concatenate(
        [mine[1], mine[0], mine[2], jnp.broadcast_to(other, (8, ny))], axis=0
    )

    both = jnp.stack([initial, target]).reshape(2, local, planes, halves, rows, ny)
    both = jnp.transpose(both, (2, 3, 0, 1, 4, 5)).reshape(groups, 2 * local * rows, ny)
    tag = jnp.pad(classes.astype(jnp.float32), (0, ny - local))
    tag = jnp.broadcast_to(tag[None, None], (groups, 8, ny))
    got = lax.all_to_all(jnp.concatenate([both, tag], axis=1), "grp", 0, 0, tiled=True)
    kind = got[:, 2 * local * rows, :local].reshape(orders).astype(jnp.int32)
    index = jnp.arange(orders, dtype=jnp.int32)
    ahead = (kind[None, :] < kind[:, None]) | (
        (kind[None, :] == kind[:, None]) & (index[None, :] < index[:, None])
    )
    rank = jnp.sum(ahead.astype(jnp.int32), axis=1)
    got = got[:, : 2 * local * rows].reshape(groups, 2, local, rows, ny)
    flat = (rows * orders, ny)
    strips = [(rows * orders, LANES)] * (ny // LANES)
    cells, goal = call(
        unpack_kernel, "unpack", 1, [rank, got], [flat] * 2, strips
    )
    shape = (rows, orders, ny)
    cells, goal = cells.reshape(shape), goal.reshape(shape)
    common = [mobility, core.reshape(1), births]
    compact, wide = (rows * kinds, ny), (3 * rows * kinds + 8, ny)
    padded = (rows + 2, orders, ny)
    edge_shape = (1, orders, ny)

    own = cells
    edge = lax.dynamic_slice_in_dim(cells, jnp.where(core == 0, rows - 1, 0), 1, axis=0)
    stored = []
    got = weights = None
    for step in range(STEPS):
        first, last = step == 0, step == STEPS - 1
        faces = faces_of(own, edge)
        operands = common + ([] if first else [got, weights]) + [own, *faces]
        if last:
            operands.append(goal)
        outs = [] if first else [shape, (2 + (kinds if step == 1 else 0), orders, LANES)]
        outs += [shape, edge_shape, shape, compact, wide]
        outs.append((devices, 2 * LANES if first else LANES))
        scratch = [padded] + ([(kinds, orders, ny)] if first else [])
        result = call(
            functools.partial(forward_kernel, step, kinds),
            f"forward{step}",
            2,
            operands,
            outs,
            scratch,
        )
        if not first:
            cells = result[0]
            stored[-1] = stored[-1] + (result[1],)
            result = result[2:]
        own, edge, potential, sums, weights, copies = result
        stored.append((cells, potential, sums, weights))
        got = everywhere(copies)
    terms = None
    for step in range(STEPS - 1, -1, -1):
        top, bottom = step == STEPS - 1, step == 0
        cells, potential, sums, weights = stored[step][:4]
        faces = faces_of(own, edge)
        operands = common + [got, weights, potential, sums]
        operands.append(goal if top else stored[step][4])
        operands += [cells, own, *faces]
        if not top:
            operands.append(stored[0][4] if bottom else terms)
        if not bottom:
            operands.append(stored[step - 1][3])
        if step == 1:
            operands += [stored[0][1], stored[0][2], stored[0][4]]
        outs = [shape] + ([shape] if top else [])
        if bottom:
            outs.append((8, LANES))
        else:
            outs += [edge_shape, (devices, LANES)]
            if step > 1:
                outs.append((kinds * kinds, LANES))
        result = list(
            call(
                functools.partial(backward_kernel, step, kinds),
                f"backward{step}",
                2,
                operands,
                outs,
                [padded],
            )
        )
        own = result.pop(0)
        if top:
            final_state = result.pop(0)
        if bottom:
            mobility_sum = result[0]
        else:
            edge, copies = result[:2]
            if step > 1:
                terms = result[2]
            got = everywhere(copies)

    (both,) = call(
        pack_kernel,
        "pack",
        1,
        [rank, final_state.reshape(flat), own.reshape(flat)],
        [(groups, 2, local, rows, ny)],
        strips,
    )
    both = both.reshape(groups, 2 * local * rows, ny)
    both = lax.all_to_all(both, "grp", 0, 0, tiled=True)
    both = both.reshape(planes, halves, 2, local, rows, ny)
    both = jnp.transpose(both, (2, 3, 0, 1, 4, 5)).reshape(2, local, planes, nz, ny)
    scale = time_step * (planes * slabs) * nz
    mobility_sum = mobility_sum[0, : kinds * kinds].reshape(kinds, kinds)
    return both[0], both[1], mobility_sum / scale


def solution(mesh):
    return jax.shard_map(
        on_device,
        mesh=mesh,
        in_specs=(
            P("grp", "slab", None, None),
            P("grp", "slab", None, None),
            P("slab", None, None),
            P("grp"),
            P(),
        ),
        out_specs=(P("grp", "slab", None, None), P("grp", "slab", None, None), P()),
        check_vma=False,
    )
```

```python
import functools

import jax
import jax.numpy as jnp
from jax import lax
from jax.experimental import pallas as pl
from jax.experimental.pallas import tpu as pltpu
from jax.sharding import PartitionSpec as P

STEPS = 4
coupling = 0.3
stiffness = 1.0
time_step = 0.06
LANES = 128
SUBLANES = 8
KINDS = 4
CHUNKS = 4
AXES = ("slab", "grp")


def spread(column, offset):
    n = column.shape[0]
    lane = lax.broadcasted_iota(jnp.int32, (n, LANES), 1)
    row = lax.broadcasted_iota(jnp.int32, (n, LANES), 0)
    return jnp.sum(jnp.where(lane == row + offset, column, 0.0), axis=0, keepdims=True)


def gather(total, offset, n):
    lane = lax.broadcasted_iota(jnp.int32, (n, LANES), 1)
    row = lax.broadcasted_iota(jnp.int32, (n, LANES), 0)
    return jnp.sum(jnp.where(lane == row + offset, total, 0.0), axis=1, keepdims=True)


def beside(cells):
    width = cells.shape[-1]
    lane = lax.broadcasted_iota(jnp.int32, cells.shape, cells.ndim - 1)
    left = jnp.where(lane == 0, 0.0, pltpu.roll(cells, 1, cells.ndim - 1))
    right = jnp.where(lane == width - 1, 0.0, pltpu.roll(cells, width - 1, cells.ndim - 1))
    return left + right


def rolled(tile):
    return [tile] + [pltpu.roll(tile, d, 0) for d in range(1, KINDS)]


def packed(values):
    row = lax.broadcasted_iota(jnp.int32, values[0].shape, 0)
    step = 1
    while len(values) > 1:
        mask = (row // step) % 2 == 0
        values = [
            jnp.where(mask, u, v) + pltpu.roll(jnp.where(mask, v, u), step, 0)
            for u, v in zip(values[0::2], values[1::2])
        ]
        step *= 2
    (tile,) = values
    while step < SUBLANES:
        tile = tile + pltpu.roll(tile, step, 0)
        step *= 2
    return tile


def total_rows(tile):
    step = 1
    while step < SUBLANES:
        tile = tile + pltpu.roll(tile, step, 0)
        step *= 2
    return tile


def class_row(tile, c):
    return jnp.broadcast_to(tile[c : c + 1, :], tile.shape)


def tables(mob_ref, ny, transposed):
    row = lax.broadcasted_iota(jnp.int32, (SUBLANES, ny), 0) % KINDS
    tiles = []
    for d in range(KINDS):
        tile = jnp.zeros((SUBLANES, ny), jnp.float32)
        for c in range(KINDS):
            k = (c - d) % KINDS
            value = mob_ref[k, c] if transposed else mob_ref[c, k]
            tile = jnp.where(row == c, value, tile)
        tiles.append(tile)
    return tiles


def mixed(table, rolls):
    return functools.reduce(jnp.add, [t * r for t, r in zip(table, rolls)])


def active(births_ref, row, step):
    return jnp.where(births_ref[pl.ds(row, 1), :] <= step, 1.0, 0.0)


class Stream:
    def __init__(self, source, target, sems, chunks=1):
        self.source, self.target, self.sems, self.chunks = source, target, sems, chunks

    def copy(self, j):
        if self.chunks == 1:
            return pltpu.make_async_copy(self.source, self.target, self.sems.at[0])
        size = self.target.shape[0] // self.chunks
        return pltpu.make_async_copy(
            self.source.at[pl.ds(j * size, size)],
            self.target.at[pl.ds(j * size, size)],
            self.sems.at[j],
        )

    def start(self, j=0):
        self.copy(j).start()

    def start_all(self):
        for j in range(self.chunks):
            self.start(j)

    def wait(self, j=0):
        self.copy(j).wait()

    def wait_all(self):
        for j in range(self.chunks):
            self.wait(j)


def forward_kernel(step, refs):
    first, last = step == 0, step == STEPS - 1
    core_ref, mob_ref, births_ref, pad_ref = (refs[n] for n in ("core", "mob", "births", "pad"))
    before_ref, after_ref = refs["before"], refs["after"]
    w_ref, sums_ref, moved_ref, pot_ref = (refs[n] for n in ("w", "sums", "moved", "pot"))
    stream = refs["stream"]
    rows, orders, ny = moved_ref.shape
    each = orders // KINDS
    cut = [slice(c * each, (c + 1) * each) for c in range(KINDS)]
    core = core_ref[0]
    inner = pad_ref.at[pl.ds(1, rows)]

    own_in = stream("own", inner)
    edge_in = stream("edge", refs["edge"])
    ins = [own_in, edge_in]
    if not first:
        wprev_ref = refs["wprev"]
        ins.append(stream("wprev", wprev_ref))
    for s in ins:
        s.start()
    sides = [stream("before", before_ref, CHUNKS), stream("after", after_ref, CHUNKS)]
    if last:
        sides.append(stream("goal", refs["goal"], CHUNKS))
    for j in range(CHUNKS):
        for s in sides:
            s.start(j)
    outs = []
    if first:
        lin_ref = refs["lin"]
        lin_ref[...] = jnp.zeros_like(lin_ref)
    else:
        stats_ref = refs["stats"]
        got = refs["got"][...]
        if step == 1:
            odd = lax.broadcasted_iota(jnp.int32, got.shape, 0) % 2 == 1
            second = jnp.sum(jnp.where(odd, got, 0.0), axis=0, keepdims=True)
            got = jnp.where(odd, 0.0, got)
        total = jnp.sum(got, axis=0, keepdims=True)
        raw = gather(total, orders, orders)
        lag = gather(total, 0, orders) / jnp.maximum(raw, 1.0)
        stats_ref[0] = jnp.broadcast_to(lag, (orders, LANES))
        stats_ref[1] = jnp.broadcast_to(raw, (orders, LANES))
        if step == 1:
            lane = lax.broadcasted_iota(jnp.int32, (1, LANES), 1)
            for k in range(KINDS):
                base = gather(second, k * orders, orders)
                level = jnp.sum(
                    jnp.where(lane == 2 * orders + k, total, 0.0), axis=1, keepdims=True
                )
                value = base - jnp.where(raw > 1.0, lag, 0.0) * level
                stats_ref[2 + k] = jnp.broadcast_to(value, (orders, LANES))
        pace = [jnp.broadcast_to(lag[cut[c]] * time_step, (each, ny)) for c in range(KINDS)]
        stats_out = stream("stats", stats_ref, out=True)
        stats_out.start()
        outs.append(stats_out)
    table = tables(mob_ref, ny, False)

    def grown(value, place, c):
        if first:
            return value
        return value + pace[c] * wprev_ref[place, pl.ds(c, 1), :]

    def rates_of(squares, place):
        sums = packed(squares)
        rolls = rolled(sums)
        summed = functools.reduce(jnp.add, rolls)
        gate = active(births_ref, place, step) / (1.0 + summed)
        w = gate * mixed(table, rolls)
        w_ref[place] = w
        return sums, summed, gate, w

    for s in ins:
        s.wait()
    if not first:

        def fill(z, carry):
            for c in range(KINDS):
                pad_ref[z + 1, cut[c], :] = grown(pad_ref[z + 1, cut[c], :], z, c)
            return carry

        lax.fori_loop(0, rows, fill, 0, unroll=2)
        cells_out = stream("cells", inner, out=True)
        cells_out.start()
        outs.append(cells_out)
    edge = [grown(refs["edge"][0, cut[c], :], 3 * rows, c) for c in range(KINDS)]
    for c in range(KINDS):
        pad_ref[0, cut[c], :] = jnp.where(core == 1, edge[c], 0.0)
        pad_ref[rows + 1, cut[c], :] = jnp.where(core == 0, edge[c], 0.0)
    rates_of([e * e for e in edge], 3 * rows)

    moved_out = stream("moved", moved_ref, CHUNKS, out=True)
    pot_out = stream("pot", pot_ref, CHUNKS, out=True)

    def line(z, carry):
        numer, denom, extra_a, extra_b, level = carry
        before = [grown(before_ref[z, cut[c], :], rows + z, c) for c in range(KINDS)]
        rates_of([v * v for v in before], rows + z)
        after = [grown(after_ref[z, cut[c], :], 2 * rows + z, c) for c in range(KINDS)]
        rates_of([v * v for v in after], 2 * rows + z)
        cells = [pad_ref[z + 1, cut[c], :] for c in range(KINDS)]
        squares = [e * e for e in cells]
        sums, summed, gate, w = rates_of(squares, z)
        sums_ref[z] = sums
        level_now = gate * sums
        step_w = time_step * w
        base = (6.0 * stiffness - 1.0) + (2.0 * coupling) * summed
        numer, extra_a = list(numer), list(extra_a)
        for c in range(KINDS):
            e = cells[c]
            around = (
                (before[c] + after[c])
                + (pad_ref[z, cut[c], :] + pad_ref[z + 2, cut[c], :])
                + beside(e)
            )
            pot = e * (base + (1.0 - 2.0 * coupling) * squares[c]) - stiffness * around
            pot_ref[z, cut[c], :] = pot
            pushed = class_row(w, c) * pot
            numer[c] = numer[c] + pushed
            moved = e - time_step * pushed
            if last:
                moved = moved - refs["goal"][z, cut[c], :]
                extra_a[c] = extra_a[c] + class_row(step_w, c) * moved
            moved_ref[z, cut[c], :] = moved
            if first:
                for k in range(KINDS):
                    lin_ref[k, cut[c], :] += pot * class_row(level_now, k)
        denom = denom + w
        if last:
            extra_b = extra_b + step_w * step_w
        if first:
            level = level + level_now
        return tuple(numer), denom, tuple(extra_a), extra_b, level

    size = rows // CHUNKS

    def chunk(j, carry):
        for s in sides:
            s.wait(j)
        carry = lax.fori_loop(j * size, (j + 1) * size, line, carry)
        moved_out.start(j)
        pot_out.start(j)
        return carry

    zero = jnp.zeros((each, ny), jnp.float32)
    numer, denom, extra_a, extra_b, level = lax.fori_loop(
        0,
        CHUNKS,
        chunk,
        ((zero,) * KINDS, zero, (zero,) * KINDS if last else (), zero if last else (), zero if first else ()),
    )
    for name, ref in (("w", w_ref), ("sums", sums_ref)):
        outs.append(stream(name, ref, out=True))
        outs[-1].start()

    def row_of(parts, offset):
        return spread(
            jnp.concatenate([jnp.sum(v, axis=1, keepdims=True) for v in parts], axis=0), offset
        )

    def row_of_classes(tile, offset):
        column = jnp.sum(tile, axis=1, keepdims=True)
        return spread(
            jnp.concatenate(
                [jnp.broadcast_to(column[c : c + 1], (each, 1)) for c in range(KINDS)], axis=0
            ),
            offset,
        )

    row = row_of(numer, 0) + row_of_classes(denom, orders)
    if first:
        row = row + spread(jnp.sum(level, axis=1, keepdims=True)[:KINDS], 2 * orders)
    if last:
        row = row + row_of(extra_a, 2 * orders) + row_of_classes(extra_b, 3 * orders)
    copies_ref = refs["copies"]
    shape = copies_ref.shape
    if first:
        second = functools.reduce(
            jnp.add,
            [
                spread(jnp.sum(lin_ref[k], axis=1, keepdims=True), k * orders)
                for k in range(KINDS)
            ],
        )
        odd = lax.broadcasted_iota(jnp.int32, shape, 0) % 2 == 1
        copies_ref[...] = jnp.where(odd, second, row)
    else:
        copies_ref[...] = jnp.broadcast_to(row, shape)
    outs.append(stream("copies", copies_ref, out=True))
    outs[-1].start()
    outs.append(stream("send", moved_ref.at[pl.ds(jnp.where(core == 0, rows - 1, 0), 1)], out=True))
    outs[-1].start()
    for s in outs:
        s.wait()
    moved_out.wait_all()
    pot_out.wait_all()


def backward_kernel(step, refs):
    top, bottom = step == STEPS - 1, step == 0
    core_ref, mob_ref, births_ref, pad_ref = (refs[n] for n in ("core", "mob", "births", "pad"))
    own_ref, before_ref, after_ref = refs["own"], refs["before"], refs["after"]
    w_ref, sums_ref, pot_ref, cells_ref = (refs[n] for n in ("w", "sums", "pot", "cells"))
    adj_ref = refs["adj"]
    stream = refs["stream"]
    rows, orders, ny = own_ref.shape
    each = orders // KINDS
    cut = [slice(c * each, (c + 1) * each) for c in range(KINDS)]
    core = core_ref[0]

    ins = [stream("own", own_ref), stream("edge", refs["edge"]), stream("w", w_ref)]
    if not top:
        ins.append(stream("stats", refs["stats"]))
    if bottom:
        ins.append(stream("linear", refs["linear"]))
        final_in = stream("final", refs["final"])
    later_ins = [stream("sums", sums_ref)]
    if not bottom:
        later_ins.append(stream("wnext", refs["wnext"], part=rows))
    if not top and not bottom:
        later_ins.append(stream("mobin", refs["mobin"]))
    if step == 1:
        later_ins += [stream("sums0", refs["sums0"]), stream("stats0", refs["stats0"])]
    sides = [("before", before_ref), ("after", after_ref), ("cells", cells_ref), ("pot", pot_ref)]
    if step == 1:
        sides.append(("pot0", refs["pot0"]))
    sides = [stream(name, ref, CHUNKS) for name, ref in sides]
    if top:
        ins.append(stream("goal", refs["goal"]))
    for s in ins + later_ins:
        s.start()
    for j in range(CHUNKS):
        for s in sides:
            s.start(j)
    if bottom:
        final_in.start()

    total = jnp.sum(refs["got"][...], axis=0, keepdims=True)
    if top:
        raw = gather(total, orders, orders)
        lag = gather(total, 0, orders) / jnp.maximum(raw, 1.0)
        lag_adj = gather(total, 2 * orders, orders) + lag * gather(total, 3 * orders, orders)
    for s in ins:
        s.wait()
    if not top:
        lag = refs["stats"][0][:, :1]
        raw = refs["stats"][1][:, :1]
        lag_adj = gather(total, orders, orders)
    slope_column = lag_adj / jnp.maximum(raw, 1.0)
    keep = jnp.where(raw > 1.0, lag, 0.0)

    def wide(column):
        return [jnp.broadcast_to(column[cut[c]], (each, ny)) for c in range(KINDS)]

    slope = wide(slope_column)
    lag_wide = wide(lag)
    slope_keep = wide(slope_column * keep)
    table = tables(mob_ref, ny, True)
    outs = []

    def grown(value, place, c):
        weight = w_ref[place, pl.ds(c, 1), :]
        if top:
            value = value + (time_step * lag_wide[c]) * weight
        return value, weight * (slope[c] - time_step * value)

    def fill(z, carry):
        for c in range(KINDS):
            value, pushed = grown(own_ref[z, cut[c], :], z, c)
            pad_ref[z + 1, cut[c], :] = pushed
            if top:
                own_ref[z, cut[c], :] = value
                refs["goal"][z, cut[c], :] = value + refs["goal"][z, cut[c], :]
        return carry

    lax.fori_loop(0, rows, fill, 0, unroll=2)
    if top:
        outs.append(stream("final", refs["goal"], out=True))
        outs[-1].start()
    for c in range(KINDS):
        pushed = grown(refs["edge"][0, cut[c], :], 3 * rows, c)[1]
        pad_ref[0, cut[c], :] = jnp.where(core == 1, pushed, 0.0)
        pad_ref[rows + 1, cut[c], :] = jnp.where(core == 0, pushed, 0.0)
    for s in later_ins:
        s.wait()
    if step == 1:
        lag0 = wide(refs["stats0"][0][:, :1])
    if not bottom:
        adj_out = stream("adj", adj_ref, CHUNKS, out=True)

    def line(z, carry):
        mob, onward = carry
        sums = sums_ref[z]
        rolls = rolled(sums)
        summed = functools.reduce(jnp.add, rolls)
        act = active(births_ref, z, step)
        adj = [own_ref[z, cut[c], :] for c in range(KINDS)]
        cells = [cells_ref[z, cut[c], :] for c in range(KINDS)]
        pots = [pot_ref[z, cut[c], :] for c in range(KINDS)]
        pushed = [pad_ref[z + 1, cut[c], :] for c in range(KINDS)]
        drive = packed(
            [
                (slope[c] * pots[c] - slope_keep[c])
                - time_step * adj[c] * (pots[c] - lag_wide[c])
                for c in range(KINDS)
            ]
        )
        plain = drive / (1.0 + summed)
        drive = act * plain
        shared = total_rows(
            (2.0 * coupling)
            * functools.reduce(jnp.add, [pushed[c] * cells[c] for c in range(KINDS)])
            - (KINDS / SUBLANES) * (w_ref[z] * plain)
        )
        class_adj = 2.0 * (mixed(table, rolled(drive)) + shared)
        if not bottom:
            mob = tuple(m + drive * r for m, r in zip(mob, rolls))
        base = (6.0 * stiffness - 1.0) + (2.0 * coupling) * summed
        onward = list(onward)
        later = []
        for c in range(KINDS):
            around = (
                grown(before_ref[z, cut[c], :], rows + z, c)[1]
                + grown(after_ref[z, cut[c], :], 2 * rows + z, c)[1]
                + (pad_ref[z, cut[c], :] + pad_ref[z + 2, cut[c], :])
                + beside(pushed[c])
            )
            e = cells[c]
            new = (
                adj[c]
                + pushed[c] * (base + (3.0 - 6.0 * coupling) * (e * e))
                - stiffness * around
                + e * class_row(class_adj, c)
            )
            adj_ref[z, cut[c], :] = new
            if not bottom:
                onward[c] = onward[c] + refs["wnext"][z, pl.ds(c, 1), :] * new
            later.append(new)
        if step == 1:
            sums0 = rolled(refs["sums0"][z])
            gate = active(births_ref, z, 0) / (1.0 + functools.reduce(jnp.add, sums0))
            drive = (-time_step * gate) * packed(
                [later[c] * (refs["pot0"][z, cut[c], :] - lag0[c]) for c in range(KINDS)]
            )
            mob = tuple(m + drive * r for m, r in zip(mob, sums0))
        return mob, tuple(onward)

    size = rows // CHUNKS

    def chunk(j, carry):
        for s in sides:
            s.wait(j)
        carry = lax.fori_loop(j * size, (j + 1) * size, line, carry)
        if not bottom:
            adj_out.start(j)
        return carry

    zero = jnp.zeros((each, ny), jnp.float32)
    mob, onward = lax.fori_loop(
        0, CHUNKS, chunk, (() if bottom else (zero,) * KINDS, () if bottom else (zero,) * KINDS)
    )
    if bottom:
        lane = lax.broadcasted_iota(jnp.int32, (1, LANES), 1)
        row = jnp.where(lane < KINDS * KINDS, total, 0.0)
        lane = lax.broadcasted_iota(jnp.int32, (orders, LANES), 1)
        home = lax.broadcasted_iota(jnp.int32, (orders, LANES), 0) // each
        for k in range(KINDS):
            value = slope_column * refs["linear"][2 + k][:, :1]
            row = row + jnp.sum(
                jnp.where(lane == home * KINDS + k, value, 0.0), axis=0, keepdims=True
            )
        refs["mobility"][...] = jnp.broadcast_to(row, refs["mobility"].shape)
        parts = [refs["part0"], refs["part1"]]
        final_in.wait()
        pack(refs["rank"], refs["packed"], 0, refs["final"], parts)
        pack(refs["rank"], refs["packed"], 1, adj_ref, parts)
        outs.append(stream("packed", refs["packed"], out=True))
        outs[-1].start()
    else:
        row = time_step * spread(
            jnp.concatenate([jnp.sum(v, axis=1, keepdims=True) for v in onward], axis=0), orders
        )
        lane = lax.broadcasted_iota(jnp.int32, (KINDS, LANES), 1)
        kind = lax.broadcasted_iota(jnp.int32, (KINDS, LANES), 0)
        terms = jnp.zeros((1, LANES), jnp.float32)
        for d in range(KINDS):
            column = jnp.sum(mob[d], axis=1, keepdims=True)[:KINDS]
            spot = kind * KINDS + (kind + (KINDS - d)) % KINDS
            terms = terms + jnp.sum(jnp.where(lane == spot, column, 0.0), axis=0, keepdims=True)
        if not top:
            terms = terms + refs["mobin"][:1]
        if step == 1:
            row = row + terms
        else:
            refs["mobout"][...] = jnp.broadcast_to(terms, refs["mobout"].shape)
            outs.append(stream("mobout", refs["mobout"], out=True))
            outs[-1].start()
        refs["copies"][...] = jnp.broadcast_to(row, refs["copies"].shape)
        outs.append(stream("copies", refs["copies"], out=True))
        outs[-1].start()
        outs.append(
            stream("send", adj_ref.at[pl.ds(jnp.where(core == 0, rows - 1, 0), 1)], out=True)
        )
        outs[-1].start()
    for s in outs:
        s.wait()
    if not bottom:
        adj_out.wait_all()


def stepped(kernel, step, smem, vmem, ins, outs, direct, scratch):
    names = list(smem) + list(vmem) + list(ins)
    pinned = [
        v if n in ("before", "after", "edge") else pltpu.with_memory_space_constraint(v, pltpu.HBM)
        for n, v in ins.items()
    ]
    operands = [*smem.values(), *vmem.values(), *pinned]
    out_names = list(outs) + list(direct)
    buffers = {n: (v.shape, v.dtype) for n, v in ins.items() if n not in scratch.get("skip", ())}
    buffers.update({n: (s, jnp.float32) for n, s in scratch["extra"].items()})
    streamed = [("i", n) for n in ins] + [("o", n) for n in outs]
    sems = [pltpu.SemaphoreType.DMA((CHUNKS,))] * len(streamed)

    def body(*args):
        args = list(args)
        table = dict(zip(names, args))
        args = args[len(names) :]
        hbm_out = dict(zip(out_names, args))
        args = args[len(out_names) :]
        bufs = dict(zip(buffers, args))
        sem = dict(zip(streamed, args[len(buffers) :]))
        hbm_in = {n: table.pop(n) for n in ins}
        refs = {**table, **bufs, **{n: hbm_out[n] for n in direct}}

        def stream(name, ref, chunks=1, out=False, part=None):
            if out:
                return Stream(ref, hbm_out[name], sem["o", name], chunks)
            source = hbm_in[name]
            if part:
                source, ref = source.at[pl.ds(0, part)], ref.at[pl.ds(0, part)]
            return Stream(source, ref, sem["i", name], chunks)

        refs["stream"] = stream
        kernel(step, refs)

    result = pl.pallas_call(
        body,
        name=f"{kernel.__name__}_{step}",
        out_shape=[pltpu.HBM(s, jnp.float32) for s in outs.values()]
        + [jax.ShapeDtypeStruct(s, jnp.float32) for s in direct.values()],
        in_specs=[SMEM] * len(smem) + [VMEM] * len(vmem) + [HBM] * len(ins),
        out_specs=[HBM] * len(outs) + [VMEM] * len(direct),
        scratch_shapes=[pltpu.VMEM(s, d) for s, d in buffers.values()] + sems,
        compiler_params=pltpu.CompilerParams(vmem_limit_bytes=24 * 1024 * 1024),
    )(*operands)
    return dict(zip(out_names, result))


def unpack_kernel(rank_ref, got_ref, *refs):
    sources, arrays, local, rows, ny = got_ref.shape
    outs, parts = refs[:arrays], refs[arrays:]
    orders = sources * local
    strips = [slice(h * LANES, (h + 1) * LANES) for h in range(ny // LANES)]
    for a in range(arrays):
        for i in range(orders):
            for h, strip in enumerate(strips):
                parts[h][pl.ds(rank_ref[i], rows, stride=orders), :] = got_ref[
                    i // local, a, i % local, :, strip
                ]
        for h, strip in enumerate(strips):
            outs[a][:, strip] = parts[h][...]


def pack(rank_ref, out_ref, array, fields, parts):
    groups, _, local, rows, ny = out_ref.shape
    orders = groups * local
    strips = [slice(h * LANES, (h + 1) * LANES) for h in range(ny // LANES)]
    for z in range(rows):
        for h, strip in enumerate(strips):
            parts[h][pl.ds(z * orders, orders), :] = fields[z, :, strip]
    for i in range(orders):
        for h, strip in enumerate(strips):
            out_ref[i // local, array, i % local, :, strip] = parts[h][
                pl.ds(rank_ref[i], rows, stride=orders), :
            ]


VMEM = pl.BlockSpec(memory_space=pltpu.VMEM)
SMEM = pl.BlockSpec(memory_space=pltpu.SMEM)
HBM = pl.BlockSpec(memory_space=pltpu.HBM)


def call(kernel, name, smem, operands, outs, scratch=()):
    return pl.pallas_call(
        kernel,
        name=name,
        out_shape=[pltpu.HBM(s, jnp.float32) for s in outs],
        in_specs=[SMEM] * smem + [VMEM] * (len(operands) - smem),
        out_specs=[VMEM] * len(outs),
        scratch_shapes=[pltpu.VMEM(s, jnp.float32) for s in scratch],
        compiler_params=pltpu.CompilerParams(vmem_limit_bytes=16 * 1024 * 1024),
    )(*operands)


def on_device(initial, target, birth_step, classes, mobility):
    slabs, groups = lax.axis_size("slab"), lax.axis_size("grp")
    devices = slabs * groups
    me = lax.axis_index("grp")
    local, planes, nz, ny = initial.shape
    halves = groups // planes
    rows = nz // halves
    orders = local * groups
    core = (me % halves).astype(jnp.int32)
    plane = me // halves

    def along_x(step):
        pairs = []
        for i in range(slabs * planes):
            j = i + step
            if 0 <= j < slabs * planes:
                pairs += [(i * halves + c, j * halves + c) for c in range(halves)]
        return pairs

    swap = [(g, g ^ 1) for g in range(groups)]

    def faces_of(cells, edge):
        return (
            lax.ppermute(cells, AXES, along_x(1)),
            lax.ppermute(cells, AXES, along_x(-1)),
            lax.ppermute(edge, "grp", swap),
        )

    def everywhere(copies):
        return lax.all_to_all(copies, AXES, 0, 0, tiled=True)

    chain = [(i, i + 1) for i in range(slabs - 1)]
    births = jnp.concatenate(
        [
            lax.ppermute(birth_step[-1:], "slab", chain),
            birth_step,
            lax.ppermute(birth_step[:1], "slab", [(j, i) for i, j in chain]),
        ]
    )
    near = lax.dynamic_slice_in_dim(births, plane, 3, axis=0)
    mine = lax.dynamic_slice_in_dim(near, core * rows, rows, axis=1)
    other = lax.dynamic_slice_in_dim(near[1], jnp.where(core == 0, rows, rows - 1), 1, axis=0)
    births = jnp.concatenate(
        [mine[1], mine[0], mine[2], jnp.broadcast_to(other, (8, ny))], axis=0
    )

    both = jnp.stack([initial, target]).reshape(2, local, planes, halves, rows, ny)
    both = jnp.transpose(both, (2, 3, 0, 1, 4, 5)).reshape(groups, 2 * local * rows, ny)
    tag = jnp.pad(classes.astype(jnp.float32), (0, ny - local))
    tag = jnp.broadcast_to(tag[None, None], (groups, 8, ny))
    got = lax.all_to_all(jnp.concatenate([both, tag], axis=1), "grp", 0, 0, tiled=True)
    kind = got[:, 2 * local * rows, :local].reshape(orders).astype(jnp.int32)
    index = jnp.arange(orders, dtype=jnp.int32)
    ahead = (kind[None, :] < kind[:, None]) | (
        (kind[None, :] == kind[:, None]) & (index[None, :] < index[:, None])
    )
    rank = jnp.sum(ahead.astype(jnp.int32), axis=1)
    got = got[:, : 2 * local * rows].reshape(groups, 2, local, rows, ny)
    flat = (rows * orders, ny)
    strips = [(rows * orders, LANES)] * (ny // LANES)
    cells, goal = call(
        unpack_kernel, "unpack", 1, [rank, got], [flat] * 2, strips
    )
    shape = (rows, orders, ny)
    cells, goal = cells.reshape(shape), goal.reshape(shape)
    smem = {"core": core.reshape(1), "mob": mobility}
    places = 3 * rows + 1
    tiles, own_tiles = (places, SUBLANES, ny), (rows, SUBLANES, ny)
    padded = (rows + 2, orders, ny)
    edge_shape = (1, orders, ny)

    own = cells
    edge = lax.dynamic_slice_in_dim(cells, jnp.where(core == 0, rows - 1, 0), 1, axis=0)
    stored = []
    got = weights = None
    for step in range(STEPS):
        first, last = step == 0, step == STEPS - 1
        before, after, beyond = faces_of(own, edge)
        vmem = {"births": births}
        ins = {"own": own, "before": before, "after": after, "edge": beyond}
        outs = {"moved": shape, "send": edge_shape, "pot": shape, "sums": own_tiles, "w": tiles}
        outs["copies"] = (2 * devices if first else devices, LANES)
        extra = {"pad": padded, **{n: s for n, s in outs.items() if n != "send"}}
        if first:
            extra["lin"] = (KINDS, orders, ny)
        else:
            vmem["got"] = got
            ins["wprev"] = weights
            outs["cells"] = shape
            outs["stats"] = (2 + (KINDS if step == 1 else 0), orders, LANES)
            extra["stats"] = outs["stats"]
        if last:
            ins["goal"] = goal
        result = stepped(
            forward_kernel, step, smem, vmem, ins, outs, {}, {"skip": ("own",), "extra": extra}
        )
        if not first:
            cells = result["cells"]
            stored[-1]["stats"] = result["stats"]
        own, edge, weights = result["moved"], result["send"], result["w"]
        stored.append({"cells": cells, **{n: result[n] for n in ("pot", "sums", "w")}})
        got = everywhere(result["copies"])
    terms = None
    for step in range(STEPS - 1, -1, -1):
        top, bottom = step == STEPS - 1, step == 0
        before, after, beyond = faces_of(own, edge)
        ins = {"own": own, "before": before, "after": after, "edge": beyond, **stored[step]}
        outs, direct = ({} if bottom else {"adj": shape}), {}
        extra = {"pad": padded, "adj": shape}
        if top:
            ins["goal"] = goal
            outs["final"] = shape
        else:
            if bottom:
                ins["linear"] = stored[0]["stats"]
            else:
                ins["mobin"] = terms
        if bottom:
            direct["mobility"] = (SUBLANES, LANES)
            ins["final"] = final_state
            outs["packed"] = extra["packed"] = (groups, 2, local, rows, ny)
            extra["part0"] = extra["part1"] = strips[0]
        else:
            ins["wnext"] = stored[step - 1]["w"]
            outs["send"] = edge_shape
            outs["copies"] = extra["copies"] = (devices, LANES)
            if step > 1:
                outs["mobout"] = extra["mobout"] = (SUBLANES, LANES)
        if step == 1:
            ins.update({n + "0": stored[0][n] for n in ("pot", "sums", "stats")})
        result = stepped(
            backward_kernel,
            step,
            {**smem, "rank": rank} if bottom else smem,
            {"births": births, "got": got},
            ins,
            outs,
            direct,
            {"extra": extra},
        )
        own = result.get("adj")
        if top:
            final_state = result["final"]
        if bottom:
            mobility_sum = result["mobility"]
        else:
            edge, terms = result["send"], result.get("mobout")
            got = everywhere(result["copies"])

    both = result["packed"]
    both = both.reshape(groups, 2 * local * rows, ny)
    both = lax.all_to_all(both, "grp", 0, 0, tiled=True)
    both = both.reshape(planes, halves, 2, local, rows, ny)
    both = jnp.transpose(both, (2, 3, 0, 1, 4, 5)).reshape(2, local, planes, nz, ny)
    scale = time_step * (planes * slabs) * nz
    mobility_sum = mobility_sum[0, : KINDS * KINDS].reshape(KINDS, KINDS)
    return both[0], both[1], mobility_sum / scale


def solution(mesh):
    return jax.shard_map(
        on_device,
        mesh=mesh,
        in_specs=(
            P("grp", "slab", None, None),
            P("grp", "slab", None, None),
            P("slab", None, None),
            P("grp"),
            P(),
        ),
        out_specs=(P("grp", "slab", None, None), P("grp", "slab", None, None), P()),
        check_vma=False,
    )
```

```python
import functools

import jax
import jax.numpy as jnp
from jax import lax
from jax.experimental import pallas as pl
from jax.experimental.pallas import tpu as pltpu
from jax.sharding import PartitionSpec as P

STEPS = 4
coupling = 0.3
stiffness = 1.0
time_step = 0.06
LANES = 128
SUBLANES = 8
KINDS = 4
CHUNKS = 4
AXES = ("slab", "grp")


def spread(column, offset):
    n = column.shape[0]
    lane = lax.broadcasted_iota(jnp.int32, (n, LANES), 1)
    row = lax.broadcasted_iota(jnp.int32, (n, LANES), 0)
    return jnp.sum(jnp.where(lane == row + offset, column, 0.0), axis=0, keepdims=True)


def gather(total, offset, n):
    lane = lax.broadcasted_iota(jnp.int32, (n, LANES), 1)
    row = lax.broadcasted_iota(jnp.int32, (n, LANES), 0)
    return jnp.sum(jnp.where(lane == row + offset, total, 0.0), axis=1, keepdims=True)


def beside(cells):
    width = cells.shape[-1]
    lane = lax.broadcasted_iota(jnp.int32, cells.shape, cells.ndim - 1)
    left = jnp.where(lane == 0, 0.0, pltpu.roll(cells, 1, cells.ndim - 1))
    right = jnp.where(lane == width - 1, 0.0, pltpu.roll(cells, width - 1, cells.ndim - 1))
    return left + right


def rolled(tile):
    return [tile] + [pltpu.roll(tile, d, 0) for d in range(1, KINDS)]


def packed(values):
    row = lax.broadcasted_iota(jnp.int32, values[0].shape, 0)
    step = 1
    while len(values) > 1:
        mask = (row // step) % 2 == 0
        values = [
            jnp.where(mask, u, v) + pltpu.roll(jnp.where(mask, v, u), step, 0)
            for u, v in zip(values[0::2], values[1::2])
        ]
        step *= 2
    (tile,) = values
    while step < SUBLANES:
        tile = tile + pltpu.roll(tile, step, 0)
        step *= 2
    return tile


def total_rows(tile):
    step = 1
    while step < SUBLANES:
        tile = tile + pltpu.roll(tile, step, 0)
        step *= 2
    return tile


def class_row(tile, c):
    return jnp.broadcast_to(tile[c : c + 1, :], tile.shape)


def tables(mob_ref, ny, transposed):
    row = lax.broadcasted_iota(jnp.int32, (SUBLANES, ny), 0) % KINDS
    tiles = []
    for d in range(KINDS):
        tile = jnp.zeros((SUBLANES, ny), jnp.float32)
        for c in range(KINDS):
            k = (c - d) % KINDS
            value = mob_ref[k, c] if transposed else mob_ref[c, k]
            tile = jnp.where(row == c, value, tile)
        tiles.append(tile)
    return tiles


def mixed(table, rolls):
    return functools.reduce(jnp.add, [t * r for t, r in zip(table, rolls)])


def active(births_ref, row, step):
    return jnp.where(births_ref[pl.ds(row, 1), :] <= step, 1.0, 0.0)


class Stream:
    def __init__(self, source, target, sems, chunks=1):
        self.source, self.target, self.sems, self.chunks = source, target, sems, chunks

    def copy(self, j):
        if self.chunks == 1:
            return pltpu.make_async_copy(self.source, self.target, self.sems.at[0])
        size = self.target.shape[0] // self.chunks
        return pltpu.make_async_copy(
            self.source.at[pl.ds(j * size, size)],
            self.target.at[pl.ds(j * size, size)],
            self.sems.at[j],
        )

    def start(self, j=0):
        self.copy(j).start()

    def start_all(self):
        for j in range(self.chunks):
            self.start(j)

    def wait(self, j=0):
        self.copy(j).wait()

    def wait_all(self):
        for j in range(self.chunks):
            self.wait(j)


def forward_kernel(step, refs):
    first, last = step == 0, step == STEPS - 1
    core_ref, mob_ref, births_ref, pad_ref = (refs[n] for n in ("core", "mob", "births", "pad"))
    before_ref, after_ref = refs["before"], refs["after"]
    w_ref, sums_ref, moved_ref, pot_ref = (refs[n] for n in ("w", "sums", "moved", "pot"))
    stream = refs["stream"]
    rows, orders, ny = moved_ref.shape
    each = orders // KINDS
    cut = [slice(c * each, (c + 1) * each) for c in range(KINDS)]
    core = core_ref[0]
    inner = pad_ref.at[pl.ds(1, rows)]

    own_in = stream("own", inner)
    edge_in = stream("edge", refs["edge"])
    ins = [own_in, edge_in]
    if not first:
        wprev_ref = refs["wprev"]
        ins.append(stream("wprev", wprev_ref))
    for s in ins:
        s.start()
    sides = [stream("before", before_ref, CHUNKS), stream("after", after_ref, CHUNKS)]
    if last:
        sides.append(stream("goal", refs["goal"], CHUNKS))
    for j in range(CHUNKS):
        for s in sides:
            s.start(j)
    outs = []
    if first:
        lin_ref = refs["lin"]
        lin_ref[...] = jnp.zeros_like(lin_ref)
    else:
        stats_ref = refs["stats"]
        got = refs["got"][...]
        if step == 1:
            odd = lax.broadcasted_iota(jnp.int32, got.shape, 0) % 2 == 1
            second = jnp.sum(jnp.where(odd, got, 0.0), axis=0, keepdims=True)
            got = jnp.where(odd, 0.0, got)
        total = jnp.sum(got, axis=0, keepdims=True)
        raw = gather(total, orders, orders)
        lag = gather(total, 0, orders) / jnp.maximum(raw, 1.0)
        stats_ref[0] = jnp.broadcast_to(lag, (orders, LANES))
        stats_ref[1] = jnp.broadcast_to(raw, (orders, LANES))
        if step == 1:
            lane = lax.broadcasted_iota(jnp.int32, (1, LANES), 1)
            for k in range(KINDS):
                base = gather(second, k * orders, orders)
                level = jnp.sum(
                    jnp.where(lane == 2 * orders + k, total, 0.0), axis=1, keepdims=True
                )
                value = base - jnp.where(raw > 1.0, lag, 0.0) * level
                stats_ref[2 + k] = jnp.broadcast_to(value, (orders, LANES))
        pace = [jnp.broadcast_to(lag[cut[c]] * time_step, (each, ny)) for c in range(KINDS)]
        stats_out = stream("stats", stats_ref, out=True)
        stats_out.start()
        outs.append(stats_out)
    table = tables(mob_ref, ny, False)

    def grown(value, place, c):
        if first:
            return value
        return value + pace[c] * wprev_ref[place, pl.ds(c, 1), :]

    def rates_of(squares, place):
        sums = packed(squares)
        rolls = rolled(sums)
        summed = functools.reduce(jnp.add, rolls)
        gate = active(births_ref, place, step) / (1.0 + summed)
        w = gate * mixed(table, rolls)
        w_ref[place] = w
        return sums, summed, gate, w

    for s in ins:
        s.wait()
    if not first:

        def fill(z, carry):
            for c in range(KINDS):
                pad_ref[z + 1, cut[c], :] = grown(pad_ref[z + 1, cut[c], :], z, c)
            return carry

        lax.fori_loop(0, rows, fill, 0, unroll=2)
        cells_out = stream("cells", inner, out=True)
        cells_out.start()
        outs.append(cells_out)
    edge = [grown(refs["edge"][0, cut[c], :], 3 * rows, c) for c in range(KINDS)]
    for c in range(KINDS):
        pad_ref[0, cut[c], :] = jnp.where(core == 1, edge[c], 0.0)
        pad_ref[rows + 1, cut[c], :] = jnp.where(core == 0, edge[c], 0.0)
    rates_of([e * e for e in edge], 3 * rows)

    moved_out = stream("moved", moved_ref, CHUNKS, out=True)
    pot_out = stream("pot", pot_ref, CHUNKS, out=True)

    def line(z, carry):
        numer, denom, extra_a, extra_b, level = carry
        before = [grown(before_ref[z, cut[c], :], rows + z, c) for c in range(KINDS)]
        rates_of([v * v for v in before], rows + z)
        after = [grown(after_ref[z, cut[c], :], 2 * rows + z, c) for c in range(KINDS)]
        rates_of([v * v for v in after], 2 * rows + z)
        cells = [pad_ref[z + 1, cut[c], :] for c in range(KINDS)]
        squares = [e * e for e in cells]
        sums, summed, gate, w = rates_of(squares, z)
        sums_ref[z] = sums
        level_now = gate * sums
        step_w = time_step * w
        base = (6.0 * stiffness - 1.0) + (2.0 * coupling) * summed
        numer, extra_a = list(numer), list(extra_a)
        for c in range(KINDS):
            e = cells[c]
            around = (
                (before[c] + after[c])
                + (pad_ref[z, cut[c], :] + pad_ref[z + 2, cut[c], :])
                + beside(e)
            )
            pot = e * (base + (1.0 - 2.0 * coupling) * squares[c]) - stiffness * around
            pot_ref[z, cut[c], :] = pot
            pushed = class_row(w, c) * pot
            numer[c] = numer[c] + pushed
            moved = e - time_step * pushed
            if last:
                moved = moved - refs["goal"][z, cut[c], :]
                extra_a[c] = extra_a[c] + class_row(step_w, c) * moved
            moved_ref[z, cut[c], :] = moved
            if first:
                for k in range(KINDS):
                    lin_ref[k, cut[c], :] += pot * class_row(level_now, k)
        denom = denom + w
        if last:
            extra_b = extra_b + step_w * step_w
        if first:
            level = level + level_now
        return tuple(numer), denom, tuple(extra_a), extra_b, level

    size = rows // CHUNKS

    def chunk(j, carry):
        for s in sides:
            s.wait(j)
        carry = lax.fori_loop(j * size, (j + 1) * size, line, carry)
        moved_out.start(j)
        pot_out.start(j)
        return carry

    zero = jnp.zeros((each, ny), jnp.float32)
    numer, denom, extra_a, extra_b, level = lax.fori_loop(
        0,
        CHUNKS,
        chunk,
        ((zero,) * KINDS, zero, (zero,) * KINDS if last else (), zero if last else (), zero if first else ()),
    )
    for name, ref in (("w", w_ref), ("sums", sums_ref)):
        outs.append(stream(name, ref, out=True))
        outs[-1].start()

    def row_of(parts, offset):
        return spread(
            jnp.concatenate([jnp.sum(v, axis=1, keepdims=True) for v in parts], axis=0), offset
        )

    def row_of_classes(tile, offset):
        column = jnp.sum(tile, axis=1, keepdims=True)
        return spread(
            jnp.concatenate(
                [jnp.broadcast_to(column[c : c + 1], (each, 1)) for c in range(KINDS)], axis=0
            ),
            offset,
        )

    row = row_of(numer, 0) + row_of_classes(denom, orders)
    if first:
        row = row + spread(jnp.sum(level, axis=1, keepdims=True)[:KINDS], 2 * orders)
    if last:
        row = row + row_of(extra_a, 2 * orders) + row_of_classes(extra_b, 3 * orders)
    copies_ref = refs["copies"]
    shape = copies_ref.shape
    if first:
        second = functools.reduce(
            jnp.add,
            [
                spread(jnp.sum(lin_ref[k], axis=1, keepdims=True), k * orders)
                for k in range(KINDS)
            ],
        )
        odd = lax.broadcasted_iota(jnp.int32, shape, 0) % 2 == 1
        copies_ref[...] = jnp.where(odd, second, row)
    else:
        copies_ref[...] = jnp.broadcast_to(row, shape)
    outs.append(stream("copies", copies_ref, out=True))
    outs[-1].start()
    outs.append(stream("send", moved_ref.at[pl.ds(jnp.where(core == 0, rows - 1, 0), 1)], out=True))
    outs[-1].start()
    for s in outs:
        s.wait()
    moved_out.wait_all()
    pot_out.wait_all()


def backward_kernel(step, refs):
    top, bottom = step == STEPS - 1, step == 0
    core_ref, mob_ref, births_ref, pad_ref = (refs[n] for n in ("core", "mob", "births", "pad"))
    own_ref, before_ref, after_ref = refs["own"], refs["before"], refs["after"]
    w_ref, sums_ref, pot_ref, cells_ref = (refs[n] for n in ("w", "sums", "pot", "cells"))
    adj_ref = refs["adj"]
    stream = refs["stream"]
    rows, orders, ny = own_ref.shape
    each = orders // KINDS
    cut = [slice(c * each, (c + 1) * each) for c in range(KINDS)]
    core = core_ref[0]

    ins = [stream("own", own_ref), stream("edge", refs["edge"]), stream("w", w_ref)]
    if not top:
        ins.append(stream("stats", refs["stats"]))
    if bottom:
        ins.append(stream("linear", refs["linear"]))
        final_in = stream("final", refs["final"])
    later_ins = [stream("sums", sums_ref)]
    if not bottom:
        later_ins.append(stream("wnext", refs["wnext"], part=rows))
    if not top and not bottom:
        later_ins.append(stream("mobin", refs["mobin"]))
    if step == 1:
        later_ins += [stream("sums0", refs["sums0"]), stream("stats0", refs["stats0"])]
    sides = [("before", before_ref), ("after", after_ref), ("cells", cells_ref), ("pot", pot_ref)]
    if step == 1:
        sides.append(("pot0", refs["pot0"]))
    sides = [stream(name, ref, CHUNKS) for name, ref in sides]
    if top:
        ins.append(stream("goal", refs["goal"]))
    for s in ins + later_ins:
        s.start()
    for j in range(CHUNKS):
        for s in sides:
            s.start(j)
    if bottom:
        final_in.start()

    total = jnp.sum(refs["got"][...], axis=0, keepdims=True)
    if top:
        raw = gather(total, orders, orders)
        lag = gather(total, 0, orders) / jnp.maximum(raw, 1.0)
        lag_adj = gather(total, 2 * orders, orders) + lag * gather(total, 3 * orders, orders)
    for s in ins:
        s.wait()
    if not top:
        lag = refs["stats"][0][:, :1]
        raw = refs["stats"][1][:, :1]
        lag_adj = gather(total, orders, orders)
    slope_column = lag_adj / jnp.maximum(raw, 1.0)
    keep = jnp.where(raw > 1.0, lag, 0.0)

    def wide(column):
        return [jnp.broadcast_to(column[cut[c]], (each, ny)) for c in range(KINDS)]

    slope = wide(slope_column)
    lag_wide = wide(lag)
    slope_keep = wide(slope_column * keep)
    table = tables(mob_ref, ny, True)
    outs = []

    def grown(value, place, c):
        weight = w_ref[place, pl.ds(c, 1), :]
        if top:
            value = value + (time_step * lag_wide[c]) * weight
        return value, weight * (slope[c] - time_step * value)

    def fill(z, carry):
        for c in range(KINDS):
            value, pushed = grown(own_ref[z, cut[c], :], z, c)
            pad_ref[z + 1, cut[c], :] = pushed
            if top:
                own_ref[z, cut[c], :] = value
                refs["goal"][z, cut[c], :] = value + refs["goal"][z, cut[c], :]
        return carry

    lax.fori_loop(0, rows, fill, 0, unroll=2)
    if top:
        outs.append(stream("final", refs["goal"], out=True))
        outs[-1].start()
    for c in range(KINDS):
        pushed = grown(refs["edge"][0, cut[c], :], 3 * rows, c)[1]
        pad_ref[0, cut[c], :] = jnp.where(core == 1, pushed, 0.0)
        pad_ref[rows + 1, cut[c], :] = jnp.where(core == 0, pushed, 0.0)
    for s in later_ins:
        s.wait()
    if step == 1:
        lag0 = wide(refs["stats0"][0][:, :1])
    if not bottom:
        adj_out = stream("adj", adj_ref, CHUNKS, out=True)

    def line(z, carry):
        mob, onward = carry
        sums = sums_ref[z]
        rolls = rolled(sums)
        summed = functools.reduce(jnp.add, rolls)
        act = active(births_ref, z, step)
        adj = [own_ref[z, cut[c], :] for c in range(KINDS)]
        cells = [cells_ref[z, cut[c], :] for c in range(KINDS)]
        pots = [pot_ref[z, cut[c], :] for c in range(KINDS)]
        pushed = [pad_ref[z + 1, cut[c], :] for c in range(KINDS)]
        drive = packed(
            [
                (slope[c] * pots[c] - slope_keep[c])
                - time_step * adj[c] * (pots[c] - lag_wide[c])
                for c in range(KINDS)
            ]
        )
        plain = drive / (1.0 + summed)
        drive = act * plain
        shared = total_rows(
            (2.0 * coupling)
            * functools.reduce(jnp.add, [pushed[c] * cells[c] for c in range(KINDS)])
            - (KINDS / SUBLANES) * (w_ref[z] * plain)
        )
        class_adj = 2.0 * (mixed(table, rolled(drive)) + shared)
        if not bottom:
            mob = tuple(m + drive * r for m, r in zip(mob, rolls))
        base = (6.0 * stiffness - 1.0) + (2.0 * coupling) * summed
        onward = list(onward)
        later = []
        for c in range(KINDS):
            around = (
                grown(before_ref[z, cut[c], :], rows + z, c)[1]
                + grown(after_ref[z, cut[c], :], 2 * rows + z, c)[1]
                + (pad_ref[z, cut[c], :] + pad_ref[z + 2, cut[c], :])
                + beside(pushed[c])
            )
            e = cells[c]
            new = (
                adj[c]
                + pushed[c] * (base + (3.0 - 6.0 * coupling) * (e * e))
                - stiffness * around
                + e * class_row(class_adj, c)
            )
            adj_ref[z, cut[c], :] = new
            if not bottom:
                onward[c] = onward[c] + refs["wnext"][z, pl.ds(c, 1), :] * new
            later.append(new)
        if step == 1:
            sums0 = rolled(refs["sums0"][z])
            gate = active(births_ref, z, 0) / (1.0 + functools.reduce(jnp.add, sums0))
            drive = (-time_step * gate) * packed(
                [later[c] * (refs["pot0"][z, cut[c], :] - lag0[c]) for c in range(KINDS)]
            )
            mob = tuple(m + drive * r for m, r in zip(mob, sums0))
        return mob, tuple(onward)

    size = rows // CHUNKS

    def chunk(j, carry):
        for s in sides:
            s.wait(j)
        carry = lax.fori_loop(j * size, (j + 1) * size, line, carry)
        if not bottom:
            adj_out.start(j)
        return carry

    zero = jnp.zeros((each, ny), jnp.float32)
    mob, onward = lax.fori_loop(
        0, CHUNKS, chunk, (() if bottom else (zero,) * KINDS, () if bottom else (zero,) * KINDS)
    )
    if bottom:
        lane = lax.broadcasted_iota(jnp.int32, (1, LANES), 1)
        row = jnp.where(lane < KINDS * KINDS, total, 0.0)
        lane = lax.broadcasted_iota(jnp.int32, (orders, LANES), 1)
        home = lax.broadcasted_iota(jnp.int32, (orders, LANES), 0) // each
        for k in range(KINDS):
            value = slope_column * refs["linear"][2 + k][:, :1]
            row = row + jnp.sum(
                jnp.where(lane == home * KINDS + k, value, 0.0), axis=0, keepdims=True
            )
        refs["mobility"][...] = jnp.broadcast_to(row, refs["mobility"].shape)
        parts = [refs["part0"], refs["part1"]]
        final_in.wait()
        pack(refs["rank"], refs["packed"], 0, refs["final"], parts)
        pack(refs["rank"], refs["packed"], 1, adj_ref, parts)
        outs.append(stream("packed", refs["packed"], out=True))
        outs[-1].start()
    else:
        row = time_step * spread(
            jnp.concatenate([jnp.sum(v, axis=1, keepdims=True) for v in onward], axis=0), orders
        )
        lane = lax.broadcasted_iota(jnp.int32, (KINDS, LANES), 1)
        kind = lax.broadcasted_iota(jnp.int32, (KINDS, LANES), 0)
        terms = jnp.zeros((1, LANES), jnp.float32)
        for d in range(KINDS):
            column = jnp.sum(mob[d], axis=1, keepdims=True)[:KINDS]
            spot = kind * KINDS + (kind + (KINDS - d)) % KINDS
            terms = terms + jnp.sum(jnp.where(lane == spot, column, 0.0), axis=0, keepdims=True)
        if not top:
            terms = terms + refs["mobin"][:1]
        if step == 1:
            row = row + terms
        else:
            refs["mobout"][...] = jnp.broadcast_to(terms, refs["mobout"].shape)
            outs.append(stream("mobout", refs["mobout"], out=True))
            outs[-1].start()
        refs["copies"][...] = jnp.broadcast_to(row, refs["copies"].shape)
        outs.append(stream("copies", refs["copies"], out=True))
        outs[-1].start()
        outs.append(
            stream("send", adj_ref.at[pl.ds(jnp.where(core == 0, rows - 1, 0), 1)], out=True)
        )
        outs[-1].start()
    for s in outs:
        s.wait()
    if not bottom:
        adj_out.wait_all()


def stepped(kernel, step, smem, vmem, ins, outs, direct, scratch):
    names = list(smem) + list(vmem) + list(ins)
    pinned = [
        v if n in ("before", "after", "edge") else pltpu.with_memory_space_constraint(v, pltpu.HBM)
        for n, v in ins.items()
    ]
    operands = [*smem.values(), *vmem.values(), *pinned]
    out_names = list(outs) + list(direct)
    buffers = {n: (v.shape, v.dtype) for n, v in ins.items() if n not in scratch.get("skip", ())}
    buffers.update({n: (s, jnp.float32) for n, s in scratch["extra"].items()})
    streamed = [("i", n) for n in ins] + [("o", n) for n in outs]
    sems = [pltpu.SemaphoreType.DMA((CHUNKS,))] * len(streamed)

    def body(*args):
        args = list(args)
        table = dict(zip(names, args))
        args = args[len(names) :]
        hbm_out = dict(zip(out_names, args))
        args = args[len(out_names) :]
        bufs = dict(zip(buffers, args))
        sem = dict(zip(streamed, args[len(buffers) :]))
        hbm_in = {n: table.pop(n) for n in ins}
        refs = {**table, **bufs, **{n: hbm_out[n] for n in direct}}

        def stream(name, ref, chunks=1, out=False, part=None):
            if out:
                return Stream(ref, hbm_out[name], sem["o", name], chunks)
            source = hbm_in[name]
            if part:
                source, ref = source.at[pl.ds(0, part)], ref.at[pl.ds(0, part)]
            return Stream(source, ref, sem["i", name], chunks)

        refs["stream"] = stream
        kernel(step, refs)

    result = pl.pallas_call(
        body,
        name=f"{kernel.__name__}_{step}",
        out_shape=[pltpu.HBM(s, jnp.float32) for s in outs.values()]
        + [jax.ShapeDtypeStruct(s, jnp.float32) for s in direct.values()],
        in_specs=[SMEM] * len(smem) + [VMEM] * len(vmem) + [HBM] * len(ins),
        out_specs=[HBM] * len(outs) + [VMEM] * len(direct),
        scratch_shapes=[pltpu.VMEM(s, d) for s, d in buffers.values()] + sems,
        compiler_params=pltpu.CompilerParams(vmem_limit_bytes=24 * 1024 * 1024),
    )(*operands)
    return dict(zip(out_names, result))


def places(groups, flip):
    ring = [(0, 0), (0, 1), (1, 1), (1, 0)]
    found = []
    for g in range(groups):
        pair, half = ring[g // 2]
        found.append((2 * (pair ^ flip) + g % 2, half))
    return found


def scatter_kernel(
    flip_ref, kinds_ref, first_ref, second_ref, out_ref, tag_ref, stage_a, stage_b, sems, sems_in
):
    groups, blocks, rows, ny = out_ref.shape
    local = first_ref.shape[0]
    loads = [
        pltpu.make_async_copy(ref.at[i], stage.at[i], sems_in.at[a * local + i])
        for a, (ref, stage) in enumerate(((first_ref, stage_a), (second_ref, stage_b)))
        for i in range(local)
    ]
    for c in loads:
        c.start()
    lane = lax.broadcasted_iota(jnp.int32, (rows, ny), 1)
    tag = jnp.zeros((rows, ny), jnp.float32)
    for i in range(local):
        tag = jnp.where(lane == i, kinds_ref[i].astype(jnp.float32), tag)
    tag_ref[...] = tag
    copies = []
    for g, (plane, half) in enumerate(places(groups, 0)):
        plane = plane ^ (2 * flip_ref[0])
        for a, ref in enumerate((stage_a, stage_b)):
            copies.append(
                pltpu.make_async_copy(
                    ref.at[:, plane, pl.ds(half * rows, rows), :],
                    out_ref.at[g, pl.ds(a * local, local)],
                    sems.at[3 * g + a],
                )
            )
        copies.append(
            pltpu.make_async_copy(tag_ref, out_ref.at[g, blocks - 1], sems.at[3 * g + 2])
        )
    for c in loads:
        c.wait()
    for c in copies:
        c.start()
    for c in copies:
        c.wait()


def collect_kernel(flip_ref, got_ref, first_ref, second_ref, sems):
    groups, _, local, rows, ny = got_ref.shape
    copies = []
    for g, (plane, half) in enumerate(places(groups, 0)):
        plane = plane ^ (2 * flip_ref[0])
        for a, ref in enumerate((first_ref, second_ref)):
            copies.append(
                pltpu.make_async_copy(
                    got_ref.at[g, a],
                    ref.at[:, plane, pl.ds(half * rows, rows), :],
                    sems.at[2 * g + a],
                )
            )
    for c in copies:
        c.start()
    for c in copies:
        c.wait()


def unpack_kernel(rank_ref, got_ref, *refs):
    sources, blocks, rows, ny = got_ref.shape
    arrays = 2
    local = blocks // arrays
    outs, parts = refs[:arrays], refs[arrays:]
    orders = sources * local
    strips = [slice(h * LANES, (h + 1) * LANES) for h in range(ny // LANES)]
    for a in range(arrays):
        for i in range(orders):
            for h, strip in enumerate(strips):
                parts[h][pl.ds(rank_ref[i], rows, stride=orders), :] = got_ref[
                    i // local, a * local + i % local, :, strip
                ]
        for h, strip in enumerate(strips):
            outs[a][:, strip] = parts[h][...]


def pack(rank_ref, out_ref, array, fields, parts):
    groups, _, local, rows, ny = out_ref.shape
    orders = groups * local
    strips = [slice(h * LANES, (h + 1) * LANES) for h in range(ny // LANES)]
    for z in range(rows):
        for h, strip in enumerate(strips):
            parts[h][pl.ds(z * orders, orders), :] = fields[z, :, strip]
    for i in range(orders):
        for h, strip in enumerate(strips):
            out_ref[i // local, array, i % local, :, strip] = parts[h][
                pl.ds(rank_ref[i], rows, stride=orders), :
            ]


VMEM = pl.BlockSpec(memory_space=pltpu.VMEM)
SMEM = pl.BlockSpec(memory_space=pltpu.SMEM)
HBM = pl.BlockSpec(memory_space=pltpu.HBM)


def call(kernel, name, smem, operands, outs, scratch=()):
    return pl.pallas_call(
        kernel,
        name=name,
        out_shape=[pltpu.HBM(s, jnp.float32) for s in outs],
        in_specs=[SMEM] * smem + [VMEM] * (len(operands) - smem),
        out_specs=[VMEM] * len(outs),
        scratch_shapes=[pltpu.VMEM(s, jnp.float32) for s in scratch],
        compiler_params=pltpu.CompilerParams(vmem_limit_bytes=16 * 1024 * 1024),
    )(*operands)


def on_device(initial, target, birth_step, classes, mobility):
    slabs, groups = lax.axis_size("slab"), lax.axis_size("grp")
    devices = slabs * groups
    slab, me = lax.axis_index("slab"), lax.axis_index("grp")
    local, planes, nz, ny = initial.shape
    rows = nz * planes // groups
    orders = local * groups
    flip = slab % 2
    chip, core = me // 2, me % 2
    half = ((chip == 1) | (chip == 2)).astype(jnp.int32)
    plane = 2 * ((chip // 2) ^ flip) + core

    across = []
    for i in range(slabs * planes // 2 - 1):
        i = 2 * i + 1
        for z in range(2):
            ends = []
            for x in (i, i + 1):
                where = places(groups, x // planes % 2).index((x % planes, z))
                ends.append(x // planes * groups + where)
            across += [tuple(ends), tuple(ends[::-1])]

    def faces_of(cells, edge):
        return (
            lax.ppermute(cells, AXES, across),
            lax.ppermute(cells, "grp", [(g, g ^ 1) for g in range(groups)]),
            lax.ppermute(edge, "grp", [(g, g ^ 2) for g in range(groups)]),
        )

    def everywhere(copies):
        return lax.all_to_all(copies, AXES, 0, 0, tiled=True)

    chain = [(i, i + 1) for i in range(slabs - 1)]
    births = jnp.concatenate(
        [
            lax.ppermute(birth_step[-1:], "slab", chain),
            birth_step,
            lax.ppermute(birth_step[:1], "slab", [(j, i) for i, j in chain]),
        ]
    )
    near = lax.dynamic_slice_in_dim(births, plane, 3, axis=0)
    mine = lax.dynamic_slice_in_dim(near, half * rows, rows, axis=1)
    other = lax.dynamic_slice_in_dim(near[1], jnp.where(half == 0, rows, rows - 1), 1, axis=0)
    first, second = jnp.where(core == 0, mine[0], mine[2]), jnp.where(core == 0, mine[2], mine[0])
    births = jnp.concatenate(
        [mine[1], first, second, jnp.broadcast_to(other, (SUBLANES, ny))], axis=0
    )

    flip = flip.astype(jnp.int32).reshape(1)
    block = (groups, 2 * local + 1, rows, ny)
    message = pl.pallas_call(
        scatter_kernel,
        name="scatter",
        out_shape=pltpu.HBM(block, jnp.float32),
        in_specs=[SMEM, SMEM, HBM, HBM],
        out_specs=HBM,
        scratch_shapes=[
            pltpu.VMEM((rows, ny), jnp.float32),
            pltpu.VMEM(initial.shape, jnp.float32),
            pltpu.VMEM(initial.shape, jnp.float32),
            pltpu.SemaphoreType.DMA((3 * groups,)),
            pltpu.SemaphoreType.DMA((2 * local,)),
        ],
    )(flip, classes, initial, target)
    got = lax.all_to_all(message, "grp", 0, 0, tiled=True)
    kind = got[:, -1, 0, :local].reshape(orders).astype(jnp.int32)
    index = jnp.arange(orders, dtype=jnp.int32)
    ahead = (kind[None, :] < kind[:, None]) | (
        (kind[None, :] == kind[:, None]) & (index[None, :] < index[:, None])
    )
    rank = jnp.sum(ahead.astype(jnp.int32), axis=1)
    flat = (rows * orders, ny)
    strips = [(rows * orders, LANES)] * (ny // LANES)
    cells, goal = call(
        unpack_kernel, "unpack", 1, [rank, got], [flat] * 2, strips
    )
    shape = (rows, orders, ny)
    cells, goal = cells.reshape(shape), goal.reshape(shape)
    smem = {"core": half.reshape(1), "mob": mobility}
    tiles, own_tiles = (3 * rows + 1, SUBLANES, ny), (rows, SUBLANES, ny)
    padded = (rows + 2, orders, ny)
    edge_shape = (1, orders, ny)

    own = cells
    edge = lax.dynamic_slice_in_dim(cells, jnp.where(half == 0, rows - 1, 0), 1, axis=0)
    stored = []
    got = weights = None
    for step in range(STEPS):
        first, last = step == 0, step == STEPS - 1
        before, after, beyond = faces_of(own, edge)
        vmem = {"births": births}
        ins = {"own": own, "before": before, "after": after, "edge": beyond}
        outs = {"moved": shape, "send": edge_shape, "pot": shape, "sums": own_tiles, "w": tiles}
        outs["copies"] = (2 * devices if first else devices, LANES)
        extra = {"pad": padded, **{n: s for n, s in outs.items() if n != "send"}}
        if first:
            extra["lin"] = (KINDS, orders, ny)
        else:
            vmem["got"] = got
            ins["wprev"] = weights
            outs["cells"] = shape
            outs["stats"] = (2 + (KINDS if step == 1 else 0), orders, LANES)
            extra["stats"] = outs["stats"]
        if last:
            ins["goal"] = goal
        result = stepped(
            forward_kernel, step, smem, vmem, ins, outs, {}, {"skip": ("own",), "extra": extra}
        )
        if not first:
            cells = result["cells"]
            stored[-1]["stats"] = result["stats"]
        own, edge, weights = result["moved"], result["send"], result["w"]
        stored.append({"cells": cells, **{n: result[n] for n in ("pot", "sums", "w")}})
        got = everywhere(result["copies"])
    terms = None
    for step in range(STEPS - 1, -1, -1):
        top, bottom = step == STEPS - 1, step == 0
        before, after, beyond = faces_of(own, edge)
        ins = {"own": own, "before": before, "after": after, "edge": beyond, **stored[step]}
        outs, direct = ({} if bottom else {"adj": shape}), {}
        extra = {"pad": padded, "adj": shape}
        if top:
            ins["goal"] = goal
            outs["final"] = shape
        else:
            if bottom:
                ins["linear"] = stored[0]["stats"]
            else:
                ins["mobin"] = terms
        if bottom:
            direct["mobility"] = (SUBLANES, LANES)
            ins["final"] = final_state
            outs["packed"] = extra["packed"] = (groups, 2, local, rows, ny)
            extra["part0"] = extra["part1"] = strips[0]
        else:
            ins["wnext"] = stored[step - 1]["w"]
            outs["send"] = edge_shape
            outs["copies"] = extra["copies"] = (devices, LANES)
            if step > 1:
                outs["mobout"] = extra["mobout"] = (SUBLANES, LANES)
        if step == 1:
            ins.update({n + "0": stored[0][n] for n in ("pot", "sums", "stats")})
        result = stepped(
            backward_kernel,
            step,
            {**smem, "rank": rank} if bottom else smem,
            {"births": births, "got": got},
            ins,
            outs,
            direct,
            {"extra": extra},
        )
        own = result.get("adj")
        if top:
            final_state = result["final"]
        if bottom:
            mobility_sum = result["mobility"]
        else:
            edge, terms = result["send"], result.get("mobout")
            got = everywhere(result["copies"])

    both = result["packed"]
    both = lax.all_to_all(both, "grp", 0, 0, tiled=True)
    final_state, gradient = pl.pallas_call(
        collect_kernel,
        name="collect",
        out_shape=[pltpu.HBM(initial.shape, jnp.float32)] * 2,
        in_specs=[SMEM, VMEM],
        out_specs=[HBM, HBM],
        scratch_shapes=[pltpu.SemaphoreType.DMA((2 * groups,))],
    )(flip, both)
    scale = time_step * (planes * slabs) * nz
    mobility_sum = mobility_sum[0, : KINDS * KINDS].reshape(KINDS, KINDS)
    return final_state, gradient, mobility_sum / scale


def solution(mesh):
    return jax.shard_map(
        on_device,
        mesh=mesh,
        in_specs=(
            P("grp", "slab", None, None),
            P("grp", "slab", None, None),
            P("slab", None, None),
            P("grp"),
            P(),
        ),
        out_specs=(P("grp", "slab", None, None), P("grp", "slab", None, None), P()),
        check_vma=False,
    )
```

```python
import functools

import jax
import jax.numpy as jnp
from jax import lax
from jax.experimental import pallas as pl
from jax.experimental.pallas import tpu as pltpu
from jax.sharding import PartitionSpec as P

STEPS = 4
coupling = 0.3
stiffness = 1.0
time_step = 0.06
LANES = 128
SUBLANES = 8
KINDS = 4
CHUNKS = 4
AXES = ("slab", "grp")


def spread(column, offset):
    n = column.shape[0]
    lane = lax.broadcasted_iota(jnp.int32, (n, LANES), 1)
    row = lax.broadcasted_iota(jnp.int32, (n, LANES), 0)
    return jnp.sum(jnp.where(lane == row + offset, column, 0.0), axis=0, keepdims=True)


def gather(total, offset, n):
    lane = lax.broadcasted_iota(jnp.int32, (n, LANES), 1)
    row = lax.broadcasted_iota(jnp.int32, (n, LANES), 0)
    return jnp.sum(jnp.where(lane == row + offset, total, 0.0), axis=1, keepdims=True)


def beside(cells):
    width = cells.shape[-1]
    lane = lax.broadcasted_iota(jnp.int32, cells.shape, cells.ndim - 1)
    left = jnp.where(lane == 0, 0.0, pltpu.roll(cells, 1, cells.ndim - 1))
    right = jnp.where(lane == width - 1, 0.0, pltpu.roll(cells, width - 1, cells.ndim - 1))
    return left + right


def rolled(tile):
    return [tile] + [pltpu.roll(tile, d, 0) for d in range(1, KINDS)]


def packed(values):
    row = lax.broadcasted_iota(jnp.int32, values[0].shape, 0)
    step = 1
    while len(values) > 1:
        mask = (row // step) % 2 == 0
        values = [
            jnp.where(mask, u, v) + pltpu.roll(jnp.where(mask, v, u), step, 0)
            for u, v in zip(values[0::2], values[1::2])
        ]
        step *= 2
    (tile,) = values
    while step < SUBLANES:
        tile = tile + pltpu.roll(tile, step, 0)
        step *= 2
    return tile


def total_rows(tile):
    step = 1
    while step < SUBLANES:
        tile = tile + pltpu.roll(tile, step, 0)
        step *= 2
    return tile


def class_row(tile, c):
    return jnp.broadcast_to(tile[c : c + 1, :], tile.shape)


def tables(mob_ref, ny, transposed):
    row = lax.broadcasted_iota(jnp.int32, (SUBLANES, ny), 0) % KINDS
    tiles = []
    for d in range(KINDS):
        tile = jnp.zeros((SUBLANES, ny), jnp.float32)
        for c in range(KINDS):
            k = (c - d) % KINDS
            value = mob_ref[k, c] if transposed else mob_ref[c, k]
            tile = jnp.where(row == c, value, tile)
        tiles.append(tile)
    return tiles


def mixed(table, rolls):
    return functools.reduce(jnp.add, [t * r for t, r in zip(table, rolls)])


def active(births_ref, row, step):
    return jnp.where(births_ref[pl.ds(row, 1), :] <= step, 1.0, 0.0)


class Stream:
    def __init__(self, source, target, sems, chunks=1):
        self.source, self.target, self.sems, self.chunks = source, target, sems, chunks

    def copy(self, j):
        if self.chunks == 1:
            return pltpu.make_async_copy(self.source, self.target, self.sems.at[0])
        size = self.target.shape[0] // self.chunks
        return pltpu.make_async_copy(
            self.source.at[pl.ds(j * size, size)],
            self.target.at[pl.ds(j * size, size)],
            self.sems.at[j],
        )

    def start(self, j=0):
        self.copy(j).start()

    def start_all(self):
        for j in range(self.chunks):
            self.start(j)

    def wait(self, j=0):
        self.copy(j).wait()

    def wait_all(self):
        for j in range(self.chunks):
            self.wait(j)


def forward_kernel(step, refs):
    first, last = step == 0, step == STEPS - 1
    core_ref, mob_ref, births_ref, pad_ref = (refs[n] for n in ("core", "mob", "births", "pad"))
    before_ref, after_ref = refs["before"], refs["after"]
    w_ref, sums_ref, moved_ref, pot_ref = (refs[n] for n in ("w", "sums", "moved", "pot"))
    stream = refs["stream"]
    rows, orders, ny = moved_ref.shape
    each = orders // KINDS
    cut = [slice(c * each, (c + 1) * each) for c in range(KINDS)]
    core = core_ref[0]
    inner = pad_ref.at[pl.ds(1, rows)]
    own_ref = refs["own"]
    if not first:
        wprev_ref = refs["wprev"]
        wprev_in = stream("wprev", wprev_ref)
        wprev_in.start()
    sides = [stream("goal", refs["goal"], CHUNKS)] if last else []
    for j in range(CHUNKS):
        for s in sides:
            s.start(j)
    outs = []
    if first:
        lin_ref = refs["lin"]
        lin_ref[...] = jnp.zeros_like(lin_ref)
    else:
        stats_ref = refs["stats"]
        got = refs["got"][...]
        if step == 1:
            odd = lax.broadcasted_iota(jnp.int32, got.shape, 0) % 2 == 1
            second = jnp.sum(jnp.where(odd, got, 0.0), axis=0, keepdims=True)
            got = jnp.where(odd, 0.0, got)
        total = jnp.sum(got, axis=0, keepdims=True)
        raw = gather(total, orders, orders)
        lag = gather(total, 0, orders) / jnp.maximum(raw, 1.0)
        stats_ref[0] = jnp.broadcast_to(lag, (orders, LANES))
        stats_ref[1] = jnp.broadcast_to(raw, (orders, LANES))
        if step == 1:
            lane = lax.broadcasted_iota(jnp.int32, (1, LANES), 1)
            for k in range(KINDS):
                base = gather(second, k * orders, orders)
                level = jnp.sum(
                    jnp.where(lane == 2 * orders + k, total, 0.0), axis=1, keepdims=True
                )
                value = base - jnp.where(raw > 1.0, lag, 0.0) * level
                stats_ref[2 + k] = jnp.broadcast_to(value, (orders, LANES))
        pace = [jnp.broadcast_to(lag[cut[c]] * time_step, (each, ny)) for c in range(KINDS)]
        stats_out = stream("stats", stats_ref, out=True)
        stats_out.start()
        outs.append(stats_out)
    table = tables(mob_ref, ny, False)

    def grown(value, place, c):
        if first:
            return value
        return value + pace[c] * wprev_ref[place, pl.ds(c, 1), :]

    def rates_of(squares, place):
        sums = packed(squares)
        rolls = rolled(sums)
        summed = functools.reduce(jnp.add, rolls)
        gate = active(births_ref, place, step) / (1.0 + summed)
        w = gate * mixed(table, rolls)
        w_ref[place] = w[:KINDS]
        return sums, summed, gate, w

    if not first:
        wprev_in.wait()

    def fill(z, carry):
        for c in range(KINDS):
            pad_ref[z + 1, cut[c], :] = grown(own_ref[z, cut[c], :], z, c)
        return carry

    lax.fori_loop(0, rows, fill, 0, unroll=2)
    cells_out = stream("cells", inner, out=True)
    cells_out.start()
    outs.append(cells_out)
    edge = [grown(refs["edge"][0, cut[c], :], 3 * rows, c) for c in range(KINDS)]
    for c in range(KINDS):
        pad_ref[0, cut[c], :] = jnp.where(core == 1, edge[c], 0.0)
        pad_ref[rows + 1, cut[c], :] = jnp.where(core == 0, edge[c], 0.0)
    rates_of([e * e for e in edge], 3 * rows)

    pot_out = stream("pot", pot_ref, CHUNKS, out=True)

    def line(z, carry):
        numer, denom, extra_a, extra_b, level = carry
        before = [grown(before_ref[z, cut[c], :], rows + z, c) for c in range(KINDS)]
        rates_of([v * v for v in before], rows + z)
        after = [grown(after_ref[z, cut[c], :], 2 * rows + z, c) for c in range(KINDS)]
        rates_of([v * v for v in after], 2 * rows + z)
        cells = [pad_ref[z + 1, cut[c], :] for c in range(KINDS)]
        squares = [e * e for e in cells]
        sums, summed, gate, w = rates_of(squares, z)
        sums_ref[z] = sums
        level_now = gate * sums
        step_w = time_step * w
        base = (6.0 * stiffness - 1.0) + (2.0 * coupling) * summed
        numer, extra_a = list(numer), list(extra_a)
        for c in range(KINDS):
            e = cells[c]
            around = (
                (before[c] + after[c])
                + (pad_ref[z, cut[c], :] + pad_ref[z + 2, cut[c], :])
                + beside(e)
            )
            pot = e * (base + (1.0 - 2.0 * coupling) * squares[c]) - stiffness * around
            pot_ref[z, cut[c], :] = pot
            pushed = class_row(w, c) * pot
            numer[c] = numer[c] + pushed
            moved = e - time_step * pushed
            if last:
                moved = moved - refs["goal"][z, cut[c], :]
                extra_a[c] = extra_a[c] + class_row(step_w, c) * moved
            moved_ref[z, cut[c], :] = moved
            if first:
                for k in range(KINDS):
                    lin_ref[k, cut[c], :] += pot * class_row(level_now, k)
        denom = denom + w
        if last:
            extra_b = extra_b + step_w * step_w
        if first:
            level = level + level_now
        return tuple(numer), denom, tuple(extra_a), extra_b, level

    size = rows // CHUNKS

    def chunk(j, carry):
        for s in sides:
            s.wait(j)
        carry = lax.fori_loop(j * size, (j + 1) * size, line, carry)
        pot_out.start(j)
        return carry

    zero = jnp.zeros((each, ny), jnp.float32)
    numer, denom, extra_a, extra_b, level = lax.fori_loop(
        0,
        CHUNKS,
        chunk,
        ((zero,) * KINDS, zero, (zero,) * KINDS if last else (), zero if last else (), zero if first else ()),
    )
    for name, ref in (("w", w_ref), ("sums", sums_ref)):
        outs.append(stream(name, ref, out=True))
        outs[-1].start()

    def row_of(parts, offset):
        return spread(
            jnp.concatenate([jnp.sum(v, axis=1, keepdims=True) for v in parts], axis=0), offset
        )

    def row_of_classes(tile, offset):
        column = jnp.sum(tile, axis=1, keepdims=True)
        return spread(
            jnp.concatenate(
                [jnp.broadcast_to(column[c : c + 1], (each, 1)) for c in range(KINDS)], axis=0
            ),
            offset,
        )

    row = row_of(numer, 0) + row_of_classes(denom, orders)
    if first:
        row = row + spread(jnp.sum(level, axis=1, keepdims=True)[:KINDS], 2 * orders)
    if last:
        row = row + row_of(extra_a, 2 * orders) + row_of_classes(extra_b, 3 * orders)
    copies_ref = refs["copies"]
    shape = copies_ref.shape
    if first:
        second = functools.reduce(
            jnp.add,
            [
                spread(jnp.sum(lin_ref[k], axis=1, keepdims=True), k * orders)
                for k in range(KINDS)
            ],
        )
        odd = lax.broadcasted_iota(jnp.int32, shape, 0) % 2 == 1
        copies_ref[...] = jnp.where(odd, second, row)
    else:
        copies_ref[...] = jnp.broadcast_to(row, shape)
    outs.append(stream("copies", copies_ref, out=True))
    outs[-1].start()
    refs["send"][0] = moved_ref[jnp.where(core == 0, rows - 1, 0)]
    for s in outs:
        s.wait()
    pot_out.wait_all()


def backward_kernel(step, refs):
    top, bottom = step == STEPS - 1, step == 0
    core_ref, mob_ref, births_ref, pad_ref = (refs[n] for n in ("core", "mob", "births", "pad"))
    own_ref, before_ref, after_ref = refs["own"], refs["before"], refs["after"]
    w_ref, sums_ref, pot_ref, cells_ref = (refs[n] for n in ("w", "sums", "pot", "cells"))
    adj_ref = refs["adj"]
    stream = refs["stream"]
    rows, orders, ny = own_ref.shape
    each = orders // KINDS
    cut = [slice(c * each, (c + 1) * each) for c in range(KINDS)]
    core = core_ref[0]

    ins = [stream("w", w_ref)]
    if not top:
        ins.append(stream("stats", refs["stats"]))
    if bottom:
        ins.append(stream("linear", refs["linear"]))
        final_in = stream("final", refs["final"])
    later_ins = [stream("sums", sums_ref)]
    if not bottom:
        later_ins.append(stream("wnext", refs["wnext"], part=rows))
    if not top and not bottom:
        later_ins.append(stream("mobin", refs["mobin"]))
    if step == 1:
        later_ins += [stream("sums0", refs["sums0"]), stream("stats0", refs["stats0"])]
    sides = [("cells", cells_ref), ("pot", pot_ref)]
    if step == 1:
        sides.append(("pot0", refs["pot0"]))
    sides = [stream(name, ref, CHUNKS) for name, ref in sides]
    if top:
        ins.append(stream("goal", refs["goal"]))
    for s in ins + later_ins:
        s.start()
    for j in range(CHUNKS):
        for s in sides:
            s.start(j)
    if bottom:
        final_in.start()

    total = jnp.sum(refs["got"][...], axis=0, keepdims=True)
    if top:
        raw = gather(total, orders, orders)
        lag = gather(total, 0, orders) / jnp.maximum(raw, 1.0)
        lag_adj = gather(total, 2 * orders, orders) + lag * gather(total, 3 * orders, orders)
    for s in ins:
        s.wait()
    if not top:
        lag = refs["stats"][0][:, :1]
        raw = refs["stats"][1][:, :1]
        lag_adj = gather(total, orders, orders)
    slope_column = lag_adj / jnp.maximum(raw, 1.0)
    keep = jnp.where(raw > 1.0, lag, 0.0)

    def wide(column):
        return [jnp.broadcast_to(column[cut[c]], (each, ny)) for c in range(KINDS)]

    slope = wide(slope_column)
    lag_wide = wide(lag)
    slope_keep = wide(slope_column * keep)
    table = tables(mob_ref, ny, True)
    outs = []

    def grown(value, place, c):
        weight = w_ref[place, pl.ds(c, 1), :]
        if top:
            value = value + (time_step * lag_wide[c]) * weight
        return value, weight * (slope[c] - time_step * value)

    def fill(z, carry):
        for c in range(KINDS):
            value, pushed = grown(own_ref[z, cut[c], :], z, c)
            pad_ref[z + 1, cut[c], :] = pushed
            if top:
                adj_ref[z, cut[c], :] = value
                refs["goal"][z, cut[c], :] = value + refs["goal"][z, cut[c], :]
        return carry

    lax.fori_loop(0, rows, fill, 0, unroll=2)
    if top:
        outs.append(stream("final", refs["goal"], out=True))
        outs[-1].start()
    for c in range(KINDS):
        pushed = grown(refs["edge"][0, cut[c], :], 3 * rows, c)[1]
        pad_ref[0, cut[c], :] = jnp.where(core == 1, pushed, 0.0)
        pad_ref[rows + 1, cut[c], :] = jnp.where(core == 0, pushed, 0.0)
    for s in later_ins:
        s.wait()
    if step == 1:
        lag0 = wide(refs["stats0"][0][:, :1])
    source_ref = adj_ref if top else own_ref

    def line(z, carry):
        mob, onward = carry
        sums = sums_ref[z]
        rolls = rolled(sums)
        summed = functools.reduce(jnp.add, rolls)
        act = active(births_ref, z, step)
        adj = [source_ref[z, cut[c], :] for c in range(KINDS)]
        cells = [cells_ref[z, cut[c], :] for c in range(KINDS)]
        pots = [pot_ref[z, cut[c], :] for c in range(KINDS)]
        pushed = [pad_ref[z + 1, cut[c], :] for c in range(KINDS)]
        drive = packed(
            [
                (slope[c] * pots[c] - slope_keep[c])
                - time_step * adj[c] * (pots[c] - lag_wide[c])
                for c in range(KINDS)
            ]
        )
        plain = drive / (1.0 + summed)
        drive = act * plain
        shared = total_rows(
            (2.0 * coupling)
            * functools.reduce(jnp.add, [pushed[c] * cells[c] for c in range(KINDS)])
            - (KINDS / SUBLANES) * (jnp.concatenate([w_ref[z]] * (SUBLANES // KINDS)) * plain)
        )
        class_adj = 2.0 * (mixed(table, rolled(drive)) + shared)
        if not bottom:
            mob = tuple(m + drive * r for m, r in zip(mob, rolls))
        base = (6.0 * stiffness - 1.0) + (2.0 * coupling) * summed
        onward = list(onward)
        later = []
        for c in range(KINDS):
            around = (
                grown(before_ref[z, cut[c], :], rows + z, c)[1]
                + grown(after_ref[z, cut[c], :], 2 * rows + z, c)[1]
                + (pad_ref[z, cut[c], :] + pad_ref[z + 2, cut[c], :])
                + beside(pushed[c])
            )
            e = cells[c]
            new = (
                adj[c]
                + pushed[c] * (base + (3.0 - 6.0 * coupling) * (e * e))
                - stiffness * around
                + e * class_row(class_adj, c)
            )
            adj_ref[z, cut[c], :] = new
            if not bottom:
                onward[c] = onward[c] + refs["wnext"][z, pl.ds(c, 1), :] * new
            later.append(new)
        if step == 1:
            sums0 = rolled(refs["sums0"][z])
            gate = active(births_ref, z, 0) / (1.0 + functools.reduce(jnp.add, sums0))
            drive = (-time_step * gate) * packed(
                [later[c] * (refs["pot0"][z, cut[c], :] - lag0[c]) for c in range(KINDS)]
            )
            mob = tuple(m + drive * r for m, r in zip(mob, sums0))
        return mob, tuple(onward)

    size = rows // CHUNKS

    def chunk(j, carry):
        for s in sides:
            s.wait(j)
        carry = lax.fori_loop(j * size, (j + 1) * size, line, carry)
        return carry

    zero = jnp.zeros((each, ny), jnp.float32)
    mob, onward = lax.fori_loop(
        0, CHUNKS, chunk, (() if bottom else (zero,) * KINDS, () if bottom else (zero,) * KINDS)
    )
    if bottom:
        lane = lax.broadcasted_iota(jnp.int32, (1, LANES), 1)
        row = jnp.where(lane < KINDS * KINDS, total, 0.0)
        lane = lax.broadcasted_iota(jnp.int32, (orders, LANES), 1)
        home = lax.broadcasted_iota(jnp.int32, (orders, LANES), 0) // each
        for k in range(KINDS):
            value = slope_column * refs["linear"][2 + k][:, :1]
            row = row + jnp.sum(
                jnp.where(lane == home * KINDS + k, value, 0.0), axis=0, keepdims=True
            )
        refs["mobility"][...] = jnp.broadcast_to(row, refs["mobility"].shape)
        final_in.wait()
        pack(refs["slot"], refs["packed"], 0, refs["final"])
        pack(refs["slot"], refs["packed"], 1, adj_ref)
        outs.append(stream("packed", refs["packed"], out=True))
        outs[-1].start()
    else:
        row = time_step * spread(
            jnp.concatenate([jnp.sum(v, axis=1, keepdims=True) for v in onward], axis=0), orders
        )
        lane = lax.broadcasted_iota(jnp.int32, (KINDS, LANES), 1)
        kind = lax.broadcasted_iota(jnp.int32, (KINDS, LANES), 0)
        terms = jnp.zeros((1, LANES), jnp.float32)
        for d in range(KINDS):
            column = jnp.sum(mob[d], axis=1, keepdims=True)[:KINDS]
            spot = kind * KINDS + (kind + (KINDS - d)) % KINDS
            terms = terms + jnp.sum(jnp.where(lane == spot, column, 0.0), axis=0, keepdims=True)
        if not top:
            terms = terms + refs["mobin"][:1]
        if step == 1:
            row = row + terms
        else:
            refs["mobout"][...] = jnp.broadcast_to(terms, refs["mobout"].shape)
            outs.append(stream("mobout", refs["mobout"], out=True))
            outs[-1].start()
        refs["copies"][...] = jnp.broadcast_to(row, refs["copies"].shape)
        outs.append(stream("copies", refs["copies"], out=True))
        outs[-1].start()
        refs["send"][0] = adj_ref[jnp.where(core == 0, rows - 1, 0)]
    for s in outs:
        s.wait()


def stepped(kernel, step, smem, vmem, ins, outs, direct, scratch):
    names = list(smem) + list(vmem) + list(ins)
    pinned = [pltpu.with_memory_space_constraint(v, pltpu.HBM) for v in ins.values()]
    near = [
        pltpu.with_memory_space_constraint(v, pltpu.VMEM) if n == "own" else v
        for n, v in vmem.items()
    ]
    operands = [*smem.values(), *near, *pinned]
    out_names = list(outs) + list(direct)
    buffers = {n: (v.shape, v.dtype) for n, v in ins.items() if n not in scratch.get("skip", ())}
    buffers.update({n: (s, jnp.float32) for n, s in scratch["extra"].items()})
    streamed = [("i", n) for n in ins] + [("o", n) for n in outs]
    sems = [pltpu.SemaphoreType.DMA((CHUNKS,))] * len(streamed)

    def body(*args):
        args = list(args)
        table = dict(zip(names, args))
        args = args[len(names) :]
        hbm_out = dict(zip(out_names, args))
        args = args[len(out_names) :]
        bufs = dict(zip(buffers, args))
        sem = dict(zip(streamed, args[len(buffers) :]))
        hbm_in = {n: table.pop(n) for n in ins}
        refs = {**table, **bufs, **{n: hbm_out[n] for n in direct}}

        def stream(name, ref, chunks=1, out=False, part=None):
            if out:
                return Stream(ref, hbm_out[name], sem["o", name], chunks)
            source = hbm_in[name]
            if part:
                source, ref = source.at[pl.ds(0, part)], ref.at[pl.ds(0, part)]
            return Stream(source, ref, sem["i", name], chunks)

        refs["stream"] = stream
        kernel(step, refs)

    result = pl.pallas_call(
        body,
        name=f"{kernel.__name__}_{step}",
        out_shape=[pltpu.HBM(s, jnp.float32) for s in outs.values()]
        + [pltpu.VMEM(s, jnp.float32) for s in direct.values()],
        in_specs=[SMEM] * len(smem) + [VMEM] * len(vmem) + [HBM] * len(ins),
        out_specs=[HBM] * len(outs) + [VMEM] * len(direct),
        scratch_shapes=[pltpu.VMEM(s, d) for s, d in buffers.values()] + sems,
        compiler_params=pltpu.CompilerParams(vmem_limit_bytes=24 * 1024 * 1024),
    )(*operands)
    return dict(zip(out_names, result))


def places(groups, flip):
    ring = [(0, 0), (0, 1), (1, 1), (1, 0)]
    found = []
    for g in range(groups):
        pair, half = ring[g // 2]
        found.append((2 * (pair ^ flip) + g % 2, half))
    return found


def scatter_kernel(
    flip_ref, kinds_ref, first_ref, second_ref, out_ref, tag_ref, stage_a, stage_b, sems, sems_in
):
    groups, blocks, rows, ny = out_ref.shape
    local = first_ref.shape[0]
    loads = [
        pltpu.make_async_copy(ref.at[i], stage.at[i], sems_in.at[a * local + i])
        for a, (ref, stage) in enumerate(((first_ref, stage_a), (second_ref, stage_b)))
        for i in range(local)
    ]
    for c in loads:
        c.start()
    lane = lax.broadcasted_iota(jnp.int32, (rows, ny), 1)
    tag = jnp.zeros((rows, ny), jnp.float32)
    for i in range(local):
        tag = jnp.where(lane == i, kinds_ref[i].astype(jnp.float32), tag)
    tag_ref[...] = tag
    copies = []
    for g, (plane, half) in enumerate(places(groups, 0)):
        plane = plane ^ (2 * flip_ref[0])
        for a, ref in enumerate((stage_a, stage_b)):
            copies.append(
                pltpu.make_async_copy(
                    ref.at[:, plane, pl.ds(half * rows, rows), :],
                    out_ref.at[g, pl.ds(a * local, local)],
                    sems.at[3 * g + a],
                )
            )
        copies.append(
            pltpu.make_async_copy(tag_ref, out_ref.at[g, blocks - 1], sems.at[3 * g + 2])
        )
    for c in loads:
        c.wait()
    for c in copies:
        c.start()
    for c in copies:
        c.wait()


def collect_kernel(flip_ref, got_ref, first_ref, second_ref, sems):
    groups, _, local, rows, ny = got_ref.shape
    copies = []
    for g, (plane, half) in enumerate(places(groups, 0)):
        plane = plane ^ (2 * flip_ref[0])
        for a, ref in enumerate((first_ref, second_ref)):
            copies.append(
                pltpu.make_async_copy(
                    got_ref.at[g, a],
                    ref.at[:, plane, pl.ds(half * rows, rows), :],
                    sems.at[2 * g + a],
                )
            )
    for c in copies:
        c.start()
    for c in copies:
        c.wait()


def unpack_kernel(array, send, slot_ref, half_ref, got_ref, out_ref, *rest):
    sources, blocks, rows, ny = got_ref.shape
    local = blocks // 2
    for first in range(0, sources * local, SUBLANES):
        slots = [slot_ref[first + i] for i in range(SUBLANES)]
        tile = jnp.stack(
            [got_ref[p // local, array * local + lax.rem(p, local)] for p in slots], axis=0
        )
        out_ref[:, first : first + SUBLANES, :] = jnp.swapaxes(tile, 0, 1)
    if send:
        rest[0][0] = out_ref[jnp.where(half_ref[0] == 0, rows - 1, 0)]


def pack(slot_ref, out_ref, array, fields):
    groups, _, local, rows, ny = out_ref.shape
    for first in range(0, groups * local, SUBLANES):
        tile = jnp.swapaxes(fields[:, first : first + SUBLANES, :], 0, 1)
        for i in range(SUBLANES):
            p = slot_ref[first + i]
            out_ref[p // local, array, lax.rem(p, local)] = tile[i]


VMEM = pl.BlockSpec(memory_space=pltpu.VMEM)
SMEM = pl.BlockSpec(memory_space=pltpu.SMEM)
HBM = pl.BlockSpec(memory_space=pltpu.HBM)


def on_device(initial, target, birth_step, classes, mobility):
    slabs, groups = lax.axis_size("slab"), lax.axis_size("grp")
    devices = slabs * groups
    slab, me = lax.axis_index("slab"), lax.axis_index("grp")
    local, planes, nz, ny = initial.shape
    rows = nz * planes // groups
    orders = local * groups
    flip = slab % 2
    chip, core = me // 2, me % 2
    half = ((chip == 1) | (chip == 2)).astype(jnp.int32)
    plane = 2 * ((chip // 2) ^ flip) + core

    across = []
    for i in range(slabs * planes // 2 - 1):
        i = 2 * i + 1
        for z in range(2):
            ends = []
            for x in (i, i + 1):
                where = places(groups, x // planes % 2).index((x % planes, z))
                ends.append(x // planes * groups + where)
            across += [tuple(ends), tuple(ends[::-1])]

    def faces_of(cells, edge):
        return (
            lax.ppermute(cells, AXES, across),
            lax.ppermute(cells, "grp", [(g, g ^ 1) for g in range(groups)]),
            lax.ppermute(edge, "grp", [(g, g ^ 2) for g in range(groups)]),
        )

    def everywhere(copies):
        return lax.all_to_all(copies, AXES, 0, 0, tiled=True)

    chain = [(i, i + 1) for i in range(slabs - 1)]
    births = jnp.concatenate(
        [
            lax.ppermute(birth_step[-1:], "slab", chain),
            birth_step,
            lax.ppermute(birth_step[:1], "slab", [(j, i) for i, j in chain]),
        ]
    )
    near = lax.dynamic_slice_in_dim(births, plane, 3, axis=0)
    mine = lax.dynamic_slice_in_dim(near, half * rows, rows, axis=1)
    other = lax.dynamic_slice_in_dim(near[1], jnp.where(half == 0, rows, rows - 1), 1, axis=0)
    first, second = jnp.where(core == 0, mine[0], mine[2]), jnp.where(core == 0, mine[2], mine[0])
    births = jnp.concatenate(
        [mine[1], first, second, jnp.broadcast_to(other, (SUBLANES, ny))], axis=0
    )

    flip = flip.astype(jnp.int32).reshape(1)
    block = (groups, 2 * local + 1, rows, ny)
    message = pl.pallas_call(
        scatter_kernel,
        name="scatter",
        out_shape=pltpu.HBM(block, jnp.float32),
        in_specs=[SMEM, SMEM, HBM, HBM],
        out_specs=HBM,
        scratch_shapes=[
            pltpu.VMEM((rows, ny), jnp.float32),
            pltpu.VMEM(initial.shape, jnp.float32),
            pltpu.VMEM(initial.shape, jnp.float32),
            pltpu.SemaphoreType.DMA((3 * groups,)),
            pltpu.SemaphoreType.DMA((2 * local,)),
        ],
    )(flip, classes, initial, target)
    got = lax.all_to_all(message, "grp", 0, 0, tiled=True)
    kind = got[:, -1, 0, :local].reshape(orders).astype(jnp.int32)
    index = jnp.arange(orders, dtype=jnp.int32)
    ahead = (kind[None, :] < kind[:, None]) | (
        (kind[None, :] == kind[:, None]) & (index[None, :] < index[:, None])
    )
    rank = jnp.sum(ahead.astype(jnp.int32), axis=1)
    slot = jnp.sum(jnp.where(rank[None, :] == index[:, None], index[None, :], 0), axis=1)
    shape, edge_shape = (rows, orders, ny), (1, orders, ny)

    def unpacked(array, outs):
        return pl.pallas_call(
            functools.partial(unpack_kernel, array, len(outs) > 1),
            name=f"unpack{array}",
            out_shape=outs,
            in_specs=[SMEM, SMEM, VMEM],
            out_specs=[VMEM] * len(outs),
            compiler_params=pltpu.CompilerParams(vmem_limit_bytes=16 * 1024 * 1024),
        )(slot, half.reshape(1), got)

    own, edge = unpacked(0, [pltpu.VMEM(s, jnp.float32) for s in (shape, edge_shape)])
    (goal,) = unpacked(1, [pltpu.HBM(shape, jnp.float32)])
    smem = {"core": half.reshape(1), "mob": mobility}
    tiles, own_tiles = (3 * rows + 1, KINDS, ny), (rows, SUBLANES, ny)
    padded = (rows + 2, orders, ny)
    stored = []
    got = weights = None
    for step in range(STEPS):
        first, last = step == 0, step == STEPS - 1
        before, after, beyond = faces_of(own, edge)
        vmem = {"births": births, "before": before, "after": after, "edge": beyond, "own": own}
        ins = {}
        direct = {"moved": shape, "send": edge_shape}
        outs = {"pot": shape, "sums": own_tiles, "w": tiles, "cells": shape}
        outs["copies"] = (2 * devices if first else devices, LANES)
        extra = {"pad": padded, **{n: s for n, s in outs.items() if n != "cells"}}
        if first:
            extra["lin"] = (KINDS, orders, ny)
        else:
            vmem["got"] = got
            ins["wprev"] = weights
            outs["stats"] = (2 + (KINDS if step == 1 else 0), orders, LANES)
            extra["stats"] = outs["stats"]
        if last:
            ins["goal"] = goal
        result = stepped(
            forward_kernel, step, smem, vmem, ins, outs, direct, {"extra": extra}
        )
        if not first:
            stored[-1]["stats"] = result["stats"]
        own, edge, weights = result["moved"], result["send"], result["w"]
        stored.append({n: result[n] for n in ("cells", "pot", "sums", "w")})
        got = everywhere(result["copies"])
    terms = None
    for step in range(STEPS - 1, -1, -1):
        top, bottom = step == STEPS - 1, step == 0
        before, after, beyond = faces_of(own, edge)
        vmem = {"births": births, "got": got, "before": before, "after": after, "edge": beyond}
        vmem["own"] = own
        ins = dict(stored[step])
        outs, direct = {}, {}
        extra = {"pad": padded}
        if top:
            ins["goal"] = goal
            outs["final"] = shape
        else:
            if bottom:
                ins["linear"] = stored[0]["stats"]
            else:
                ins["mobin"] = terms
        if bottom:
            extra["adj"] = shape
            direct["mobility"] = (SUBLANES, LANES)
            ins["final"] = final_state
            outs["packed"] = extra["packed"] = (groups, 2, local, rows, ny)
        else:
            ins["wnext"] = stored[step - 1]["w"]
            direct["adj"], direct["send"] = shape, edge_shape
            outs["copies"] = extra["copies"] = (devices, LANES)
            if step > 1:
                outs["mobout"] = extra["mobout"] = (SUBLANES, LANES)
        if step == 1:
            ins.update({n + "0": stored[0][n] for n in ("pot", "sums", "stats")})
        result = stepped(
            backward_kernel,
            step,
            {**smem, "slot": slot} if bottom else smem,
            vmem,
            ins,
            outs,
            direct,
            {"extra": extra},
        )
        own = result.get("adj")
        if top:
            final_state = result["final"]
        if bottom:
            mobility_sum = result["mobility"]
        else:
            edge, terms = result["send"], result.get("mobout")
            got = everywhere(result["copies"])

    both = result["packed"]
    both = lax.all_to_all(both, "grp", 0, 0, tiled=True)
    final_state, gradient = pl.pallas_call(
        collect_kernel,
        name="collect",
        out_shape=[pltpu.HBM(initial.shape, jnp.float32)] * 2,
        in_specs=[SMEM, VMEM],
        out_specs=[HBM, HBM],
        scratch_shapes=[pltpu.SemaphoreType.DMA((2 * groups,))],
    )(flip, pltpu.with_memory_space_constraint(both, pltpu.VMEM))
    scale = time_step * (planes * slabs) * nz
    mobility_sum = mobility_sum[0, : KINDS * KINDS].reshape(KINDS, KINDS)
    return final_state, gradient, mobility_sum / scale


def solution(mesh):
    return jax.shard_map(
        on_device,
        mesh=mesh,
        in_specs=(
            P("grp", "slab", None, None),
            P("grp", "slab", None, None),
            P("slab", None, None),
            P("grp"),
            P(),
        ),
        out_specs=(P("grp", "slab", None, None), P("grp", "slab", None, None), P()),
        check_vma=False,
    )
```

```python
import functools

import jax
import jax.numpy as jnp
from jax import lax
from jax.experimental import pallas as pl
from jax.experimental.pallas import tpu as pltpu
from jax.sharding import PartitionSpec as P

STEPS = 4
coupling = 0.3
stiffness = 1.0
time_step = 0.06
LANES = 128
SUBLANES = 8
KINDS = 4
CHUNKS = 4
AXES = ("slab", "grp")


def spread(column, offset):
    n = column.shape[0]
    lane = lax.broadcasted_iota(jnp.int32, (n, LANES), 1)
    row = lax.broadcasted_iota(jnp.int32, (n, LANES), 0)
    return jnp.sum(jnp.where(lane == row + offset, column, 0.0), axis=0, keepdims=True)


def gather(total, offset, n):
    lane = lax.broadcasted_iota(jnp.int32, (n, LANES), 1)
    row = lax.broadcasted_iota(jnp.int32, (n, LANES), 0)
    return jnp.sum(jnp.where(lane == row + offset, total, 0.0), axis=1, keepdims=True)


def beside(cells):
    width = cells.shape[-1]
    lane = lax.broadcasted_iota(jnp.int32, cells.shape, cells.ndim - 1)
    left = jnp.where(lane == 0, 0.0, pltpu.roll(cells, 1, cells.ndim - 1))
    right = jnp.where(lane == width - 1, 0.0, pltpu.roll(cells, width - 1, cells.ndim - 1))
    return left + right


def rolled(tile):
    return [tile] + [pltpu.roll(tile, d, 0) for d in range(1, KINDS)]


def packed(values):
    row = lax.broadcasted_iota(jnp.int32, values[0].shape, 0)
    step = 1
    while len(values) > 1:
        mask = (row // step) % 2 == 0
        values = [
            jnp.where(mask, u, v) + pltpu.roll(jnp.where(mask, v, u), step, 0)
            for u, v in zip(values[0::2], values[1::2])
        ]
        step *= 2
    (tile,) = values
    while step < SUBLANES:
        tile = tile + pltpu.roll(tile, step, 0)
        step *= 2
    return tile


def total_rows(tile):
    step = 1
    while step < SUBLANES:
        tile = tile + pltpu.roll(tile, step, 0)
        step *= 2
    return tile


def class_row(tile, c):
    return jnp.broadcast_to(tile[c : c + 1, :], tile.shape)


def tables(mob_ref, ny, transposed):
    row = lax.broadcasted_iota(jnp.int32, (SUBLANES, ny), 0) % KINDS
    tiles = []
    for d in range(KINDS):
        tile = jnp.zeros((SUBLANES, ny), jnp.float32)
        for c in range(KINDS):
            k = (c - d) % KINDS
            value = mob_ref[k, c] if transposed else mob_ref[c, k]
            tile = jnp.where(row == c, value, tile)
        tiles.append(tile)
    return tiles


def mixed(table, rolls):
    return functools.reduce(jnp.add, [t * r for t, r in zip(table, rolls)])


def active(births_ref, row, step):
    return jnp.where(births_ref[pl.ds(row, 1), :] <= step, 1.0, 0.0)


class Stream:
    def __init__(self, source, target, sems, chunks=1):
        self.source, self.target, self.sems, self.chunks = source, target, sems, chunks

    def copy(self, j):
        if self.chunks == 1:
            return pltpu.make_async_copy(self.source, self.target, self.sems.at[0])
        size = self.target.shape[0] // self.chunks
        return pltpu.make_async_copy(
            self.source.at[pl.ds(j * size, size)],
            self.target.at[pl.ds(j * size, size)],
            self.sems.at[j],
        )

    def start(self, j=0):
        self.copy(j).start()

    def start_all(self):
        for j in range(self.chunks):
            self.start(j)

    def wait(self, j=0):
        self.copy(j).wait()

    def wait_all(self):
        for j in range(self.chunks):
            self.wait(j)


def forward_kernel(step, refs):
    first, last = step == 0, step == STEPS - 1
    core_ref, mob_ref, births_ref, pad_ref = (refs[n] for n in ("core", "mob", "births", "pad"))
    before_ref, after_ref = refs["before"], refs["after"]
    w_ref, sums_ref, moved_ref, pot_ref = (refs[n] for n in ("w", "sums", "moved", "pot"))
    stream = refs["stream"]
    rows, orders, ny = moved_ref.shape
    each = orders // KINDS
    cut = [slice(c * each, (c + 1) * each) for c in range(KINDS)]
    core = core_ref[0]
    inner = pad_ref.at[pl.ds(1, rows)]
    own_ref = refs["own"]
    if not first:
        wprev_ref = refs["wprev"]
        wprev_in = stream("wprev", wprev_ref)
        wprev_in.start()
    sides = [stream("goal", refs["goal"], CHUNKS)] if last else []
    for j in range(CHUNKS):
        for s in sides:
            s.start(j)
    outs = []
    if first:
        lin_ref = refs["lin"]
        lin_ref[...] = jnp.zeros_like(lin_ref)
    else:
        stats_ref = refs["stats"]
        got = refs["got"][...]
        if step == 1:
            odd = lax.broadcasted_iota(jnp.int32, got.shape, 0) % 2 == 1
            second = jnp.sum(jnp.where(odd, got, 0.0), axis=0, keepdims=True)
            got = jnp.where(odd, 0.0, got)
        total = jnp.sum(got, axis=0, keepdims=True)
        raw = gather(total, orders, orders)
        lag = gather(total, 0, orders) / jnp.maximum(raw, 1.0)
        stats_ref[0] = jnp.broadcast_to(lag, (orders, LANES))
        stats_ref[1] = jnp.broadcast_to(raw, (orders, LANES))
        if step == 1:
            lane = lax.broadcasted_iota(jnp.int32, (1, LANES), 1)
            for k in range(KINDS):
                base = gather(second, k * orders, orders)
                level = jnp.sum(
                    jnp.where(lane == 2 * orders + k, total, 0.0), axis=1, keepdims=True
                )
                value = base - jnp.where(raw > 1.0, lag, 0.0) * level
                stats_ref[2 + k] = jnp.broadcast_to(value, (orders, LANES))
        pace = [jnp.broadcast_to(lag[cut[c]] * time_step, (each, ny)) for c in range(KINDS)]
        stats_out = stream("stats", stats_ref, out=True)
        stats_out.start()
        outs.append(stats_out)
    table = tables(mob_ref, ny, False)

    def grown(value, place, c):
        if first:
            return value
        return value + pace[c] * wprev_ref[place, pl.ds(c, 1), :]

    def rates_of(squares, place):
        sums = packed(squares)
        rolls = rolled(sums)
        summed = functools.reduce(jnp.add, rolls)
        gate = active(births_ref, place, step) / (1.0 + summed)
        w = gate * mixed(table, rolls)
        w_ref[place] = w[:KINDS]
        return sums, summed, gate, w

    if not first:
        wprev_in.wait()

    def fill(z, carry):
        for c in range(KINDS):
            pad_ref[z + 1, cut[c], :] = grown(own_ref[z, cut[c], :], z, c)
        return carry

    lax.fori_loop(0, rows, fill, 0, unroll=2)
    cells_out = stream("cells", inner, out=True)
    cells_out.start()
    outs.append(cells_out)
    edge = [grown(refs["edge"][0, cut[c], :], 3 * rows, c) for c in range(KINDS)]
    for c in range(KINDS):
        pad_ref[0, cut[c], :] = jnp.where(core == 1, edge[c], 0.0)
        pad_ref[rows + 1, cut[c], :] = jnp.where(core == 0, edge[c], 0.0)
    rates_of([e * e for e in edge], 3 * rows)

    pot_out = stream("pot", pot_ref, CHUNKS, out=True)

    def line(z, carry):
        numer, denom, extra_a, extra_b, level = carry
        before = [grown(before_ref[z, cut[c], :], rows + z, c) for c in range(KINDS)]
        rates_of([v * v for v in before], rows + z)
        after = [grown(after_ref[z, cut[c], :], 2 * rows + z, c) for c in range(KINDS)]
        rates_of([v * v for v in after], 2 * rows + z)
        cells = [pad_ref[z + 1, cut[c], :] for c in range(KINDS)]
        squares = [e * e for e in cells]
        sums, summed, gate, w = rates_of(squares, z)
        sums_ref[z] = sums
        level_now = gate * sums
        step_w = time_step * w
        base = (6.0 * stiffness - 1.0) + (2.0 * coupling) * summed
        numer, extra_a = list(numer), list(extra_a)
        for c in range(KINDS):
            e = cells[c]
            around = (
                (before[c] + after[c])
                + (pad_ref[z, cut[c], :] + pad_ref[z + 2, cut[c], :])
                + beside(e)
            )
            pot = e * (base + (1.0 - 2.0 * coupling) * squares[c]) - stiffness * around
            pot_ref[z, cut[c], :] = pot
            pushed = class_row(w, c) * pot
            numer[c] = numer[c] + pushed
            moved = e - time_step * pushed
            if last:
                moved = moved - refs["goal"][z, cut[c], :]
                extra_a[c] = extra_a[c] + class_row(step_w, c) * moved
            moved_ref[z, cut[c], :] = moved
            if first:
                for k in range(KINDS):
                    lin_ref[k, cut[c], :] += pot * class_row(level_now, k)
        denom = denom + w
        if last:
            extra_b = extra_b + step_w * step_w
        if first:
            level = level + level_now
        return tuple(numer), denom, tuple(extra_a), extra_b, level

    size = rows // CHUNKS

    def chunk(j, carry):
        for s in sides:
            s.wait(j)
        carry = lax.fori_loop(0, size, lambda i, c: line(j * size + i, c), carry, unroll=4)
        pot_out.start(j)
        return carry

    zero = jnp.zeros((each, ny), jnp.float32)
    numer, denom, extra_a, extra_b, level = lax.fori_loop(
        0,
        CHUNKS,
        chunk,
        ((zero,) * KINDS, zero, (zero,) * KINDS if last else (), zero if last else (), zero if first else ()),
    )
    for name, ref in (("w", w_ref), ("sums", sums_ref)):
        outs.append(stream(name, ref, out=True))
        outs[-1].start()

    def row_of(parts, offset):
        return spread(
            jnp.concatenate([jnp.sum(v, axis=1, keepdims=True) for v in parts], axis=0), offset
        )

    def row_of_classes(tile, offset):
        column = jnp.sum(tile, axis=1, keepdims=True)
        return spread(
            jnp.concatenate(
                [jnp.broadcast_to(column[c : c + 1], (each, 1)) for c in range(KINDS)], axis=0
            ),
            offset,
        )

    row = row_of(numer, 0) + row_of_classes(denom, orders)
    if first:
        row = row + spread(jnp.sum(level, axis=1, keepdims=True)[:KINDS], 2 * orders)
    if last:
        row = row + row_of(extra_a, 2 * orders) + row_of_classes(extra_b, 3 * orders)
    copies_ref = refs["copies"]
    shape = copies_ref.shape
    if first:
        second = functools.reduce(
            jnp.add,
            [
                spread(jnp.sum(lin_ref[k], axis=1, keepdims=True), k * orders)
                for k in range(KINDS)
            ],
        )
        odd = lax.broadcasted_iota(jnp.int32, shape, 0) % 2 == 1
        copies_ref[...] = jnp.where(odd, second, row)
    else:
        copies_ref[...] = jnp.broadcast_to(row, shape)
    outs.append(stream("copies", copies_ref, out=True))
    outs[-1].start()
    refs["send"][0] = moved_ref[jnp.where(core == 0, rows - 1, 0)]
    for s in outs:
        s.wait()
    pot_out.wait_all()


def backward_kernel(step, refs):
    top, bottom = step == STEPS - 1, step == 0
    core_ref, mob_ref, births_ref, pad_ref = (refs[n] for n in ("core", "mob", "births", "pad"))
    own_ref, before_ref, after_ref = refs["own"], refs["before"], refs["after"]
    w_ref, sums_ref, pot_ref, cells_ref = (refs[n] for n in ("w", "sums", "pot", "cells"))
    adj_ref = refs["adj"]
    stream = refs["stream"]
    rows, orders, ny = own_ref.shape
    each = orders // KINDS
    cut = [slice(c * each, (c + 1) * each) for c in range(KINDS)]
    core = core_ref[0]

    ins = [stream("w", w_ref)]
    if not top:
        ins.append(stream("stats", refs["stats"]))
    if bottom:
        ins.append(stream("linear", refs["linear"]))
        final_in = stream("final", refs["final"])
    later_ins = [stream("sums", sums_ref)]
    if not bottom:
        later_ins.append(stream("wnext", refs["wnext"], part=rows))
    if not top and not bottom:
        later_ins.append(stream("mobin", refs["mobin"]))
    if step == 1:
        later_ins += [stream("sums0", refs["sums0"]), stream("stats0", refs["stats0"])]
    sides = [("cells", cells_ref), ("pot", pot_ref)]
    if step == 1:
        sides.append(("pot0", refs["pot0"]))
    sides = [stream(name, ref, CHUNKS) for name, ref in sides]
    if top:
        ins.append(stream("goal", refs["goal"]))
    for s in ins + later_ins:
        s.start()
    for j in range(CHUNKS):
        for s in sides:
            s.start(j)
    if bottom:
        final_in.start()

    total = jnp.sum(refs["got"][...], axis=0, keepdims=True)
    if top:
        raw = gather(total, orders, orders)
        lag = gather(total, 0, orders) / jnp.maximum(raw, 1.0)
        lag_adj = gather(total, 2 * orders, orders) + lag * gather(total, 3 * orders, orders)
    for s in ins:
        s.wait()
    if not top:
        lag = refs["stats"][0][:, :1]
        raw = refs["stats"][1][:, :1]
        lag_adj = gather(total, orders, orders)
    slope_column = lag_adj / jnp.maximum(raw, 1.0)
    keep = jnp.where(raw > 1.0, lag, 0.0)

    def wide(column):
        return [jnp.broadcast_to(column[cut[c]], (each, ny)) for c in range(KINDS)]

    slope = wide(slope_column)
    lag_wide = wide(lag)
    slope_keep = wide(slope_column * keep)
    table = tables(mob_ref, ny, True)
    outs = []

    def grown(value, place, c):
        weight = w_ref[place, pl.ds(c, 1), :]
        if top:
            value = value + (time_step * lag_wide[c]) * weight
        return value, weight * (slope[c] - time_step * value)

    def fill(z, carry):
        for c in range(KINDS):
            value, pushed = grown(own_ref[z, cut[c], :], z, c)
            pad_ref[z + 1, cut[c], :] = pushed
            if top:
                adj_ref[z, cut[c], :] = value
                refs["goal"][z, cut[c], :] = value + refs["goal"][z, cut[c], :]
        return carry

    lax.fori_loop(0, rows, fill, 0, unroll=2)
    if top:
        outs.append(stream("final", refs["goal"], out=True))
        outs[-1].start()
    for c in range(KINDS):
        pushed = grown(refs["edge"][0, cut[c], :], 3 * rows, c)[1]
        pad_ref[0, cut[c], :] = jnp.where(core == 1, pushed, 0.0)
        pad_ref[rows + 1, cut[c], :] = jnp.where(core == 0, pushed, 0.0)
    for s in later_ins:
        s.wait()
    if step == 1:
        lag0 = wide(refs["stats0"][0][:, :1])
    source_ref = adj_ref if top else own_ref

    def line(z, carry):
        mob, onward = carry
        sums = sums_ref[z]
        rolls = rolled(sums)
        summed = functools.reduce(jnp.add, rolls)
        act = active(births_ref, z, step)
        adj = [source_ref[z, cut[c], :] for c in range(KINDS)]
        cells = [cells_ref[z, cut[c], :] for c in range(KINDS)]
        pots = [pot_ref[z, cut[c], :] for c in range(KINDS)]
        pushed = [pad_ref[z + 1, cut[c], :] for c in range(KINDS)]
        drive = packed(
            [
                (slope[c] * pots[c] - slope_keep[c])
                - time_step * adj[c] * (pots[c] - lag_wide[c])
                for c in range(KINDS)
            ]
        )
        plain = drive / (1.0 + summed)
        drive = act * plain
        shared = total_rows(
            (2.0 * coupling)
            * functools.reduce(jnp.add, [pushed[c] * cells[c] for c in range(KINDS)])
            - (KINDS / SUBLANES) * (jnp.concatenate([w_ref[z]] * (SUBLANES // KINDS)) * plain)
        )
        class_adj = 2.0 * (mixed(table, rolled(drive)) + shared)
        if not bottom:
            mob = tuple(m + drive * r for m, r in zip(mob, rolls))
        base = (6.0 * stiffness - 1.0) + (2.0 * coupling) * summed
        onward = list(onward)
        later = []
        for c in range(KINDS):
            around = (
                grown(before_ref[z, cut[c], :], rows + z, c)[1]
                + grown(after_ref[z, cut[c], :], 2 * rows + z, c)[1]
                + (pad_ref[z, cut[c], :] + pad_ref[z + 2, cut[c], :])
                + beside(pushed[c])
            )
            e = cells[c]
            new = (
                adj[c]
                + pushed[c] * (base + (3.0 - 6.0 * coupling) * (e * e))
                - stiffness * around
                + e * class_row(class_adj, c)
            )
            adj_ref[z, cut[c], :] = new
            if not bottom:
                onward[c] = onward[c] + refs["wnext"][z, pl.ds(c, 1), :] * new
            later.append(new)
        if step == 1:
            sums0 = rolled(refs["sums0"][z])
            gate = active(births_ref, z, 0) / (1.0 + functools.reduce(jnp.add, sums0))
            drive = (-time_step * gate) * packed(
                [later[c] * (refs["pot0"][z, cut[c], :] - lag0[c]) for c in range(KINDS)]
            )
            mob = tuple(m + drive * r for m, r in zip(mob, sums0))
        return mob, tuple(onward)

    size = rows // CHUNKS

    def chunk(j, carry):
        for s in sides:
            s.wait(j)
        carry = lax.fori_loop(0, size, lambda i, c: line(j * size + i, c), carry, unroll=4)
        return carry

    zero = jnp.zeros((each, ny), jnp.float32)
    mob, onward = lax.fori_loop(
        0, CHUNKS, chunk, (() if bottom else (zero,) * KINDS, () if bottom else (zero,) * KINDS)
    )
    if bottom:
        lane = lax.broadcasted_iota(jnp.int32, (1, LANES), 1)
        row = jnp.where(lane < KINDS * KINDS, total, 0.0)
        lane = lax.broadcasted_iota(jnp.int32, (orders, LANES), 1)
        home = lax.broadcasted_iota(jnp.int32, (orders, LANES), 0) // each
        for k in range(KINDS):
            value = slope_column * refs["linear"][2 + k][:, :1]
            row = row + jnp.sum(
                jnp.where(lane == home * KINDS + k, value, 0.0), axis=0, keepdims=True
            )
        refs["mobility"][...] = jnp.broadcast_to(row, refs["mobility"].shape)
        final_in.wait()
        pack(refs["slot"], refs["packed"], 0, refs["final"])
        pack(refs["slot"], refs["packed"], 1, adj_ref)
        outs.append(stream("packed", refs["packed"], out=True))
        outs[-1].start()
    else:
        row = time_step * spread(
            jnp.concatenate([jnp.sum(v, axis=1, keepdims=True) for v in onward], axis=0), orders
        )
        lane = lax.broadcasted_iota(jnp.int32, (KINDS, LANES), 1)
        kind = lax.broadcasted_iota(jnp.int32, (KINDS, LANES), 0)
        terms = jnp.zeros((1, LANES), jnp.float32)
        for d in range(KINDS):
            column = jnp.sum(mob[d], axis=1, keepdims=True)[:KINDS]
            spot = kind * KINDS + (kind + (KINDS - d)) % KINDS
            terms = terms + jnp.sum(jnp.where(lane == spot, column, 0.0), axis=0, keepdims=True)
        if not top:
            terms = terms + refs["mobin"][:1]
        if step == 1:
            row = row + terms
        else:
            refs["mobout"][...] = jnp.broadcast_to(terms, refs["mobout"].shape)
            outs.append(stream("mobout", refs["mobout"], out=True))
            outs[-1].start()
        refs["copies"][...] = jnp.broadcast_to(row, refs["copies"].shape)
        outs.append(stream("copies", refs["copies"], out=True))
        outs[-1].start()
        refs["send"][0] = adj_ref[jnp.where(core == 0, rows - 1, 0)]
    for s in outs:
        s.wait()


def stepped(kernel, step, smem, vmem, ins, outs, direct, scratch):
    names = list(smem) + list(vmem) + list(ins)
    pinned = [pltpu.with_memory_space_constraint(v, pltpu.HBM) for v in ins.values()]
    near = [
        pltpu.with_memory_space_constraint(v, pltpu.VMEM) if n == "own" else v
        for n, v in vmem.items()
    ]
    operands = [*smem.values(), *near, *pinned]
    out_names = list(outs) + list(direct)
    buffers = {n: (v.shape, v.dtype) for n, v in ins.items() if n not in scratch.get("skip", ())}
    buffers.update({n: (s, jnp.float32) for n, s in scratch["extra"].items()})
    streamed = [("i", n) for n in ins] + [("o", n) for n in outs]
    sems = [pltpu.SemaphoreType.DMA((CHUNKS,))] * len(streamed)

    def body(*args):
        args = list(args)
        table = dict(zip(names, args))
        args = args[len(names) :]
        hbm_out = dict(zip(out_names, args))
        args = args[len(out_names) :]
        bufs = dict(zip(buffers, args))
        sem = dict(zip(streamed, args[len(buffers) :]))
        hbm_in = {n: table.pop(n) for n in ins}
        refs = {**table, **bufs, **{n: hbm_out[n] for n in direct}}

        def stream(name, ref, chunks=1, out=False, part=None):
            if out:
                return Stream(ref, hbm_out[name], sem["o", name], chunks)
            source = hbm_in[name]
            if part:
                source, ref = source.at[pl.ds(0, part)], ref.at[pl.ds(0, part)]
            return Stream(source, ref, sem["i", name], chunks)

        refs["stream"] = stream
        kernel(step, refs)

    result = pl.pallas_call(
        body,
        name=f"{kernel.__name__}_{step}",
        out_shape=[pltpu.HBM(s, jnp.float32) for s in outs.values()]
        + [pltpu.VMEM(s, jnp.float32) for s in direct.values()],
        in_specs=[SMEM] * len(smem) + [VMEM] * len(vmem) + [HBM] * len(ins),
        out_specs=[HBM] * len(outs) + [VMEM] * len(direct),
        scratch_shapes=[pltpu.VMEM(s, d) for s, d in buffers.values()] + sems,
        compiler_params=pltpu.CompilerParams(vmem_limit_bytes=24 * 1024 * 1024),
    )(*operands)
    return dict(zip(out_names, result))


def places(groups, flip):
    ring = [(0, 0), (0, 1), (1, 1), (1, 0)]
    found = []
    for g in range(groups):
        pair, half = ring[g // 2]
        found.append((2 * (pair ^ flip) + g % 2, half))
    return found


def scatter_kernel(
    flip_ref, kinds_ref, first_ref, second_ref, out_ref, tag_ref, stage_a, stage_b, sems, sems_in
):
    groups, blocks, rows, ny = out_ref.shape
    local = first_ref.shape[0]
    loads = [
        pltpu.make_async_copy(ref.at[i], stage.at[i], sems_in.at[a * local + i])
        for a, (ref, stage) in enumerate(((first_ref, stage_a), (second_ref, stage_b)))
        for i in range(local)
    ]
    for c in loads:
        c.start()
    lane = lax.broadcasted_iota(jnp.int32, (rows, ny), 1)
    tag = jnp.zeros((rows, ny), jnp.float32)
    for i in range(local):
        tag = jnp.where(lane == i, kinds_ref[i].astype(jnp.float32), tag)
    tag_ref[...] = tag
    copies = []
    for g, (plane, half) in enumerate(places(groups, 0)):
        plane = plane ^ (2 * flip_ref[0])
        for a, ref in enumerate((stage_a, stage_b)):
            copies.append(
                pltpu.make_async_copy(
                    ref.at[:, plane, pl.ds(half * rows, rows), :],
                    out_ref.at[g, pl.ds(a * local, local)],
                    sems.at[3 * g + a],
                )
            )
        copies.append(
            pltpu.make_async_copy(tag_ref, out_ref.at[g, blocks - 1], sems.at[3 * g + 2])
        )
    for c in loads:
        c.wait()
    for c in copies:
        c.start()
    for c in copies:
        c.wait()


def collect_kernel(flip_ref, got_ref, first_ref, second_ref, sems):
    groups, _, local, rows, ny = got_ref.shape
    copies = []
    for g, (plane, half) in enumerate(places(groups, 0)):
        plane = plane ^ (2 * flip_ref[0])
        for a, ref in enumerate((first_ref, second_ref)):
            copies.append(
                pltpu.make_async_copy(
                    got_ref.at[g, a],
                    ref.at[:, plane, pl.ds(half * rows, rows), :],
                    sems.at[2 * g + a],
                )
            )
    for c in copies:
        c.start()
    for c in copies:
        c.wait()


def unpack_kernel(array, send, slot_ref, half_ref, got_ref, out_ref, *rest):
    sources, blocks, rows, ny = got_ref.shape
    local = blocks // 2
    for first in range(0, sources * local, SUBLANES):
        slots = [slot_ref[first + i] for i in range(SUBLANES)]
        tile = jnp.stack(
            [got_ref[p // local, array * local + lax.rem(p, local)] for p in slots], axis=0
        )
        out_ref[:, first : first + SUBLANES, :] = jnp.swapaxes(tile, 0, 1)
    if send:
        rest[0][0] = out_ref[jnp.where(half_ref[0] == 0, rows - 1, 0)]


def pack(slot_ref, out_ref, array, fields):
    groups, _, local, rows, ny = out_ref.shape
    for first in range(0, groups * local, SUBLANES):
        tile = jnp.swapaxes(fields[:, first : first + SUBLANES, :], 0, 1)
        for i in range(SUBLANES):
            p = slot_ref[first + i]
            out_ref[p // local, array, lax.rem(p, local)] = tile[i]


VMEM = pl.BlockSpec(memory_space=pltpu.VMEM)
SMEM = pl.BlockSpec(memory_space=pltpu.SMEM)
HBM = pl.BlockSpec(memory_space=pltpu.HBM)


def on_device(initial, target, birth_step, classes, mobility):
    slabs, groups = lax.axis_size("slab"), lax.axis_size("grp")
    devices = slabs * groups
    slab, me = lax.axis_index("slab"), lax.axis_index("grp")
    local, planes, nz, ny = initial.shape
    rows = nz * planes // groups
    orders = local * groups
    flip = slab % 2
    chip, core = me // 2, me % 2
    half = ((chip == 1) | (chip == 2)).astype(jnp.int32)
    plane = 2 * ((chip // 2) ^ flip) + core

    across = []
    for i in range(slabs * planes // 2 - 1):
        i = 2 * i + 1
        for z in range(2):
            ends = []
            for x in (i, i + 1):
                where = places(groups, x // planes % 2).index((x % planes, z))
                ends.append(x // planes * groups + where)
            across += [tuple(ends), tuple(ends[::-1])]

    def faces_of(cells, edge):
        return (
            lax.ppermute(cells, AXES, across),
            lax.ppermute(cells, "grp", [(g, g ^ 1) for g in range(groups)]),
            lax.ppermute(edge, "grp", [(g, g ^ 2) for g in range(groups)]),
        )

    def everywhere(copies):
        return lax.all_to_all(copies, AXES, 0, 0, tiled=True)

    chain = [(i, i + 1) for i in range(slabs - 1)]
    births = jnp.concatenate(
        [
            lax.ppermute(birth_step[-1:], "slab", chain),
            birth_step,
            lax.ppermute(birth_step[:1], "slab", [(j, i) for i, j in chain]),
        ]
    )
    near = lax.dynamic_slice_in_dim(births, plane, 3, axis=0)
    mine = lax.dynamic_slice_in_dim(near, half * rows, rows, axis=1)
    other = lax.dynamic_slice_in_dim(near[1], jnp.where(half == 0, rows, rows - 1), 1, axis=0)
    first, second = jnp.where(core == 0, mine[0], mine[2]), jnp.where(core == 0, mine[2], mine[0])
    births = jnp.concatenate(
        [mine[1], first, second, jnp.broadcast_to(other, (SUBLANES, ny))], axis=0
    )

    flip = flip.astype(jnp.int32).reshape(1)
    block = (groups, 2 * local + 1, rows, ny)
    message = pl.pallas_call(
        scatter_kernel,
        name="scatter",
        out_shape=pltpu.HBM(block, jnp.float32),
        in_specs=[SMEM, SMEM, HBM, HBM],
        out_specs=HBM,
        scratch_shapes=[
            pltpu.VMEM((rows, ny), jnp.float32),
            pltpu.VMEM(initial.shape, jnp.float32),
            pltpu.VMEM(initial.shape, jnp.float32),
            pltpu.SemaphoreType.DMA((3 * groups,)),
            pltpu.SemaphoreType.DMA((2 * local,)),
        ],
    )(flip, classes, initial, target)
    got = lax.all_to_all(message, "grp", 0, 0, tiled=True)
    kind = got[:, -1, 0, :local].reshape(orders).astype(jnp.int32)
    index = jnp.arange(orders, dtype=jnp.int32)
    ahead = (kind[None, :] < kind[:, None]) | (
        (kind[None, :] == kind[:, None]) & (index[None, :] < index[:, None])
    )
    rank = jnp.sum(ahead.astype(jnp.int32), axis=1)
    slot = jnp.sum(jnp.where(rank[None, :] == index[:, None], index[None, :], 0), axis=1)
    shape, edge_shape = (rows, orders, ny), (1, orders, ny)

    def unpacked(array, outs):
        return pl.pallas_call(
            functools.partial(unpack_kernel, array, len(outs) > 1),
            name=f"unpack{array}",
            out_shape=outs,
            in_specs=[SMEM, SMEM, VMEM],
            out_specs=[VMEM] * len(outs),
            compiler_params=pltpu.CompilerParams(vmem_limit_bytes=16 * 1024 * 1024),
        )(slot, half.reshape(1), got)

    own, edge = unpacked(0, [pltpu.VMEM(s, jnp.float32) for s in (shape, edge_shape)])
    (goal,) = unpacked(1, [pltpu.HBM(shape, jnp.float32)])
    smem = {"core": half.reshape(1), "mob": mobility}
    tiles, own_tiles = (3 * rows + 1, KINDS, ny), (rows, SUBLANES, ny)
    padded = (rows + 2, orders, ny)
    stored = []
    got = weights = None
    for step in range(STEPS):
        first, last = step == 0, step == STEPS - 1
        before, after, beyond = faces_of(own, edge)
        vmem = {"births": births, "before": before, "after": after, "edge": beyond, "own": own}
        ins = {}
        direct = {"moved": shape, "send": edge_shape}
        outs = {"pot": shape, "sums": own_tiles, "w": tiles, "cells": shape}
        outs["copies"] = (2 * devices if first else devices, LANES)
        extra = {"pad": padded, **{n: s for n, s in outs.items() if n != "cells"}}
        if first:
            extra["lin"] = (KINDS, orders, ny)
        else:
            vmem["got"] = got
            ins["wprev"] = weights
            outs["stats"] = (2 + (KINDS if step == 1 else 0), orders, LANES)
            extra["stats"] = outs["stats"]
        if last or first:
            ins["goal"] = goal
        skip = ("goal",) if first else ()
        result = stepped(
            forward_kernel, step, smem, vmem, ins, outs, direct, {"skip": skip, "extra": extra}
        )
        if not first:
            stored[-1]["stats"] = result["stats"]
        own, edge, weights = result["moved"], result["send"], result["w"]
        stored.append({n: result[n] for n in ("cells", "pot", "sums", "w")})
        got = everywhere(result["copies"])
    terms = None
    for step in range(STEPS - 1, -1, -1):
        top, bottom = step == STEPS - 1, step == 0
        before, after, beyond = faces_of(own, edge)
        vmem = {"births": births, "got": got, "before": before, "after": after, "edge": beyond}
        vmem["own"] = own
        ins = dict(stored[step])
        outs, direct = {}, {}
        extra = {"pad": padded}
        if top:
            ins["goal"] = goal
            outs["final"] = shape
        else:
            if bottom:
                ins["linear"] = stored[0]["stats"]
            else:
                ins["mobin"] = terms
        if bottom:
            extra["adj"] = shape
            direct["mobility"] = (SUBLANES, LANES)
            ins["final"] = final_state
            outs["packed"] = extra["packed"] = (groups, 2, local, rows, ny)
        else:
            ins["wnext"] = stored[step - 1]["w"]
            direct["adj"], direct["send"] = shape, edge_shape
            outs["copies"] = extra["copies"] = (devices, LANES)
            if step > 1:
                outs["mobout"] = extra["mobout"] = (SUBLANES, LANES)
        if step == 1:
            ins.update({n + "0": stored[0][n] for n in ("pot", "sums", "stats")})
        result = stepped(
            backward_kernel,
            step,
            {**smem, "slot": slot} if bottom else smem,
            vmem,
            ins,
            outs,
            direct,
            {"extra": extra},
        )
        own = result.get("adj")
        if top:
            final_state = result["final"]
        if bottom:
            mobility_sum = result["mobility"]
        else:
            edge, terms = result["send"], result.get("mobout")
            got = everywhere(result["copies"])

    both = result["packed"]
    both = lax.all_to_all(both, "grp", 0, 0, tiled=True)
    final_state, gradient = pl.pallas_call(
        collect_kernel,
        name="collect",
        out_shape=[pltpu.HBM(initial.shape, jnp.float32)] * 2,
        in_specs=[SMEM, VMEM],
        out_specs=[HBM, HBM],
        scratch_shapes=[pltpu.SemaphoreType.DMA((2 * groups,))],
    )(flip, pltpu.with_memory_space_constraint(both, pltpu.VMEM))
    scale = time_step * (planes * slabs) * nz
    mobility_sum = mobility_sum[0, : KINDS * KINDS].reshape(KINDS, KINDS)
    return final_state, gradient, mobility_sum / scale


def solution(mesh):
    return jax.shard_map(
        on_device,
        mesh=mesh,
        in_specs=(
            P("grp", "slab", None, None),
            P("grp", "slab", None, None),
            P("slab", None, None),
            P("grp"),
            P(),
        ),
        out_specs=(P("grp", "slab", None, None), P("grp", "slab", None, None), P()),
        check_vma=False,
    )
```

```python
import functools

import jax
import jax.numpy as jnp
from jax import lax
from jax.experimental import pallas as pl
from jax.experimental.pallas import tpu as pltpu
from jax.sharding import PartitionSpec as P

STEPS = 4
coupling = 0.3
stiffness = 1.0
time_step = 0.06
LANES = 128
SUBLANES = 8
KINDS = 4
CHUNKS = 4
AXES = ("slab", "grp")


def spread(column, offset):
    n = column.shape[0]
    lane = lax.broadcasted_iota(jnp.int32, (n, LANES), 1)
    row = lax.broadcasted_iota(jnp.int32, (n, LANES), 0)
    return jnp.sum(jnp.where(lane == row + offset, column, 0.0), axis=0, keepdims=True)


def gather(total, offset, n):
    lane = lax.broadcasted_iota(jnp.int32, (n, LANES), 1)
    row = lax.broadcasted_iota(jnp.int32, (n, LANES), 0)
    return jnp.sum(jnp.where(lane == row + offset, total, 0.0), axis=1, keepdims=True)


def beside(cells):
    width = cells.shape[-1]
    lane = lax.broadcasted_iota(jnp.int32, cells.shape, cells.ndim - 1)
    left = jnp.where(lane == 0, 0.0, pltpu.roll(cells, 1, cells.ndim - 1))
    right = jnp.where(lane == width - 1, 0.0, pltpu.roll(cells, width - 1, cells.ndim - 1))
    return left + right


def rolled(tile):
    return [tile] + [pltpu.roll(tile, d, 0) for d in range(1, KINDS)]


def packed(values):
    row = lax.broadcasted_iota(jnp.int32, values[0].shape, 0)
    step = 1
    while len(values) > 1:
        mask = (row // step) % 2 == 0
        values = [
            jnp.where(mask, u, v) + pltpu.roll(jnp.where(mask, v, u), step, 0)
            for u, v in zip(values[0::2], values[1::2])
        ]
        step *= 2
    (tile,) = values
    while step < SUBLANES:
        tile = tile + pltpu.roll(tile, step, 0)
        step *= 2
    return tile


def total_rows(tile):
    step = 1
    while step < SUBLANES:
        tile = tile + pltpu.roll(tile, step, 0)
        step *= 2
    return tile


def class_row(tile, c):
    return jnp.broadcast_to(tile[c : c + 1, :], tile.shape)


def tables(mob_ref, ny, transposed):
    row = lax.broadcasted_iota(jnp.int32, (SUBLANES, ny), 0) % KINDS
    tiles = []
    for d in range(KINDS):
        tile = jnp.zeros((SUBLANES, ny), jnp.float32)
        for c in range(KINDS):
            k = (c - d) % KINDS
            value = mob_ref[k, c] if transposed else mob_ref[c, k]
            tile = jnp.where(row == c, value, tile)
        tiles.append(tile)
    return tiles


def mixed(table, rolls):
    return functools.reduce(jnp.add, [t * r for t, r in zip(table, rolls)])


def active(births_ref, row, step):
    return jnp.where(births_ref[pl.ds(row, 1), :] <= step, 1.0, 0.0)


class Stream:
    def __init__(self, source, target, sems, chunks=1):
        self.source, self.target, self.sems, self.chunks = source, target, sems, chunks

    def copy(self, j):
        if self.chunks == 1:
            return pltpu.make_async_copy(self.source, self.target, self.sems.at[0])
        size = self.target.shape[0] // self.chunks
        return pltpu.make_async_copy(
            self.source.at[pl.ds(j * size, size)],
            self.target.at[pl.ds(j * size, size)],
            self.sems.at[j],
        )

    def start(self, j=0):
        self.copy(j).start()

    def start_all(self):
        for j in range(self.chunks):
            self.start(j)

    def wait(self, j=0):
        self.copy(j).wait()

    def wait_all(self):
        for j in range(self.chunks):
            self.wait(j)


def forward_kernel(step, refs):
    first, last = step == 0, step == STEPS - 1
    core_ref, mob_ref, births_ref, pad_ref = (refs[n] for n in ("core", "mob", "births", "pad"))
    before_ref, after_ref = refs["before"], refs["after"]
    w_ref, sums_ref, moved_ref, pot_ref = (refs[n] for n in ("w", "sums", "moved", "pot"))
    stream = refs["stream"]
    rows, orders, ny = moved_ref.shape
    each = orders // KINDS
    cut = [slice(c * each, (c + 1) * each) for c in range(KINDS)]
    core = core_ref[0]
    inner = pad_ref.at[pl.ds(1, rows)]
    own_ref = refs["own"]
    if not first:
        wprev_ref = refs["wprev"]
        wprev_in = stream("wprev", wprev_ref)
        wprev_in.start()
    sides = [stream("goal", refs["goal"], CHUNKS)] if last else []
    for j in range(CHUNKS):
        for s in sides:
            s.start(j)
    outs = []
    if first:
        lin_ref = refs["lin"]
        lin_ref[...] = jnp.zeros_like(lin_ref)
    else:
        stats_ref = refs["stats"]
        got = refs["got"][...]
        if step == 1:
            odd = lax.broadcasted_iota(jnp.int32, got.shape, 0) % 2 == 1
            second = jnp.sum(jnp.where(odd, got, 0.0), axis=0, keepdims=True)
            got = jnp.where(odd, 0.0, got)
        total = jnp.sum(got, axis=0, keepdims=True)
        raw = gather(total, orders, orders)
        lag = gather(total, 0, orders) / jnp.maximum(raw, 1.0)
        stats_ref[0] = jnp.broadcast_to(lag, (orders, LANES))
        stats_ref[1] = jnp.broadcast_to(raw, (orders, LANES))
        if step == 1:
            lane = lax.broadcasted_iota(jnp.int32, (1, LANES), 1)
            for k in range(KINDS):
                base = gather(second, k * orders, orders)
                level = jnp.sum(
                    jnp.where(lane == 2 * orders + k, total, 0.0), axis=1, keepdims=True
                )
                value = base - jnp.where(raw > 1.0, lag, 0.0) * level
                stats_ref[2 + k] = jnp.broadcast_to(value, (orders, LANES))
        pace = [jnp.broadcast_to(lag[cut[c]] * time_step, (each, ny)) for c in range(KINDS)]
        stats_out = stream("stats", stats_ref, out=True)
        stats_out.start()
        outs.append(stats_out)
    table = tables(mob_ref, ny, False)

    def grown(value, place, c):
        if first:
            return value
        return value + pace[c] * wprev_ref[place, pl.ds(c, 1), :]

    def rates_of(squares, place):
        sums = packed(squares)
        rolls = rolled(sums)
        summed = functools.reduce(jnp.add, rolls)
        gate = active(births_ref, place, step) / (1.0 + summed)
        w = gate * mixed(table, rolls)
        w_ref[place] = w[:KINDS]
        return sums, summed, gate, w

    if not first:
        wprev_in.wait()

    def fill(z, carry):
        for c in range(KINDS):
            pad_ref[z + 1, cut[c], :] = grown(own_ref[z, cut[c], :], z, c)
        return carry

    lax.fori_loop(0, rows, fill, 0, unroll=2)
    cells_out = stream("cells", inner, out=True)
    cells_out.start()
    outs.append(cells_out)
    edge = [grown(refs["edge"][0, cut[c], :], 3 * rows, c) for c in range(KINDS)]
    for c in range(KINDS):
        pad_ref[0, cut[c], :] = jnp.where(core == 1, edge[c], 0.0)
        pad_ref[rows + 1, cut[c], :] = jnp.where(core == 0, edge[c], 0.0)
    rates_of([e * e for e in edge], 3 * rows)

    pot_out = stream("pot", pot_ref, CHUNKS, out=True)

    def line(z, carry):
        numer, denom, extra_a, extra_b, level = carry
        before = [grown(before_ref[z, cut[c], :], rows + z, c) for c in range(KINDS)]
        rates_of([v * v for v in before], rows + z)
        after = [grown(after_ref[z, cut[c], :], 2 * rows + z, c) for c in range(KINDS)]
        rates_of([v * v for v in after], 2 * rows + z)
        cells = [pad_ref[z + 1, cut[c], :] for c in range(KINDS)]
        squares = [e * e for e in cells]
        sums, summed, gate, w = rates_of(squares, z)
        sums_ref[z] = sums
        level_now = gate * sums
        step_w = time_step * w
        base = (6.0 * stiffness - 1.0) + (2.0 * coupling) * summed
        numer, extra_a = list(numer), list(extra_a)
        for c in range(KINDS):
            e = cells[c]
            around = (
                (before[c] + after[c])
                + (pad_ref[z, cut[c], :] + pad_ref[z + 2, cut[c], :])
                + beside(e)
            )
            pot = e * (base + (1.0 - 2.0 * coupling) * squares[c]) - stiffness * around
            pot_ref[z, cut[c], :] = pot
            pushed = class_row(w, c) * pot
            numer[c] = numer[c] + pushed
            moved = e - time_step * pushed
            if last:
                moved = moved - refs["goal"][z, cut[c], :]
                extra_a[c] = extra_a[c] + class_row(step_w, c) * moved
            moved_ref[z, cut[c], :] = moved
            if first:
                for k in range(KINDS):
                    lin_ref[k, cut[c], :] += pot * class_row(level_now, k)
        denom = denom + w
        if last:
            extra_b = extra_b + step_w * step_w
        if first:
            level = level + level_now
        return tuple(numer), denom, tuple(extra_a), extra_b, level

    size = rows // CHUNKS

    def chunk(j, carry):
        for s in sides:
            s.wait(j)
        carry = lax.fori_loop(0, size, lambda i, c: line(j * size + i, c), carry, unroll=4)
        pot_out.start(j)
        return carry

    zero = jnp.zeros((each, ny), jnp.float32)
    numer, denom, extra_a, extra_b, level = lax.fori_loop(
        0,
        CHUNKS,
        chunk,
        ((zero,) * KINDS, zero, (zero,) * KINDS if last else (), zero if last else (), zero if first else ()),
    )
    for name, ref in (("w", w_ref), ("sums", sums_ref)):
        outs.append(stream(name, ref, out=True))
        outs[-1].start()

    def row_of(parts, offset):
        return spread(
            jnp.concatenate([jnp.sum(v, axis=1, keepdims=True) for v in parts], axis=0), offset
        )

    def row_of_classes(tile, offset):
        column = jnp.sum(tile, axis=1, keepdims=True)
        return spread(
            jnp.concatenate(
                [jnp.broadcast_to(column[c : c + 1], (each, 1)) for c in range(KINDS)], axis=0
            ),
            offset,
        )

    row = row_of(numer, 0) + row_of_classes(denom, orders)
    if first:
        row = row + spread(jnp.sum(level, axis=1, keepdims=True)[:KINDS], 2 * orders)
    if last:
        row = row + row_of(extra_a, 2 * orders) + row_of_classes(extra_b, 3 * orders)
    copies_ref = refs["copies"]
    shape = copies_ref.shape
    if first:
        second = functools.reduce(
            jnp.add,
            [
                spread(jnp.sum(lin_ref[k], axis=1, keepdims=True), k * orders)
                for k in range(KINDS)
            ],
        )
        odd = lax.broadcasted_iota(jnp.int32, shape, 0) % 2 == 1
        copies_ref[...] = jnp.where(odd, second, row)
    else:
        copies_ref[...] = jnp.broadcast_to(row, shape)
    outs.append(stream("copies", copies_ref, out=True))
    outs[-1].start()
    refs["send"][0] = moved_ref[jnp.where(core == 0, rows - 1, 0)]
    for s in outs:
        s.wait()
    pot_out.wait_all()


def backward_kernel(step, refs):
    top, bottom = step == STEPS - 1, step == 0
    core_ref, mob_ref, births_ref, pad_ref = (refs[n] for n in ("core", "mob", "births", "pad"))
    own_ref, before_ref, after_ref = refs["own"], refs["before"], refs["after"]
    w_ref, sums_ref, pot_ref, cells_ref = (refs[n] for n in ("w", "sums", "pot", "cells"))
    adj_ref = refs["adj"]
    stream = refs["stream"]
    rows, orders, ny = own_ref.shape
    each = orders // KINDS
    cut = [slice(c * each, (c + 1) * each) for c in range(KINDS)]
    core = core_ref[0]

    ins = [stream("w", w_ref)]
    if not top:
        ins.append(stream("stats", refs["stats"]))
    if bottom:
        ins.append(stream("linear", refs["linear"]))
        final_in = stream("final", refs["final"])
    later_ins = [stream("sums", sums_ref)]
    if not bottom:
        later_ins.append(stream("wnext", refs["wnext"], part=rows))
    if not top and not bottom:
        later_ins.append(stream("mobin", refs["mobin"]))
    if step == 1:
        later_ins += [stream("sums0", refs["sums0"]), stream("stats0", refs["stats0"])]
    sides = [("cells", cells_ref), ("pot", pot_ref)]
    if step == 1:
        sides.append(("pot0", refs["pot0"]))
    sides = [stream(name, ref, CHUNKS) for name, ref in sides]
    if top:
        ins.append(stream("goal", refs["goal"]))
    for s in ins + later_ins:
        s.start()
    for j in range(CHUNKS):
        for s in sides:
            s.start(j)
    if bottom:
        final_in.start()

    total = jnp.sum(refs["got"][...], axis=0, keepdims=True)
    if top:
        raw = gather(total, orders, orders)
        lag = gather(total, 0, orders) / jnp.maximum(raw, 1.0)
        lag_adj = gather(total, 2 * orders, orders) + lag * gather(total, 3 * orders, orders)
    for s in ins:
        s.wait()
    if not top:
        lag = refs["stats"][0][:, :1]
        raw = refs["stats"][1][:, :1]
        lag_adj = gather(total, orders, orders)
    slope_column = lag_adj / jnp.maximum(raw, 1.0)
    keep = jnp.where(raw > 1.0, lag, 0.0)

    def wide(column):
        return [jnp.broadcast_to(column[cut[c]], (each, ny)) for c in range(KINDS)]

    slope = wide(slope_column)
    lag_wide = wide(lag)
    slope_keep = wide(slope_column * keep)
    table = tables(mob_ref, ny, True)
    outs = []

    def grown(value, place, c):
        weight = w_ref[place, pl.ds(c, 1), :]
        if top:
            value = value + (time_step * lag_wide[c]) * weight
        return value, weight * (slope[c] - time_step * value)

    def fill(z, carry):
        for c in range(KINDS):
            value, pushed = grown(own_ref[z, cut[c], :], z, c)
            pad_ref[z + 1, cut[c], :] = pushed
            if top:
                adj_ref[z, cut[c], :] = value
                refs["goal"][z, cut[c], :] = value + refs["goal"][z, cut[c], :]
        return carry

    lax.fori_loop(0, rows, fill, 0, unroll=2)
    if top:
        outs.append(stream("final", refs["goal"], out=True))
        outs[-1].start()
    for c in range(KINDS):
        pushed = grown(refs["edge"][0, cut[c], :], 3 * rows, c)[1]
        pad_ref[0, cut[c], :] = jnp.where(core == 1, pushed, 0.0)
        pad_ref[rows + 1, cut[c], :] = jnp.where(core == 0, pushed, 0.0)
    for s in later_ins:
        s.wait()
    if step == 1:
        lag0 = wide(refs["stats0"][0][:, :1])
    source_ref = adj_ref if top else own_ref
    if bottom:
        final_in.wait()
        pack(refs["slot"], refs["packed"], 0, refs["final"])
        outs.append(stream("packed", refs["packed"], out=True, field=0))
        outs[-1].start()

    def line(z, carry):
        mob, onward = carry
        sums = sums_ref[z]
        rolls = rolled(sums)
        summed = functools.reduce(jnp.add, rolls)
        act = active(births_ref, z, step)
        adj = [source_ref[z, cut[c], :] for c in range(KINDS)]
        cells = [cells_ref[z, cut[c], :] for c in range(KINDS)]
        pots = [pot_ref[z, cut[c], :] for c in range(KINDS)]
        pushed = [pad_ref[z + 1, cut[c], :] for c in range(KINDS)]
        drive = packed(
            [
                (slope[c] * pots[c] - slope_keep[c])
                - time_step * adj[c] * (pots[c] - lag_wide[c])
                for c in range(KINDS)
            ]
        )
        plain = drive / (1.0 + summed)
        drive = act * plain
        shared = total_rows(
            (2.0 * coupling)
            * functools.reduce(jnp.add, [pushed[c] * cells[c] for c in range(KINDS)])
            - (KINDS / SUBLANES) * (jnp.concatenate([w_ref[z]] * (SUBLANES // KINDS)) * plain)
        )
        class_adj = 2.0 * (mixed(table, rolled(drive)) + shared)
        if not bottom:
            mob = tuple(m + drive * r for m, r in zip(mob, rolls))
        base = (6.0 * stiffness - 1.0) + (2.0 * coupling) * summed
        onward = list(onward)
        later = []
        for c in range(KINDS):
            around = (
                grown(before_ref[z, cut[c], :], rows + z, c)[1]
                + grown(after_ref[z, cut[c], :], 2 * rows + z, c)[1]
                + (pad_ref[z, cut[c], :] + pad_ref[z + 2, cut[c], :])
                + beside(pushed[c])
            )
            e = cells[c]
            new = (
                adj[c]
                + pushed[c] * (base + (3.0 - 6.0 * coupling) * (e * e))
                - stiffness * around
                + e * class_row(class_adj, c)
            )
            adj_ref[z, cut[c], :] = new
            if not bottom:
                onward[c] = onward[c] + refs["wnext"][z, pl.ds(c, 1), :] * new
            later.append(new)
        if step == 1:
            sums0 = rolled(refs["sums0"][z])
            gate = active(births_ref, z, 0) / (1.0 + functools.reduce(jnp.add, sums0))
            drive = (-time_step * gate) * packed(
                [later[c] * (refs["pot0"][z, cut[c], :] - lag0[c]) for c in range(KINDS)]
            )
            mob = tuple(m + drive * r for m, r in zip(mob, sums0))
        return mob, tuple(onward)

    size = rows // CHUNKS

    def chunk(j, carry):
        for s in sides:
            s.wait(j)
        carry = lax.fori_loop(0, size, lambda i, c: line(j * size + i, c), carry, unroll=4)
        return carry

    zero = jnp.zeros((each, ny), jnp.float32)
    mob, onward = lax.fori_loop(
        0, CHUNKS, chunk, (() if bottom else (zero,) * KINDS, () if bottom else (zero,) * KINDS)
    )
    if bottom:
        lane = lax.broadcasted_iota(jnp.int32, (1, LANES), 1)
        row = jnp.where(lane < KINDS * KINDS, total, 0.0)
        lane = lax.broadcasted_iota(jnp.int32, (orders, LANES), 1)
        home = lax.broadcasted_iota(jnp.int32, (orders, LANES), 0) // each
        for k in range(KINDS):
            value = slope_column * refs["linear"][2 + k][:, :1]
            row = row + jnp.sum(
                jnp.where(lane == home * KINDS + k, value, 0.0), axis=0, keepdims=True
            )
        refs["mobility"][...] = jnp.broadcast_to(row, refs["mobility"].shape)
        pack(refs["slot"], refs["packed"], 1, adj_ref)
        outs.append(stream("packed", refs["packed"], out=True, field=1))
        outs[-1].start()
    else:
        row = time_step * spread(
            jnp.concatenate([jnp.sum(v, axis=1, keepdims=True) for v in onward], axis=0), orders
        )
        lane = lax.broadcasted_iota(jnp.int32, (KINDS, LANES), 1)
        kind = lax.broadcasted_iota(jnp.int32, (KINDS, LANES), 0)
        terms = jnp.zeros((1, LANES), jnp.float32)
        for d in range(KINDS):
            column = jnp.sum(mob[d], axis=1, keepdims=True)[:KINDS]
            spot = kind * KINDS + (kind + (KINDS - d)) % KINDS
            terms = terms + jnp.sum(jnp.where(lane == spot, column, 0.0), axis=0, keepdims=True)
        if not top:
            terms = terms + refs["mobin"][:1]
        if step == 1:
            row = row + terms
        else:
            refs["mobout"][...] = jnp.broadcast_to(terms, refs["mobout"].shape)
            outs.append(stream("mobout", refs["mobout"], out=True))
            outs[-1].start()
        refs["copies"][...] = jnp.broadcast_to(row, refs["copies"].shape)
        outs.append(stream("copies", refs["copies"], out=True))
        outs[-1].start()
        refs["send"][0] = adj_ref[jnp.where(core == 0, rows - 1, 0)]
    for s in outs:
        s.wait()


def stepped(kernel, step, smem, vmem, ins, outs, direct, scratch):
    names = list(smem) + list(vmem) + list(ins)
    pinned = [pltpu.with_memory_space_constraint(v, pltpu.HBM) for v in ins.values()]
    near = [
        pltpu.with_memory_space_constraint(v, pltpu.VMEM) if n == "own" else v
        for n, v in vmem.items()
    ]
    operands = [*smem.values(), *near, *pinned]
    out_names = list(outs) + list(direct)
    buffers = {n: (v.shape, v.dtype) for n, v in ins.items() if n not in scratch.get("skip", ())}
    buffers.update({n: (s, jnp.float32) for n, s in scratch["extra"].items()})
    streamed = [("i", n) for n in ins] + [("o", n) for n in outs]
    sems = [pltpu.SemaphoreType.DMA((CHUNKS,))] * len(streamed)

    def body(*args):
        args = list(args)
        table = dict(zip(names, args))
        args = args[len(names) :]
        hbm_out = dict(zip(out_names, args))
        args = args[len(out_names) :]
        bufs = dict(zip(buffers, args))
        sem = dict(zip(streamed, args[len(buffers) :]))
        hbm_in = {n: table.pop(n) for n in ins}
        refs = {**table, **bufs, **{n: hbm_out[n] for n in direct}}

        def stream(name, ref, chunks=1, out=False, part=None, field=None):
            if field is not None:
                target, sems = hbm_out[name].at[:, field], sem["o", name].at[pl.ds(field, 1)]
                return Stream(ref.at[:, field], target, sems)
            if out:
                return Stream(ref, hbm_out[name], sem["o", name], chunks)
            source = hbm_in[name]
            if part:
                source, ref = source.at[pl.ds(0, part)], ref.at[pl.ds(0, part)]
            return Stream(source, ref, sem["i", name], chunks)

        refs["stream"] = stream
        kernel(step, refs)

    result = pl.pallas_call(
        body,
        name=f"{kernel.__name__}_{step}",
        out_shape=[pltpu.HBM(s, jnp.float32) for s in outs.values()]
        + [pltpu.VMEM(s, jnp.float32) for s in direct.values()],
        in_specs=[SMEM] * len(smem) + [VMEM] * len(vmem) + [HBM] * len(ins),
        out_specs=[HBM] * len(outs) + [VMEM] * len(direct),
        scratch_shapes=[pltpu.VMEM(s, d) for s, d in buffers.values()] + sems,
        compiler_params=pltpu.CompilerParams(vmem_limit_bytes=24 * 1024 * 1024),
    )(*operands)
    return dict(zip(out_names, result))


def places(groups, flip):
    ring = [(0, 0), (0, 1), (1, 1), (1, 0)]
    found = []
    for g in range(groups):
        pair, half = ring[g // 2]
        found.append((2 * (pair ^ flip) + g % 2, half))
    return found


def scatter_kernel(
    flip_ref, kinds_ref, first_ref, second_ref, out_ref, tag_ref, stage_a, stage_b, sems, sems_in
):
    groups, blocks, rows, ny = out_ref.shape
    local = first_ref.shape[0]
    loads = [
        pltpu.make_async_copy(ref.at[i], stage.at[i], sems_in.at[a * local + i])
        for a, (ref, stage) in enumerate(((first_ref, stage_a), (second_ref, stage_b)))
        for i in range(local)
    ]
    for c in loads:
        c.start()
    lane = lax.broadcasted_iota(jnp.int32, (rows, ny), 1)
    tag = jnp.zeros((rows, ny), jnp.float32)
    for i in range(local):
        tag = jnp.where(lane == i, kinds_ref[i].astype(jnp.float32), tag)
    tag_ref[...] = tag
    copies = []
    for g, (plane, half) in enumerate(places(groups, 0)):
        plane = plane ^ (2 * flip_ref[0])
        for a, ref in enumerate((stage_a, stage_b)):
            copies.append(
                pltpu.make_async_copy(
                    ref.at[:, plane, pl.ds(half * rows, rows), :],
                    out_ref.at[g, pl.ds(a * local, local)],
                    sems.at[3 * g + a],
                )
            )
        copies.append(
            pltpu.make_async_copy(tag_ref, out_ref.at[g, blocks - 1], sems.at[3 * g + 2])
        )
    for a in range(2):
        for c in loads[a * local : (a + 1) * local]:
            c.wait()
        for c in copies[a::3] + (copies[2::3] if a == 0 else []):
            c.start()
    for c in copies:
        c.wait()


def collect_kernel(flip_ref, got_ref, first_ref, second_ref, sems):
    groups, _, local, rows, ny = got_ref.shape
    copies = []
    for g, (plane, half) in enumerate(places(groups, 0)):
        plane = plane ^ (2 * flip_ref[0])
        for a, ref in enumerate((first_ref, second_ref)):
            copies.append(
                pltpu.make_async_copy(
                    got_ref.at[g, a],
                    ref.at[:, plane, pl.ds(half * rows, rows), :],
                    sems.at[2 * g + a],
                )
            )
    for c in copies:
        c.start()
    for c in copies:
        c.wait()


def unpack_kernel(array, send, slot_ref, half_ref, got_ref, out_ref, *rest):
    sources, blocks, rows, ny = got_ref.shape
    local = blocks // 2
    for first in range(0, sources * local, SUBLANES):
        slots = [slot_ref[first + i] for i in range(SUBLANES)]
        tile = jnp.stack(
            [got_ref[p // local, array * local + lax.rem(p, local)] for p in slots], axis=0
        )
        out_ref[:, first : first + SUBLANES, :] = jnp.swapaxes(tile, 0, 1)
    if send:
        rest[0][0] = out_ref[jnp.where(half_ref[0] == 0, rows - 1, 0)]


def pack(slot_ref, out_ref, array, fields):
    groups, _, local, rows, ny = out_ref.shape
    for first in range(0, groups * local, SUBLANES):
        tile = jnp.swapaxes(fields[:, first : first + SUBLANES, :], 0, 1)
        for i in range(SUBLANES):
            p = slot_ref[first + i]
            out_ref[p // local, array, lax.rem(p, local)] = tile[i]


VMEM = pl.BlockSpec(memory_space=pltpu.VMEM)
SMEM = pl.BlockSpec(memory_space=pltpu.SMEM)
HBM = pl.BlockSpec(memory_space=pltpu.HBM)


def on_device(initial, target, birth_step, classes, mobility):
    slabs, groups = lax.axis_size("slab"), lax.axis_size("grp")
    devices = slabs * groups
    slab, me = lax.axis_index("slab"), lax.axis_index("grp")
    local, planes, nz, ny = initial.shape
    rows = nz * planes // groups
    orders = local * groups
    flip = slab % 2
    chip, core = me // 2, me % 2
    half = ((chip == 1) | (chip == 2)).astype(jnp.int32)
    plane = 2 * ((chip // 2) ^ flip) + core

    across = []
    for i in range(slabs * planes // 2 - 1):
        i = 2 * i + 1
        for z in range(2):
            ends = []
            for x in (i, i + 1):
                where = places(groups, x // planes % 2).index((x % planes, z))
                ends.append(x // planes * groups + where)
            across += [tuple(ends), tuple(ends[::-1])]

    def faces_of(cells, edge):
        return (
            lax.ppermute(cells, AXES, across),
            lax.ppermute(cells, "grp", [(g, g ^ 1) for g in range(groups)]),
            lax.ppermute(edge, "grp", [(g, g ^ 2) for g in range(groups)]),
        )

    def everywhere(copies):
        return lax.all_to_all(copies, AXES, 0, 0, tiled=True)

    chain = [(i, i + 1) for i in range(slabs - 1)]
    births = jnp.concatenate(
        [
            lax.ppermute(birth_step[-1:], "slab", chain),
            birth_step,
            lax.ppermute(birth_step[:1], "slab", [(j, i) for i, j in chain]),
        ]
    )
    near = lax.dynamic_slice_in_dim(births, plane, 3, axis=0)
    mine = lax.dynamic_slice_in_dim(near, half * rows, rows, axis=1)
    other = lax.dynamic_slice_in_dim(near[1], jnp.where(half == 0, rows, rows - 1), 1, axis=0)
    first, second = jnp.where(core == 0, mine[0], mine[2]), jnp.where(core == 0, mine[2], mine[0])
    births = jnp.concatenate(
        [mine[1], first, second, jnp.broadcast_to(other, (SUBLANES, ny))], axis=0
    )

    flip = flip.astype(jnp.int32).reshape(1)
    block = (groups, 2 * local + 1, rows, ny)
    message = pl.pallas_call(
        scatter_kernel,
        name="scatter",
        out_shape=pltpu.HBM(block, jnp.float32),
        in_specs=[SMEM, SMEM, HBM, HBM],
        out_specs=HBM,
        scratch_shapes=[
            pltpu.VMEM((rows, ny), jnp.float32),
            pltpu.VMEM(initial.shape, jnp.float32),
            pltpu.VMEM(initial.shape, jnp.float32),
            pltpu.SemaphoreType.DMA((3 * groups,)),
            pltpu.SemaphoreType.DMA((2 * local,)),
        ],
    )(flip, classes, initial, target)
    got = lax.all_to_all(message, "grp", 0, 0, tiled=True)
    kind = got[:, -1, 0, :local].reshape(orders).astype(jnp.int32)
    index = jnp.arange(orders, dtype=jnp.int32)
    ahead = (kind[None, :] < kind[:, None]) | (
        (kind[None, :] == kind[:, None]) & (index[None, :] < index[:, None])
    )
    rank = jnp.sum(ahead.astype(jnp.int32), axis=1)
    slot = jnp.sum(jnp.where(rank[None, :] == index[:, None], index[None, :], 0), axis=1)
    shape, edge_shape = (rows, orders, ny), (1, orders, ny)

    def unpacked(array, outs):
        return pl.pallas_call(
            functools.partial(unpack_kernel, array, len(outs) > 1),
            name=f"unpack{array}",
            out_shape=outs,
            in_specs=[SMEM, SMEM, VMEM],
            out_specs=[VMEM] * len(outs),
            compiler_params=pltpu.CompilerParams(vmem_limit_bytes=16 * 1024 * 1024),
        )(slot, half.reshape(1), got)

    own, edge = unpacked(0, [pltpu.VMEM(s, jnp.float32) for s in (shape, edge_shape)])
    (goal,) = unpacked(1, [pltpu.HBM(shape, jnp.float32)])
    smem = {"core": half.reshape(1), "mob": mobility}
    tiles, own_tiles = (3 * rows + 1, KINDS, ny), (rows, SUBLANES, ny)
    padded = (rows + 2, orders, ny)
    stored = []
    got = weights = None
    for step in range(STEPS):
        first, last = step == 0, step == STEPS - 1
        before, after, beyond = faces_of(own, edge)
        vmem = {"births": births, "before": before, "after": after, "edge": beyond, "own": own}
        ins = {}
        direct = {"moved": shape, "send": edge_shape}
        outs = {"pot": shape, "sums": own_tiles, "w": tiles, "cells": shape}
        outs["copies"] = (2 * devices if first else devices, LANES)
        extra = {"pad": padded, **{n: s for n, s in outs.items() if n != "cells"}}
        if first:
            extra["lin"] = (KINDS, orders, ny)
        else:
            vmem["got"] = got
            ins["wprev"] = weights
            outs["stats"] = (2 + (KINDS if step == 1 else 0), orders, LANES)
            extra["stats"] = outs["stats"]
        if last or first:
            ins["goal"] = goal
        skip = ("goal",) if first else ()
        result = stepped(
            forward_kernel, step, smem, vmem, ins, outs, direct, {"skip": skip, "extra": extra}
        )
        if not first:
            stored[-1]["stats"] = result["stats"]
        own, edge, weights = result["moved"], result["send"], result["w"]
        stored.append({n: result[n] for n in ("cells", "pot", "sums", "w")})
        got = everywhere(result["copies"])
    terms = None
    for step in range(STEPS - 1, -1, -1):
        top, bottom = step == STEPS - 1, step == 0
        before, after, beyond = faces_of(own, edge)
        vmem = {"births": births, "got": got, "before": before, "after": after, "edge": beyond}
        vmem["own"] = own
        ins = dict(stored[step])
        outs, direct = {}, {}
        extra = {"pad": padded}
        if top:
            ins["goal"] = goal
            outs["final"] = shape
        else:
            if bottom:
                ins["linear"] = stored[0]["stats"]
            else:
                ins["mobin"] = terms
        if bottom:
            extra["adj"] = shape
            direct["mobility"] = (SUBLANES, LANES)
            ins["final"] = final_state
            outs["packed"] = extra["packed"] = (groups, 2, local, rows, ny)
        else:
            ins["wnext"] = stored[step - 1]["w"]
            direct["adj"], direct["send"] = shape, edge_shape
            outs["copies"] = extra["copies"] = (devices, LANES)
            if step > 1:
                outs["mobout"] = extra["mobout"] = (SUBLANES, LANES)
        if step == 1:
            ins.update({n + "0": stored[0][n] for n in ("pot", "sums", "stats")})
        result = stepped(
            backward_kernel,
            step,
            {**smem, "slot": slot} if bottom else smem,
            vmem,
            ins,
            outs,
            direct,
            {"extra": extra},
        )
        own = result.get("adj")
        if top:
            final_state = result["final"]
        if bottom:
            mobility_sum = result["mobility"]
        else:
            edge, terms = result["send"], result.get("mobout")
            got = everywhere(result["copies"])

    both = result["packed"]
    both = lax.all_to_all(both, "grp", 0, 0, tiled=True)
    final_state, gradient = pl.pallas_call(
        collect_kernel,
        name="collect",
        out_shape=[pltpu.HBM(initial.shape, jnp.float32)] * 2,
        in_specs=[SMEM, VMEM],
        out_specs=[HBM, HBM],
        scratch_shapes=[pltpu.SemaphoreType.DMA((2 * groups,))],
    )(flip, pltpu.with_memory_space_constraint(both, pltpu.VMEM))
    scale = time_step * (planes * slabs) * nz
    mobility_sum = mobility_sum[0, : KINDS * KINDS].reshape(KINDS, KINDS)
    return final_state, gradient, mobility_sum / scale


def solution(mesh):
    return jax.shard_map(
        on_device,
        mesh=mesh,
        in_specs=(
            P("grp", "slab", None, None),
            P("grp", "slab", None, None),
            P("slab", None, None),
            P("grp"),
            P(),
        ),
        out_specs=(P("grp", "slab", None, None), P("grp", "slab", None, None), P()),
        check_vma=False,
    )
```

```python
import functools

import jax
import jax.numpy as jnp
from jax import lax
from jax.experimental import pallas as pl
from jax.experimental.pallas import tpu as pltpu
from jax.sharding import PartitionSpec as P

STEPS = 4
coupling = 0.3
stiffness = 1.0
time_step = 0.06
LANES = 128
SUBLANES = 8
KINDS = 4
CHUNKS = 2
AXES = ("slab", "grp")


def spread(column, offset):
    n = column.shape[0]
    lane = lax.broadcasted_iota(jnp.int32, (n, LANES), 1)
    row = lax.broadcasted_iota(jnp.int32, (n, LANES), 0)
    return jnp.sum(jnp.where(lane == row + offset, column, 0.0), axis=0, keepdims=True)


def gather(total, offset, n):
    lane = lax.broadcasted_iota(jnp.int32, (n, LANES), 1)
    row = lax.broadcasted_iota(jnp.int32, (n, LANES), 0)
    return jnp.sum(jnp.where(lane == row + offset, total, 0.0), axis=1, keepdims=True)


def beside(cells):
    width = cells.shape[-1]
    lane = lax.broadcasted_iota(jnp.int32, cells.shape, cells.ndim - 1)
    left = jnp.where(lane == 0, 0.0, pltpu.roll(cells, 1, cells.ndim - 1))
    right = jnp.where(lane == width - 1, 0.0, pltpu.roll(cells, width - 1, cells.ndim - 1))
    return left + right


def rolled(tile):
    return [tile] + [pltpu.roll(tile, d, 0) for d in range(1, KINDS)]


def packed(values):
    row = lax.broadcasted_iota(jnp.int32, values[0].shape, 0)
    step = 1
    while len(values) > 1:
        mask = (row // step) % 2 == 0
        values = [
            jnp.where(mask, u, v) + pltpu.roll(jnp.where(mask, v, u), step, 0)
            for u, v in zip(values[0::2], values[1::2])
        ]
        step *= 2
    (tile,) = values
    while step < SUBLANES:
        tile = tile + pltpu.roll(tile, step, 0)
        step *= 2
    return tile


def total_rows(tile):
    step = 1
    while step < SUBLANES:
        tile = tile + pltpu.roll(tile, step, 0)
        step *= 2
    return tile


def class_row(tile, c):
    return jnp.broadcast_to(tile[c : c + 1, :], tile.shape)


def tables(mob_ref, ny, transposed):
    row = lax.broadcasted_iota(jnp.int32, (SUBLANES, ny), 0) % KINDS
    tiles = []
    for d in range(KINDS):
        tile = jnp.zeros((SUBLANES, ny), jnp.float32)
        for c in range(KINDS):
            k = (c - d) % KINDS
            value = mob_ref[k, c] if transposed else mob_ref[c, k]
            tile = jnp.where(row == c, value, tile)
        tiles.append(tile)
    return tiles


def mixed(table, rolls):
    return functools.reduce(jnp.add, [t * r for t, r in zip(table, rolls)])


def active(births_ref, row, step):
    return jnp.where(births_ref[pl.ds(row, 1), :] <= step, 1.0, 0.0)


class Stream:
    def __init__(self, source, target, sems, chunks=1):
        self.source, self.target, self.sems, self.chunks = source, target, sems, chunks

    def copy(self, j):
        if self.chunks == 1:
            return pltpu.make_async_copy(self.source, self.target, self.sems.at[0])
        size = self.target.shape[0] // self.chunks
        return pltpu.make_async_copy(
            self.source.at[pl.ds(j * size, size)],
            self.target.at[pl.ds(j * size, size)],
            self.sems.at[j],
        )

    def start(self, j=0):
        self.copy(j).start()

    def start_all(self):
        for j in range(self.chunks):
            self.start(j)

    def wait(self, j=0):
        self.copy(j).wait()

    def wait_all(self):
        for j in range(self.chunks):
            self.wait(j)


def forward_kernel(step, refs):
    first, last = step == 0, step == STEPS - 1
    core_ref, mob_ref, births_ref, pad_ref = (refs[n] for n in ("core", "mob", "births", "pad"))
    before_ref, after_ref = refs["before"], refs["after"]
    w_ref, sums_ref, moved_ref, pot_ref = (refs[n] for n in ("w", "sums", "moved", "pot"))
    stream = refs["stream"]
    rows, orders, ny = moved_ref.shape
    each = orders // KINDS
    cut = [slice(c * each, (c + 1) * each) for c in range(KINDS)]
    core = core_ref[0]
    inner = pad_ref.at[pl.ds(1, rows)]
    own_ref = refs["own"]
    if not first:
        wprev_ref = refs["wprev"]
        wprev_in = stream("wprev", wprev_ref)
        wprev_in.start()
    sides = [stream("goal", refs["goal"], CHUNKS)] if last else []
    for j in range(CHUNKS):
        for s in sides:
            s.start(j)
    outs = []
    if first:
        lin_ref = refs["lin"]
        lin_ref[...] = jnp.zeros_like(lin_ref)
    else:
        stats_ref = refs["stats"]
        got = refs["got"][...]
        if step == 1:
            odd = lax.broadcasted_iota(jnp.int32, got.shape, 0) % 2 == 1
            second = jnp.sum(jnp.where(odd, got, 0.0), axis=0, keepdims=True)
            got = jnp.where(odd, 0.0, got)
        total = jnp.sum(got, axis=0, keepdims=True)
        raw = gather(total, orders, orders)
        lag = gather(total, 0, orders) / jnp.maximum(raw, 1.0)
        stats_ref[0] = jnp.broadcast_to(lag, (orders, LANES))
        stats_ref[1] = jnp.broadcast_to(raw, (orders, LANES))
        if step == 1:
            lane = lax.broadcasted_iota(jnp.int32, (1, LANES), 1)
            for k in range(KINDS):
                base = gather(second, k * orders, orders)
                level = jnp.sum(
                    jnp.where(lane == 2 * orders + k, total, 0.0), axis=1, keepdims=True
                )
                value = base - jnp.where(raw > 1.0, lag, 0.0) * level
                stats_ref[2 + k] = jnp.broadcast_to(value, (orders, LANES))
        pace = [jnp.broadcast_to(lag[cut[c]] * time_step, (each, ny)) for c in range(KINDS)]
        stats_out = stream("stats", stats_ref, out=True)
        stats_out.start()
        outs.append(stats_out)
    table = tables(mob_ref, ny, False)

    def grown(value, place, c):
        if first:
            return value
        return value + pace[c] * wprev_ref[place, pl.ds(c, 1), :]

    def rates_of(squares, place):
        sums = packed(squares)
        rolls = rolled(sums)
        summed = functools.reduce(jnp.add, rolls)
        gate = active(births_ref, place, step) / (1.0 + summed)
        w = gate * mixed(table, rolls)
        w_ref[place] = w[:KINDS]
        return sums, summed, gate, w

    if not first:
        wprev_in.wait()

    def fill(z, carry):
        for c in range(KINDS):
            pad_ref[z + 1, cut[c], :] = grown(own_ref[z, cut[c], :], z, c)
        return carry

    lax.fori_loop(0, rows, fill, 0, unroll=4)
    cells_out = stream("cells", inner, out=True)
    cells_out.start()
    outs.append(cells_out)
    edge = [grown(refs["edge"][0, cut[c], :], 3 * rows, c) for c in range(KINDS)]
    for c in range(KINDS):
        pad_ref[0, cut[c], :] = jnp.where(core == 1, edge[c], 0.0)
        pad_ref[rows + 1, cut[c], :] = jnp.where(core == 0, edge[c], 0.0)
    rates_of([e * e for e in edge], 3 * rows)

    pot_out = stream("pot", pot_ref, CHUNKS, out=True)

    def line(z, carry):
        numer, denom, extra_a, extra_b, level = carry
        before = [grown(before_ref[z, cut[c], :], rows + z, c) for c in range(KINDS)]
        rates_of([v * v for v in before], rows + z)
        after = [grown(after_ref[z, cut[c], :], 2 * rows + z, c) for c in range(KINDS)]
        rates_of([v * v for v in after], 2 * rows + z)
        cells = [pad_ref[z + 1, cut[c], :] for c in range(KINDS)]
        squares = [e * e for e in cells]
        sums, summed, gate, w = rates_of(squares, z)
        sums_ref[z] = sums
        level_now = gate * sums
        step_w = time_step * w
        base = (6.0 * stiffness - 1.0) + (2.0 * coupling) * summed
        numer, extra_a = list(numer), list(extra_a)
        for c in range(KINDS):
            e = cells[c]
            around = (
                (before[c] + after[c])
                + (pad_ref[z, cut[c], :] + pad_ref[z + 2, cut[c], :])
                + beside(e)
            )
            pot = e * (base + (1.0 - 2.0 * coupling) * squares[c]) - stiffness * around
            pot_ref[z, cut[c], :] = pot
            pushed = class_row(w, c) * pot
            numer[c] = numer[c] + pushed
            moved = e - time_step * pushed
            if last:
                moved = moved - refs["goal"][z, cut[c], :]
                extra_a[c] = extra_a[c] + class_row(step_w, c) * moved
            moved_ref[z, cut[c], :] = moved
            if first:
                for k in range(KINDS):
                    lin_ref[k, cut[c], :] += pot * class_row(level_now, k)
        denom = denom + w
        if last:
            extra_b = extra_b + step_w * step_w
        if first:
            level = level + level_now
        return tuple(numer), denom, tuple(extra_a), extra_b, level

    size = rows // CHUNKS

    def chunk(j, carry):
        for s in sides:
            s.wait(j)
        carry = lax.fori_loop(0, size, lambda i, c: line(j * size + i, c), carry, unroll=8)
        pot_out.start(j)
        return carry

    zero = jnp.zeros((each, ny), jnp.float32)
    numer, denom, extra_a, extra_b, level = lax.fori_loop(
        0,
        CHUNKS,
        chunk,
        ((zero,) * KINDS, zero, (zero,) * KINDS if last else (), zero if last else (), zero if first else ()),
    )
    for name, ref in (("w", w_ref), ("sums", sums_ref)):
        outs.append(stream(name, ref, out=True))
        outs[-1].start()

    def row_of(parts, offset):
        return spread(
            jnp.concatenate([jnp.sum(v, axis=1, keepdims=True) for v in parts], axis=0), offset
        )

    def row_of_classes(tile, offset):
        column = jnp.sum(tile, axis=1, keepdims=True)
        return spread(
            jnp.concatenate(
                [jnp.broadcast_to(column[c : c + 1], (each, 1)) for c in range(KINDS)], axis=0
            ),
            offset,
        )

    row = row_of(numer, 0) + row_of_classes(denom, orders)
    if first:
        row = row + spread(jnp.sum(level, axis=1, keepdims=True)[:KINDS], 2 * orders)
    if last:
        row = row + row_of(extra_a, 2 * orders) + row_of_classes(extra_b, 3 * orders)
    copies_ref = refs["copies"]
    shape = copies_ref.shape
    if first:
        second = functools.reduce(
            jnp.add,
            [
                spread(jnp.sum(lin_ref[k], axis=1, keepdims=True), k * orders)
                for k in range(KINDS)
            ],
        )
        odd = lax.broadcasted_iota(jnp.int32, shape, 0) % 2 == 1
        copies_ref[...] = jnp.where(odd, second, row)
    else:
        copies_ref[...] = jnp.broadcast_to(row, shape)
    outs.append(stream("copies", copies_ref, out=True))
    outs[-1].start()
    refs["send"][0] = moved_ref[jnp.where(core == 0, rows - 1, 0)]
    for s in outs:
        s.wait()
    pot_out.wait_all()


def backward_kernel(step, refs):
    top, bottom = step == STEPS - 1, step == 0
    core_ref, mob_ref, births_ref, pad_ref = (refs[n] for n in ("core", "mob", "births", "pad"))
    own_ref, before_ref, after_ref = refs["own"], refs["before"], refs["after"]
    w_ref, sums_ref, pot_ref, cells_ref = (refs[n] for n in ("w", "sums", "pot", "cells"))
    adj_ref = refs["adj"]
    stream = refs["stream"]
    rows, orders, ny = own_ref.shape
    each = orders // KINDS
    cut = [slice(c * each, (c + 1) * each) for c in range(KINDS)]
    core = core_ref[0]

    ins = [stream("w", w_ref)]
    if not top:
        ins.append(stream("stats", refs["stats"]))
    if bottom:
        ins.append(stream("linear", refs["linear"]))
        final_in = stream("final", refs["final"])
    later_ins = [stream("sums", sums_ref)]
    if not bottom:
        later_ins.append(stream("wnext", refs["wnext"], part=rows))
    if not top and not bottom:
        later_ins.append(stream("mobin", refs["mobin"]))
    if step == 1:
        later_ins += [stream("sums0", refs["sums0"]), stream("stats0", refs["stats0"])]
    sides = [("cells", cells_ref), ("pot", pot_ref)]
    if step == 1:
        sides.append(("pot0", refs["pot0"]))
    sides = [stream(name, ref, CHUNKS) for name, ref in sides]
    if top:
        ins.append(stream("goal", refs["goal"]))
    for s in ins + later_ins:
        s.start()
    for j in range(CHUNKS):
        for s in sides:
            s.start(j)
    if bottom:
        final_in.start()

    total = jnp.sum(refs["got"][...], axis=0, keepdims=True)
    if top:
        raw = gather(total, orders, orders)
        lag = gather(total, 0, orders) / jnp.maximum(raw, 1.0)
        lag_adj = gather(total, 2 * orders, orders) + lag * gather(total, 3 * orders, orders)
    for s in ins:
        s.wait()
    if not top:
        lag = refs["stats"][0][:, :1]
        raw = refs["stats"][1][:, :1]
        lag_adj = gather(total, orders, orders)
    slope_column = lag_adj / jnp.maximum(raw, 1.0)
    keep = jnp.where(raw > 1.0, lag, 0.0)

    def wide(column):
        return [jnp.broadcast_to(column[cut[c]], (each, ny)) for c in range(KINDS)]

    slope = wide(slope_column)
    lag_wide = wide(lag)
    slope_keep = wide(slope_column * keep)
    table = tables(mob_ref, ny, True)
    outs = []

    def grown(value, place, c):
        weight = w_ref[place, pl.ds(c, 1), :]
        if top:
            value = value + (time_step * lag_wide[c]) * weight
        return value, weight * (slope[c] - time_step * value)

    def fill(z, carry):
        for c in range(KINDS):
            value, pushed = grown(own_ref[z, cut[c], :], z, c)
            pad_ref[z + 1, cut[c], :] = pushed
            if top:
                adj_ref[z, cut[c], :] = value
                refs["goal"][z, cut[c], :] = value + refs["goal"][z, cut[c], :]
        return carry

    lax.fori_loop(0, rows, fill, 0, unroll=4)
    if top:
        outs.append(stream("final", refs["goal"], out=True))
        outs[-1].start()
    for c in range(KINDS):
        pushed = grown(refs["edge"][0, cut[c], :], 3 * rows, c)[1]
        pad_ref[0, cut[c], :] = jnp.where(core == 1, pushed, 0.0)
        pad_ref[rows + 1, cut[c], :] = jnp.where(core == 0, pushed, 0.0)
    for s in later_ins:
        s.wait()
    if step == 1:
        lag0 = wide(refs["stats0"][0][:, :1])
    source_ref = adj_ref if top else own_ref

    def line(z, carry):
        mob, onward = carry
        sums = sums_ref[z]
        rolls = rolled(sums)
        summed = functools.reduce(jnp.add, rolls)
        act = active(births_ref, z, step)
        adj = [source_ref[z, cut[c], :] for c in range(KINDS)]
        cells = [cells_ref[z, cut[c], :] for c in range(KINDS)]
        pots = [pot_ref[z, cut[c], :] for c in range(KINDS)]
        pushed = [pad_ref[z + 1, cut[c], :] for c in range(KINDS)]
        drive = packed(
            [
                (slope[c] * pots[c] - slope_keep[c])
                - time_step * adj[c] * (pots[c] - lag_wide[c])
                for c in range(KINDS)
            ]
        )
        plain = drive / (1.0 + summed)
        drive = act * plain
        shared = total_rows(
            (2.0 * coupling)
            * functools.reduce(jnp.add, [pushed[c] * cells[c] for c in range(KINDS)])
            - (KINDS / SUBLANES) * (jnp.concatenate([w_ref[z]] * (SUBLANES // KINDS)) * plain)
        )
        class_adj = 2.0 * (mixed(table, rolled(drive)) + shared)
        if not bottom:
            mob = tuple(m + drive * r for m, r in zip(mob, rolls))
        base = (6.0 * stiffness - 1.0) + (2.0 * coupling) * summed
        onward = list(onward)
        later = []
        for c in range(KINDS):
            around = (
                grown(before_ref[z, cut[c], :], rows + z, c)[1]
                + grown(after_ref[z, cut[c], :], 2 * rows + z, c)[1]
                + (pad_ref[z, cut[c], :] + pad_ref[z + 2, cut[c], :])
                + beside(pushed[c])
            )
            e = cells[c]
            new = (
                adj[c]
                + pushed[c] * (base + (3.0 - 6.0 * coupling) * (e * e))
                - stiffness * around
                + e * class_row(class_adj, c)
            )
            adj_ref[z, cut[c], :] = new
            if not bottom:
                onward[c] = onward[c] + refs["wnext"][z, pl.ds(c, 1), :] * new
            later.append(new)
        if step == 1:
            sums0 = rolled(refs["sums0"][z])
            gate = active(births_ref, z, 0) / (1.0 + functools.reduce(jnp.add, sums0))
            drive = (-time_step * gate) * packed(
                [later[c] * (refs["pot0"][z, cut[c], :] - lag0[c]) for c in range(KINDS)]
            )
            mob = tuple(m + drive * r for m, r in zip(mob, sums0))
        return mob, tuple(onward)

    size = rows // CHUNKS

    def chunk(j, carry):
        for s in sides:
            s.wait(j)
        carry = lax.fori_loop(0, size, lambda i, c: line(j * size + i, c), carry, unroll=8)
        return carry

    zero = jnp.zeros((each, ny), jnp.float32)
    mob, onward = lax.fori_loop(
        0, CHUNKS, chunk, (() if bottom else (zero,) * KINDS, () if bottom else (zero,) * KINDS)
    )
    if bottom:
        lane = lax.broadcasted_iota(jnp.int32, (1, LANES), 1)
        row = jnp.where(lane < KINDS * KINDS, total, 0.0)
        lane = lax.broadcasted_iota(jnp.int32, (orders, LANES), 1)
        home = lax.broadcasted_iota(jnp.int32, (orders, LANES), 0) // each
        for k in range(KINDS):
            value = slope_column * refs["linear"][2 + k][:, :1]
            row = row + jnp.sum(
                jnp.where(lane == home * KINDS + k, value, 0.0), axis=0, keepdims=True
            )
        refs["mobility"][...] = jnp.broadcast_to(row, refs["mobility"].shape)
        final_in.wait()
        pack(refs["slot"], refs["packed"], 0, refs["final"])
        pack(refs["slot"], refs["packed"], 1, adj_ref)
        outs.append(stream("packed", refs["packed"], out=True))
        outs[-1].start()
    else:
        row = time_step * spread(
            jnp.concatenate([jnp.sum(v, axis=1, keepdims=True) for v in onward], axis=0), orders
        )
        lane = lax.broadcasted_iota(jnp.int32, (KINDS, LANES), 1)
        kind = lax.broadcasted_iota(jnp.int32, (KINDS, LANES), 0)
        terms = jnp.zeros((1, LANES), jnp.float32)
        for d in range(KINDS):
            column = jnp.sum(mob[d], axis=1, keepdims=True)[:KINDS]
            spot = kind * KINDS + (kind + (KINDS - d)) % KINDS
            terms = terms + jnp.sum(jnp.where(lane == spot, column, 0.0), axis=0, keepdims=True)
        if not top:
            terms = terms + refs["mobin"][:1]
        if step == 1:
            row = row + terms
        else:
            refs["mobout"][...] = jnp.broadcast_to(terms, refs["mobout"].shape)
            outs.append(stream("mobout", refs["mobout"], out=True))
            outs[-1].start()
        refs["copies"][...] = jnp.broadcast_to(row, refs["copies"].shape)
        outs.append(stream("copies", refs["copies"], out=True))
        outs[-1].start()
        refs["send"][0] = adj_ref[jnp.where(core == 0, rows - 1, 0)]
    for s in outs:
        s.wait()


def stepped(kernel, step, smem, vmem, ins, outs, direct, scratch):
    names = list(smem) + list(vmem) + list(ins)
    pinned = [pltpu.with_memory_space_constraint(v, pltpu.HBM) for v in ins.values()]
    near = [
        pltpu.with_memory_space_constraint(v, pltpu.VMEM) if n == "own" else v
        for n, v in vmem.items()
    ]
    operands = [*smem.values(), *near, *pinned]
    out_names = list(outs) + list(direct)
    buffers = {n: (v.shape, v.dtype) for n, v in ins.items() if n not in scratch.get("skip", ())}
    buffers.update({n: (s, jnp.float32) for n, s in scratch["extra"].items()})
    streamed = [("i", n) for n in ins] + [("o", n) for n in outs]
    sems = [pltpu.SemaphoreType.DMA((CHUNKS,))] * len(streamed)

    def body(*args):
        args = list(args)
        table = dict(zip(names, args))
        args = args[len(names) :]
        hbm_out = dict(zip(out_names, args))
        args = args[len(out_names) :]
        bufs = dict(zip(buffers, args))
        sem = dict(zip(streamed, args[len(buffers) :]))
        hbm_in = {n: table.pop(n) for n in ins}
        refs = {**table, **bufs, **{n: hbm_out[n] for n in direct}}

        def stream(name, ref, chunks=1, out=False, part=None):
            if out:
                return Stream(ref, hbm_out[name], sem["o", name], chunks)
            source = hbm_in[name]
            if part:
                source, ref = source.at[pl.ds(0, part)], ref.at[pl.ds(0, part)]
            return Stream(source, ref, sem["i", name], chunks)

        refs["stream"] = stream
        kernel(step, refs)

    result = pl.pallas_call(
        body,
        name=f"{kernel.__name__}_{step}",
        out_shape=[pltpu.HBM(s, jnp.float32) for s in outs.values()]
        + [pltpu.VMEM(s, jnp.float32) for s in direct.values()],
        in_specs=[SMEM] * len(smem) + [VMEM] * len(vmem) + [HBM] * len(ins),
        out_specs=[HBM] * len(outs) + [VMEM] * len(direct),
        scratch_shapes=[pltpu.VMEM(s, d) for s, d in buffers.values()] + sems,
        compiler_params=pltpu.CompilerParams(vmem_limit_bytes=24 * 1024 * 1024),
    )(*operands)
    return dict(zip(out_names, result))


def places(groups, flip):
    ring = [(0, 0), (0, 1), (1, 1), (1, 0)]
    found = []
    for g in range(groups):
        pair, half = ring[g // 2]
        found.append((2 * (pair ^ flip) + g % 2, half))
    return found


def scatter_kernel(
    flip_ref, kinds_ref, first_ref, second_ref, out_ref, tag_ref, stage_a, stage_b, sems, sems_in
):
    groups, blocks, rows, ny = out_ref.shape
    local = first_ref.shape[0]
    loads = [
        pltpu.make_async_copy(ref.at[i], stage.at[i], sems_in.at[a * local + i])
        for a, (ref, stage) in enumerate(((first_ref, stage_a), (second_ref, stage_b)))
        for i in range(local)
    ]
    for c in loads:
        c.start()
    lane = lax.broadcasted_iota(jnp.int32, (rows, ny), 1)
    tag = jnp.zeros((rows, ny), jnp.float32)
    for i in range(local):
        tag = jnp.where(lane == i, kinds_ref[i].astype(jnp.float32), tag)
    tag_ref[...] = tag
    copies = []
    for g, (plane, half) in enumerate(places(groups, 0)):
        plane = plane ^ (2 * flip_ref[0])
        for a, ref in enumerate((stage_a, stage_b)):
            copies.append(
                pltpu.make_async_copy(
                    ref.at[:, plane, pl.ds(half * rows, rows), :],
                    out_ref.at[g, pl.ds(a * local, local)],
                    sems.at[3 * g + a],
                )
            )
        copies.append(
            pltpu.make_async_copy(tag_ref, out_ref.at[g, blocks - 1], sems.at[3 * g + 2])
        )
    for c in loads:
        c.wait()
    for c in copies:
        c.start()
    for c in copies:
        c.wait()


def collect_kernel(flip_ref, got_ref, first_ref, second_ref, sems):
    groups, _, local, rows, ny = got_ref.shape
    copies = []
    for g, (plane, half) in enumerate(places(groups, 0)):
        plane = plane ^ (2 * flip_ref[0])
        for a, ref in enumerate((first_ref, second_ref)):
            copies.append(
                pltpu.make_async_copy(
                    got_ref.at[g, a],
                    ref.at[:, plane, pl.ds(half * rows, rows), :],
                    sems.at[2 * g + a],
                )
            )
    for c in copies:
        c.start()
    for c in copies:
        c.wait()


def unpack_kernel(array, send, slot_ref, half_ref, got_ref, out_ref, *rest):
    sources, blocks, rows, ny = got_ref.shape
    local = blocks // 2
    for first in range(0, sources * local, SUBLANES):
        slots = [slot_ref[first + i] for i in range(SUBLANES)]
        tile = jnp.stack(
            [got_ref[p // local, array * local + lax.rem(p, local)] for p in slots], axis=0
        )
        out_ref[:, first : first + SUBLANES, :] = jnp.swapaxes(tile, 0, 1)
    if send:
        rest[0][0] = out_ref[jnp.where(half_ref[0] == 0, rows - 1, 0)]


def pack(slot_ref, out_ref, array, fields):
    groups, _, local, rows, ny = out_ref.shape
    for first in range(0, groups * local, SUBLANES):
        tile = jnp.swapaxes(fields[:, first : first + SUBLANES, :], 0, 1)
        for i in range(SUBLANES):
            p = slot_ref[first + i]
            out_ref[p // local, array, lax.rem(p, local)] = tile[i]


VMEM = pl.BlockSpec(memory_space=pltpu.VMEM)
SMEM = pl.BlockSpec(memory_space=pltpu.SMEM)
HBM = pl.BlockSpec(memory_space=pltpu.HBM)


def on_device(initial, target, birth_step, classes, mobility):
    slabs, groups = lax.axis_size("slab"), lax.axis_size("grp")
    devices = slabs * groups
    slab, me = lax.axis_index("slab"), lax.axis_index("grp")
    local, planes, nz, ny = initial.shape
    rows = nz * planes // groups
    orders = local * groups
    flip = slab % 2
    chip, core = me // 2, me % 2
    half = ((chip == 1) | (chip == 2)).astype(jnp.int32)
    plane = 2 * ((chip // 2) ^ flip) + core

    across = []
    for i in range(slabs * planes // 2 - 1):
        i = 2 * i + 1
        for z in range(2):
            ends = []
            for x in (i, i + 1):
                where = places(groups, x // planes % 2).index((x % planes, z))
                ends.append(x // planes * groups + where)
            across += [tuple(ends), tuple(ends[::-1])]

    def faces_of(cells, edge):
        return (
            lax.ppermute(cells, AXES, across),
            lax.ppermute(cells, "grp", [(g, g ^ 1) for g in range(groups)]),
            lax.ppermute(edge, "grp", [(g, g ^ 2) for g in range(groups)]),
        )

    def everywhere(copies):
        return lax.all_to_all(copies, AXES, 0, 0, tiled=True)

    chain = [(i, i + 1) for i in range(slabs - 1)]
    births = jnp.concatenate(
        [
            lax.ppermute(birth_step[-1:], "slab", chain),
            birth_step,
            lax.ppermute(birth_step[:1], "slab", [(j, i) for i, j in chain]),
        ]
    )
    near = lax.dynamic_slice_in_dim(births, plane, 3, axis=0)
    mine = lax.dynamic_slice_in_dim(near, half * rows, rows, axis=1)
    other = lax.dynamic_slice_in_dim(near[1], jnp.where(half == 0, rows, rows - 1), 1, axis=0)
    first, second = jnp.where(core == 0, mine[0], mine[2]), jnp.where(core == 0, mine[2], mine[0])
    births = jnp.concatenate(
        [mine[1], first, second, jnp.broadcast_to(other, (SUBLANES, ny))], axis=0
    )

    flip = flip.astype(jnp.int32).reshape(1)
    block = (groups, 2 * local + 1, rows, ny)
    message = pl.pallas_call(
        scatter_kernel,
        name="scatter",
        out_shape=pltpu.HBM(block, jnp.float32),
        in_specs=[SMEM, SMEM, HBM, HBM],
        out_specs=HBM,
        scratch_shapes=[
            pltpu.VMEM((rows, ny), jnp.float32),
            pltpu.VMEM(initial.shape, jnp.float32),
            pltpu.VMEM(initial.shape, jnp.float32),
            pltpu.SemaphoreType.DMA((3 * groups,)),
            pltpu.SemaphoreType.DMA((2 * local,)),
        ],
    )(flip, classes, initial, target)
    got = lax.all_to_all(message, "grp", 0, 0, tiled=True)
    kind = got[:, -1, 0, :local].reshape(orders).astype(jnp.int32)
    index = jnp.arange(orders, dtype=jnp.int32)
    ahead = (kind[None, :] < kind[:, None]) | (
        (kind[None, :] == kind[:, None]) & (index[None, :] < index[:, None])
    )
    rank = jnp.sum(ahead.astype(jnp.int32), axis=1)
    slot = jnp.sum(jnp.where(rank[None, :] == index[:, None], index[None, :], 0), axis=1)
    shape, edge_shape = (rows, orders, ny), (1, orders, ny)

    def unpacked(array, outs):
        return pl.pallas_call(
            functools.partial(unpack_kernel, array, len(outs) > 1),
            name=f"unpack{array}",
            out_shape=outs,
            in_specs=[SMEM, SMEM, VMEM],
            out_specs=[VMEM] * len(outs),
            compiler_params=pltpu.CompilerParams(vmem_limit_bytes=16 * 1024 * 1024),
        )(slot, half.reshape(1), got)

    own, edge = unpacked(0, [pltpu.VMEM(s, jnp.float32) for s in (shape, edge_shape)])
    (goal,) = unpacked(1, [pltpu.HBM(shape, jnp.float32)])
    smem = {"core": half.reshape(1), "mob": mobility}
    tiles, own_tiles = (3 * rows + 1, KINDS, ny), (rows, SUBLANES, ny)
    padded = (rows + 2, orders, ny)
    stored = []
    got = weights = None
    for step in range(STEPS):
        first, last = step == 0, step == STEPS - 1
        before, after, beyond = faces_of(own, edge)
        vmem = {"births": births, "before": before, "after": after, "edge": beyond, "own": own}
        ins = {}
        direct = {"moved": shape, "send": edge_shape}
        outs = {"pot": shape, "sums": own_tiles, "w": tiles, "cells": shape}
        outs["copies"] = (2 * devices if first else devices, LANES)
        extra = {"pad": padded, **{n: s for n, s in outs.items() if n != "cells"}}
        if first:
            extra["lin"] = (KINDS, orders, ny)
        else:
            vmem["got"] = got
            ins["wprev"] = weights
            outs["stats"] = (2 + (KINDS if step == 1 else 0), orders, LANES)
            extra["stats"] = outs["stats"]
        if last or first:
            ins["goal"] = goal
        skip = ("goal",) if first else ()
        result = stepped(
            forward_kernel, step, smem, vmem, ins, outs, direct, {"skip": skip, "extra": extra}
        )
        if not first:
            stored[-1]["stats"] = result["stats"]
        own, edge, weights = result["moved"], result["send"], result["w"]
        stored.append({n: result[n] for n in ("cells", "pot", "sums", "w")})
        got = everywhere(result["copies"])
    terms = None
    for step in range(STEPS - 1, -1, -1):
        top, bottom = step == STEPS - 1, step == 0
        before, after, beyond = faces_of(own, edge)
        vmem = {"births": births, "got": got, "before": before, "after": after, "edge": beyond}
        vmem["own"] = own
        ins = dict(stored[step])
        outs, direct = {}, {}
        extra = {"pad": padded}
        if top:
            ins["goal"] = goal
            outs["final"] = shape
        else:
            if bottom:
                ins["linear"] = stored[0]["stats"]
            else:
                ins["mobin"] = terms
        if bottom:
            extra["adj"] = shape
            direct["mobility"] = (SUBLANES, LANES)
            ins["final"] = final_state
            outs["packed"] = extra["packed"] = (groups, 2, local, rows, ny)
        else:
            ins["wnext"] = stored[step - 1]["w"]
            direct["adj"], direct["send"] = shape, edge_shape
            outs["copies"] = extra["copies"] = (devices, LANES)
            if step > 1:
                outs["mobout"] = extra["mobout"] = (SUBLANES, LANES)
        if step == 1:
            ins.update({n + "0": stored[0][n] for n in ("pot", "sums", "stats")})
        result = stepped(
            backward_kernel,
            step,
            {**smem, "slot": slot} if bottom else smem,
            vmem,
            ins,
            outs,
            direct,
            {"extra": extra},
        )
        own = result.get("adj")
        if top:
            final_state = result["final"]
        if bottom:
            mobility_sum = result["mobility"]
        else:
            edge, terms = result["send"], result.get("mobout")
            got = everywhere(result["copies"])

    both = result["packed"]
    both = lax.all_to_all(both, "grp", 0, 0, tiled=True)
    final_state, gradient = pl.pallas_call(
        collect_kernel,
        name="collect",
        out_shape=[pltpu.HBM(initial.shape, jnp.float32)] * 2,
        in_specs=[SMEM, VMEM],
        out_specs=[HBM, HBM],
        scratch_shapes=[pltpu.SemaphoreType.DMA((2 * groups,))],
    )(flip, pltpu.with_memory_space_constraint(both, pltpu.VMEM))
    scale = time_step * (planes * slabs) * nz
    mobility_sum = mobility_sum[0, : KINDS * KINDS].reshape(KINDS, KINDS)
    return final_state, gradient, mobility_sum / scale


def solution(mesh):
    return jax.shard_map(
        on_device,
        mesh=mesh,
        in_specs=(
            P("grp", "slab", None, None),
            P("grp", "slab", None, None),
            P("slab", None, None),
            P("grp"),
            P(),
        ),
        out_specs=(P("grp", "slab", None, None), P("grp", "slab", None, None), P()),
        check_vma=False,
    )
```
